32 devices in a mesh: gx: 4 (over z), gy: 8 (over y, x, core).
Axes of the slice: x: 2, y: 2, z: 4, core: 2. Of those that a mesh axis runs over, the one named last changes fastest.
Arguments:
- sensitivity: float32 [3, 262144], P(None, ('gx', 'gy')), may hold values from -24 to 24
- node_weight: float32 [262144], P(('gx', 'gy')), may hold values from 0.05 to 0.5
- dest_device: int32 [262144, 1], P(('gx', 'gy')), may hold values from 0 to 31; in each aligned block of 8192 rows (0 to 8191, 8192 to 16383, ...) at most 512 rows name the same one
- dest_cell: int32 [262144], P(('gx', 'gy')), may hold values from 0 to 131071
- box_owner: int32 [262144, 1], P(('gx', 'gy')), may hold values from 0 to 31; in each aligned block of 8192 rows (0 to 8191, 8192 to 16383, ...) at most 512 rows name the same one
- box_slot: int32 [262144], P(('gx', 'gy')), may hold values from 0 to 63
- stiffness: float32 [64, 256, 256], P('gx', 'gy'), may hold values from 0.5 to 2
- anchor: float32 [3, 64, 256, 256], P(None, 'gx', 'gy'), may hold values from 3 to 6
- coupling: float32 [9, 64, 256, 256], P(None, 'gx', 'gy'), may hold values from -1 to 1
Outputs:
- adjoint: float32 [3, 64, 256, 256], P(None, 'gx', 'gy')
- box_gradient: float32 [3, 2048], P(None, ('gx', 'gy'))
The draws below stay inside these ranges and needn't reach their ends.
Inputs may be any that keep to these rules, and one draw needn't show every extreme that they name: `dest_device`: among the rows of one device, no deformation device is named more than 512 times, and in some device's rows one is named exactly 512 times. `box_owner`: among the rows of one device, no owner is named more than 512 times, and in some device's rows one is named exactly 512 times.
All inputs are finite; a program needn't handle non-finite values.
Results may differ from the reference program's by a relative error of at most 0.0003.
Values sent between devices are 32-bit elements; how exact they have to be, the bound alone decides.
A program may use at most 192 MiB of HBM per device.

```python
import math
import jax
import jax.numpy as jnp
import numpy as np

CX = 16
CY = 32
CZ = 256
SR_DEV = 8192
BOX_DEV = 64
SWEEPS = 4
CAP = 512
NX = 64
NY = 256
NZ = 256
ROWS = 262144
BOXES = 2048
N_GX = 4
N_GY = 8


def set_ends(result, own_key, smallest, high):
    place = [jax.random.randint(jax.random.fold_in(own_key, axis), (), 0, length) for axis, length in enumerate(result.shape)]
    longest = result.shape.index(max(result.shape))
    neighbour = place[:longest] + [(place[longest] + 1) % result.shape[longest]] + place[longest + 1:]
    return result.at[tuple(place)].set(smallest).at[tuple(neighbour)].set(high)


def levels(rng, shape, cuts, least, high):
    def one(position, parts):
        heights = jax.random.uniform(jax.random.fold_in(jax.random.fold_in(rng, 6), position), (parts,), jnp.float32, least / len(cuts), high / len(cuts))
        return jnp.repeat(jnp.exp(heights), shape[position] // parts).reshape((-1,) + (1,) * (len(shape) - position - 1))

    gain = one(*cuts[0])
    for cut in cuts[1:]:
        gain = gain * one(*cut)
    return gain


def assign_block(own_key, own, number, rows, number_of, top, most, lean):
    sequence = jax.random.permutation(own_key, number_of)
    heavy_load, common = load_shares(number_of, rows * top, most, lean, True), load_shares(number_of, rows * top, most, lean, False)
    places = jnp.arange(number_of)

    def named(tallies, rotation):
        used = int((tallies > 0).sum())
        fixed = max(1, used // 4)
        moved = fixed + (places - fixed + rotation * (used - fixed)) % max(1, number_of - fixed)
        return jnp.zeros((number_of,), jnp.int32).at[sequence[jnp.where(places < fixed, places, moved)]].set(jnp.asarray(tallies, jnp.int32))

    tallies = jnp.where(number % 4 == 0, named(heavy_load, number // 4), named(common, number - number // 4 - 1))
    mixed = jax.random.permutation(jax.random.fold_in(own, 3), number_of)
    donor, receiver = mixed[0:number_of // 2 * 2:2], mixed[1:number_of // 2 * 2:2]
    slack = jnp.minimum(tallies[donor] - 1, most - tallies[receiver]) // 2
    slack = jnp.where((donor == sequence[0]) | (receiver == sequence[0]) | (tallies[receiver] == 0), 0, jnp.maximum(slack, 0))
    moved = jax.random.randint(jax.random.fold_in(own, 4), (number_of // 2,), 0, 1 << 20) % (slack + 1)
    tallies = tallies.at[donor].add(-moved).at[receiver].add(moved)
    labels = jnp.searchsorted(jnp.cumsum(tallies), jnp.arange(rows * top), side="right").astype(jnp.int32)
    grid = labels.reshape(top, rows).T
    grid = grid[jax.random.permutation(jax.random.fold_in(own, 1), rows)]
    rotation = jax.random.randint(jax.random.fold_in(own, 2), (rows, 1), 0, top)
    return jnp.take_along_axis(grid, (jnp.arange(top)[None, :] + rotation) % top, axis=1)


def load_shares(count, total, limit, lean, full):
    loads = [(1 << 20) // math.isqrt(grade ** lean) + 1 for grade in range(1, count + 1)]
    largest = limit if full else min(limit, max(-(-total // count), total * loads[0] // sum(loads)))
    least = 1 if total - largest >= count - 1 else 0
    counts, surplus = [largest] + [least] * (count - 1), total - largest - least * (count - 1)
    while surplus > 0:
        candidates = [i for i in range(1, count) if counts[i] < largest] or [i for i in range(1, count) if counts[i] < limit]
        mass, left = sum([loads[i] for i in candidates]), surplus
        for i in candidates:
            extra = min(limit - counts[i], max(1, left * loads[i] // mass), surplus)
            counts[i] = counts[i] + extra
            surplus = surplus - extra
    return np.array(counts)


def noise(rng, shape, width, bound, split=(), dtype=jnp.bfloat16):
    array = jax.random.normal(rng, shape, jnp.float32) * width
    if len(split) > 0:
        array = levels(rng, shape, split, -0.22, 0.18) * array
    return jnp.clip(array, min=-bound, max=bound).astype(dtype)


def setup_inputs(seed: int = 0) -> dict:
    keys = jax.random.split(jax.random.key(seed), 10)
    sensitivity = noise(keys[0], (3, ROWS), 4.0, 24.0, ((1, 32),), jnp.float32)
    node_weight = jnp.clip(0.05 + 0.45 * jax.random.uniform(keys[1], (ROWS,), jnp.float32) ** levels(keys[1], (ROWS,), ((0, 32),), -0.2, 0.2), 0.05, 0.5)
    dest_device_keys = jax.random.split(jax.random.fold_in(keys[2], 1), ROWS // SR_DEV)
    dest_device_turns = jax.random.permutation(jax.random.fold_in(keys[2], 3), ROWS // SR_DEV)
    dest_device = jax.vmap(lambda own, number: assign_block(jax.random.fold_in(keys[2], 2), own, number, SR_DEV, N_GX * N_GY, 1, CAP, 2))(dest_device_keys, dest_device_turns).reshape((ROWS, 1))
    dest_cell = set_ends(jax.random.randint(keys[3], (ROWS,), 0, CX * CY * CZ), jax.random.fold_in(keys[3], 1), 0, (CX * CY * CZ) - 1).astype(jnp.int32)
    box_owner_keys = jax.random.split(jax.random.fold_in(keys[4], 1), ROWS // SR_DEV)
    box_owner_turns = jax.random.permutation(jax.random.fold_in(keys[4], 3), ROWS // SR_DEV)
    box_owner = jax.vmap(lambda own, number: assign_block(jax.random.fold_in(keys[4], 2), own, number, SR_DEV, N_GX * N_GY, 1, CAP, 1))(box_owner_keys, box_owner_turns).reshape((ROWS, 1))
    box_slot = set_ends(jax.random.randint(keys[5], (ROWS,), 0, BOX_DEV), jax.random.fold_in(keys[5], 1), 0, BOX_DEV - 1).astype(jnp.int32)
    stiffness = jnp.clip(jnp.exp(math.log(2.0) - 1.3862944 * jax.random.uniform(keys[6], (NX, NY, NZ), jnp.float32) ** levels(keys[6], (NX, NY, NZ), ((0, 4), (1, 8)), -0.2, 0.2)), 0.5, 2.0)
    anchor = jnp.clip(jnp.exp(math.log(6.0) - 0.6931472 * jax.random.uniform(keys[7], (3, NX, NY, NZ), jnp.float32) ** levels(keys[7], (3, NX, NY, NZ), ((1, 4), (2, 8)), -0.2, 0.2)), 3.0, 6.0)
    coupling = jnp.clip(jax.random.uniform(keys[8], (9, NX, NY, NZ), jnp.float32, -1.0, 1.0) * levels(keys[8], (9, NX, NY, NZ), ((1, 4), (2, 8)), -0.4, 0.0), -1.0, 1.0)
    return dict(sensitivity=sensitivity, node_weight=node_weight, dest_device=dest_device, dest_cell=dest_cell, box_owner=box_owner, box_slot=box_slot, stiffness=stiffness, anchor=anchor, coupling=coupling)


def neighbour_sum(padded):
    z_padded = jnp.pad(padded, ((0, 0), (0, 0), (0, 0), (1, 1)))
    middle = z_padded[:, 1:-1, 1:-1, :]
    total = z_padded[:, 2:, 1:-1, 1:-1] + z_padded[:, :-2, 1:-1, 1:-1]
    total = total + z_padded[:, 1:-1, 2:, 1:-1] + z_padded[:, 1:-1, :-2, 1:-1]
    return total + middle[..., 2:] + middle[..., :-2]


def apply_transposed(field, weighted_pad, stiff, anchor, coupling):
    blocks = coupling.reshape((3, 3) + coupling.shape[1:])
    mixing = jnp.sum(blocks * field[:, None], axis=0)
    return 6.0 * stiff[None] * field - neighbour_sum(weighted_pad) + mixing + anchor * field


def reference(sensitivity, node_weight, dest_device, dest_cell, box_owner, box_slot, stiffness, anchor, coupling):
    target = dest_device[:, 0]
    local_cell = dest_cell
    x_cell = (target // N_GY) * CX + local_cell // (CY * CZ)
    y_cell = (target % N_GY) * CY + (local_cell // CZ) % CY
    z_cell = local_cell % CZ
    flat_ids = ((x_cell * NY + y_cell) * NZ + z_cell).astype(jnp.int32)
    load = jnp.zeros((3, NX * NY * NZ), jnp.float32).at[:, flat_ids].add(sensitivity)
    load = load.reshape(3, NX, NY, NZ)
    diagonal = 6.0 * stiffness[None] + anchor + jnp.stack([coupling[0], coupling[4], coupling[8]])
    adjoint = jnp.zeros((3, NX, NY, NZ), jnp.float32)
    for sweep_idx in range(SWEEPS):
        weighted = jnp.pad(stiffness[None] * adjoint, ((0, 0), (1, 1), (1, 1), (0, 0)))
        applied = apply_transposed(adjoint, weighted, stiffness, anchor, coupling)
        adjoint = adjoint + (load - applied) / diagonal
    flat_field = adjoint.reshape(3, NX * NY * NZ)
    row_gradient = node_weight[None] * flat_field[:, flat_ids]
    box_ids = (box_owner[:, 0] * BOX_DEV + box_slot).astype(jnp.int32)
    box_gradient = jax.ops.segment_sum(row_gradient.T, box_ids, num_segments=BOXES).T
    return adjoint, box_gradient
```

```python
import functools

import jax
import jax.numpy as jnp
from jax import lax
from jax.experimental import pallas as pl
from jax.experimental.pallas import tpu as pltpu
from jax.sharding import PartitionSpec as P

BOX_DEV = 64
SWEEPS = 4
SENT = 6
NT = (((1,), (1,)), ((), ()))
F32 = jnp.float32
BF16 = jnp.bfloat16
MESH = pl.DeviceIdType.MESH


def two_terms(x):
    hi = x.astype(BF16).astype(F32)
    return hi, x - hi


def matches(count, row):
    return lax.broadcasted_iota(jnp.int32, (count, row.shape[1]), 0) == row


def one_hot(mask):
    return jnp.where(mask, 1.0, 0.0).astype(BF16)


def scaled(mask, row):
    return jnp.where(mask, row, 0.0).astype(BF16)


def dot_nt(a, b):
    return lax.dot_general(a, b, NT, preferred_element_type=F32)


def pack_kernel(step, sens, weight, device, cell, owner, slot, out, tri, seen):
    targets, fields, capacity = out.shape
    rows = sens.shape[1]
    out[...] = jnp.zeros_like(out)
    seen[...] = jnp.zeros_like(seen)
    tri[...] = one_hot(
        lax.broadcasted_iota(jnp.int32, (step, step), 0)
        < lax.broadcasted_iota(jnp.int32, (step, step), 1)
    )

    def block(index, carry):
        span = pl.ds(pl.multiple_of(index * step, step), step)
        target = device[:, span]
        chosen = matches(targets, target)
        before = jnp.dot(one_hot(chosen), tri[...], preferred_element_type=F32) + seen[:, :1]
        rank = jnp.sum(jnp.where(chosen, before, 0.0), axis=0, keepdims=True).astype(jnp.int32)
        seen[...] = seen[...] + jnp.sum(jnp.where(chosen, 1.0, 0.0), axis=1, keepdims=True)
        place = one_hot(matches(capacity, rank))
        payload = jnp.concatenate(
            [
                sens[:, span],
                cell[:, span].astype(F32),
                weight[:, span],
                (owner[:, span] * BOX_DEV + slot[:, span]).astype(F32),
                jnp.zeros((fields - SENT, step), F32),
            ],
            axis=0,
        )
        wide = (targets, fields, step)
        to = lax.broadcasted_iota(jnp.int32, wide, 0) == target[None]
        terms = [
            jnp.where(to, term[None], 0.0).reshape(targets * fields, step).astype(BF16)
            for term in two_terms(payload)
        ]
        product = dot_nt(jnp.concatenate(terms, axis=0), place)
        product = product[: targets * fields] + product[targets * fields :]
        out[...] = out[...] + product.reshape(targets, fields, capacity)
        return carry

    lax.fori_loop(0, rows // step, block, 0)


def pack_rows(devices, capacity, sens, weight, device, cell, owner, slot):
    step = min(2048, sens.shape[1])
    return pl.pallas_call(
        functools.partial(pack_kernel, step),
        out_shape=jax.ShapeDtypeStruct((devices, 8, capacity), F32),
        in_specs=[pl.BlockSpec(memory_space=pltpu.VMEM)] * 6,
        out_specs=pl.BlockSpec(memory_space=pltpu.VMEM),
        scratch_shapes=[pltpu.VMEM((step, step), BF16), pltpu.VMEM((devices, 128), F32)],
        name="pack_rows",
    )(sens, weight, device, cell, owner, slot)


def split(value, size):
    if size & (size - 1) == 0:
        return value >> (size.bit_length() - 1), value & (size - 1)
    return value // size, value % size


def sort_kernel(cut, slabs, arrived, tiles, ends):
    senders, fields, capacity = arrived.shape
    per_group, _, width = tiles.shape
    join = max(1, min(senders, 512 // capacity))
    count, length = senders // join, join * capacity
    blocks = [
        jnp.concatenate([arrived[q * join + i] for i in range(join)], axis=1)
        for q in range(count)
    ]
    chosen = [matches(slabs, split(block[3:4].astype(jnp.int32), cut)[0]) for block in blocks]
    stacked = one_hot(jnp.concatenate(chosen, axis=0))
    total = count * slabs
    earlier = one_hot(
        lax.broadcasted_iota(jnp.int32, (length, length), 0)
        < lax.broadcasted_iota(jnp.int32, (length, length), 1)
    )
    before = jnp.dot(stacked, earlier, preferred_element_type=F32)
    number = jnp.dot(stacked, jnp.ones((length, 128), BF16), preferred_element_type=F32)
    this = lax.broadcasted_iota(jnp.int32, (total, total), 0)
    other = lax.broadcasted_iota(jnp.int32, (total, total), 1)
    ahead = one_hot((other % slabs < this % slabs) | ((other % slabs == this % slabs) & (other < this)))
    tens = jnp.floor(number * 0.0625)
    first = 16.0 * jnp.dot(ahead, tens.astype(BF16), preferred_element_type=F32)
    first = first + jnp.dot(ahead, (number - 16.0 * tens).astype(BF16), preferred_element_type=F32)

    start = first[:slabs]
    later = lax.broadcasted_iota(jnp.int32, start.shape, 0) > 0
    begin = (lax.broadcasted_iota(jnp.int32, start.shape, 1) * width).astype(F32)
    low = jnp.sum(jnp.where(later & (start <= begin), 1.0, 0.0), axis=0, keepdims=True)
    high = jnp.sum(jnp.where(later & (start < begin + width), 1.0, 0.0), axis=0, keepdims=True)
    ends[0] = jnp.concatenate([low, high, jnp.zeros((6, 128), F32)], axis=0).astype(jnp.int32)

    sums = jnp.zeros((per_group * 2 * fields, width), F32)
    for q in range(count):
        rows = slice(q * slabs, (q + 1) * slabs)
        where = before[rows] + first[rows, :1]
        place = jnp.sum(jnp.where(chosen[q], where, 0.0), axis=0, keepdims=True).astype(jnp.int32)
        tile, lane = split(place, width)
        terms = jnp.concatenate(two_terms(blocks[q]), axis=0)
        spread = jnp.concatenate([scaled(tile == t, terms) for t in range(per_group)], axis=0)
        sums = sums + dot_nt(spread, one_hot(matches(width, lane)))
    for t in range(per_group):
        at = t * 2 * fields
        tiles[t] = sums[at : at + fields] + sums[at + fields : at + 2 * fields]


def sort_rows(arrived, slabs, cut):
    devices, fields, capacity = arrived.shape
    rows = devices * capacity
    size = min(4096, rows)
    width = min(256, size)
    groups = rows // size
    return pl.pallas_call(
        functools.partial(sort_kernel, cut, slabs),
        grid=(groups,),
        out_shape=[
            jax.ShapeDtypeStruct((rows // width, fields, width), F32),
            jax.ShapeDtypeStruct((groups, 8, 128), jnp.int32),
        ],
        in_specs=[pl.BlockSpec((size // capacity, fields, capacity), lambda i: (i, 0, 0))],
        out_specs=[
            pl.BlockSpec((size // width, fields, width), lambda i: (i, 0, 0)),
            pl.BlockSpec((1, 8, 128), lambda i: (i, 0, 0)),
        ],
        name="sort_rows",
    )(arrived)


def located(tile, size_z):
    return split(tile[3:4].astype(jnp.int32), size_z)


def scatter_kernel(size_y, ends, tiles, load):
    parts, size_xy, size_z = load.shape
    per_group = tiles.shape[0] // ends.shape[0]
    half = parts * size_y
    load[...] = jnp.zeros_like(load)

    def one_tile(t, carry):
        group, index = t // per_group, t % per_group
        tile = tiles[t]
        xy, z = located(tile, size_z)
        at_z = one_hot(matches(size_z, z))
        pairs = [two_terms(tile[k : k + 1]) for k in range(parts)]
        values = [hi for hi, lo in pairs] + [lo for hi, lo in pairs]

        def one_slab(x, carry):
            at_y = matches(size_y, xy - x * size_y)
            terms = jnp.concatenate([scaled(at_y, value) for value in values], axis=0)
            product = dot_nt(terms, at_z)
            product = product[:half] + product[half:]
            span = pl.ds(pl.multiple_of(x * size_y, size_y), size_y)
            for k in range(parts):
                load[k, span] = load[k, span] + product[k * size_y : (k + 1) * size_y]
            return carry

        return lax.fori_loop(ends[group, 0, index], ends[group, 1, index] + 1, one_slab, carry)

    lax.fori_loop(0, tiles.shape[0], one_tile, 0)


def scatter_rows(tiles, ends, size_x, size_y, size_z):
    return pl.pallas_call(
        functools.partial(scatter_kernel, size_y),
        out_shape=jax.ShapeDtypeStruct((3, size_x * size_y, size_z), F32),
        in_specs=[pl.BlockSpec(memory_space=pltpu.SMEM), pl.BlockSpec(memory_space=pltpu.VMEM)],
        out_specs=pl.BlockSpec(memory_space=pltpu.VMEM),
        name="scatter_rows",
    )(ends, tiles)


def gather_kernel(ends, tiles, field, boxes, terms, sums):
    parts, size_x, size_y, size_z = field.shape
    per_group = tiles.shape[0] // ends.shape[0]
    devices = boxes.shape[0]
    half = parts * size_y
    width = tiles.shape[2]
    sums[...] = jnp.zeros_like(sums)

    def cut(x, carry):
        for k in range(parts):
            hi, lo = two_terms(field[k, x])
            terms[x, k * size_y : (k + 1) * size_y] = hi.astype(BF16)
            terms[x, half + k * size_y : half + (k + 1) * size_y] = lo.astype(BF16)
        return carry

    lax.fori_loop(0, size_x, cut, 0)

    def one_tile(t, carry):
        group, index = t // per_group, t % per_group
        tile = tiles[t]
        xy, z = located(tile, size_z)
        at_z = one_hot(matches(size_z, z))

        def one_slab(x, found):
            at_y = matches(size_y, xy - x * size_y)
            columns = jnp.dot(terms[x], at_z, preferred_element_type=F32)
            columns = columns[:half] + columns[half:]
            return tuple(
                found[k] + jnp.sum(jnp.where(at_y, columns[k * size_y : (k + 1) * size_y], 0.0).reshape(size_y // 8, 8, width), axis=0)
                for k in range(parts)
            )

        empty = tuple(jnp.zeros((8, width), F32) for _ in range(parts))
        found = lax.fori_loop(ends[group, 0, index], ends[group, 1, index] + 1, one_slab, empty)
        owner, slot = split(tile[5:6].astype(jnp.int32), BOX_DEV)
        at_owner = matches(devices, owner)
        pairs = [two_terms(jnp.sum(part, axis=0, keepdims=True) * tile[4:5]) for part in found]
        values = [hi for hi, lo in pairs] + [lo for hi, lo in pairs]
        spread = jnp.concatenate([scaled(at_owner, value) for value in values], axis=0)
        sums[...] = sums[...] + dot_nt(spread, one_hot(matches(BOX_DEV, slot)))
        return carry

    lax.fori_loop(0, tiles.shape[0], one_tile, 0)
    for k in range(parts):
        part = sums[k * devices : (k + 1) * devices] + sums[(parts + k) * devices : (parts + k + 1) * devices]
        boxes[:, k * BOX_DEV : (k + 1) * BOX_DEV] = part


def gather_rows(tiles, ends, field):
    groups = ends.shape[0]
    parts, size_x, size_y, size_z = field.shape
    devices = lax.axis_size("gx") * lax.axis_size("gy")
    return pl.pallas_call(
        gather_kernel,
        out_shape=jax.ShapeDtypeStruct((devices, 3 * BOX_DEV), F32),
        in_specs=[pl.BlockSpec(memory_space=pltpu.SMEM)] + [pl.BlockSpec(memory_space=pltpu.VMEM)] * 2,
        out_specs=pl.BlockSpec(memory_space=pltpu.VMEM),
        scratch_shapes=[
            pltpu.VMEM((size_x, 2 * parts * size_y, size_z), BF16),
            pltpu.VMEM((2 * parts * devices, BOX_DEV), F32),
        ],
        name="gather_rows",
    )(ends, tiles, field)


def sweep_kernel(load, stiff, anchor, coupling, adjoint, weighted, rest, inverse, edge, halo, x_send, x_recv, y_send, y_recv):
    parts, size_x, size_y, size_z = load.shape
    exchanges = weighted.shape[0]
    gx, gy = lax.axis_index("gx"), lax.axis_index("gy")
    last_x, last_y = lax.axis_size("gx") - 1, lax.axis_size("gy") - 1
    sides = (("gx", gx, -1, gx > 0), ("gx", gx, 1, gx < last_x), ("gy", gy, -1, gy > 0), ("gy", gy, 1, gy < last_y))
    y_at = lax.broadcasted_iota(jnp.int32, (size_y, size_z), 0)
    z_at = lax.broadcasted_iota(jnp.int32, (size_y, size_z), 1)

    for index in range(exchanges):
        for k in range(parts):
            weighted[index, k, 0] = jnp.zeros((size_y, size_z), F32)
            weighted[index, k, size_x + 1] = jnp.zeros((size_y, size_z), F32)
    halo[...] = jnp.zeros_like(halo)

    barrier = pltpu.get_barrier_semaphore()
    known = 0
    for axis, place, move, present in sides:
        known = known + present.astype(jnp.int32)

        @pl.when(present)
        def _():
            pl.semaphore_signal(barrier, inc=1, device_id={axis: place + move}, device_id_type=MESH)

    pl.semaphore_wait(barrier, known)

    def copies(index):
        made = []
        for side, (axis, place, move, present) in enumerate(sides):
            there = 1 - side % 2
            if axis == "gx":
                pair = (weighted.at[index, :, 1 if move < 0 else size_x], weighted.at[index, :, size_x + 1 if move < 0 else 0])
                sems = (x_send, x_recv)
            else:
                pair = (edge.at[index, side % 2], halo.at[index, there])
                sems = (y_send, y_recv)
            made.append((present, pltpu.make_async_remote_copy(
                src_ref=pair[0],
                dst_ref=pair[1],
                send_sem=sems[0].at[index, side % 2],
                recv_sem=sems[1].at[index, there],
                device_id={axis: place + move},
                device_id_type=MESH,
            )))
        return made

    def arrivals(index):
        made = []
        for side, (axis, place, move, present) in enumerate(sides):
            if axis == "gx":
                pair = (weighted.at[index, :, 1 if move < 0 else size_x], weighted.at[index, :, 0 if move < 0 else size_x + 1])
                sems = (x_send, x_recv)
            else:
                pair = (edge.at[index, side % 2], halo.at[index, side % 2])
                sems = (y_send, y_recv)
            made.append((present, pltpu.make_async_remote_copy(
                src_ref=pair[0],
                dst_ref=pair[1],
                send_sem=sems[0].at[index, side % 2],
                recv_sem=sems[1].at[index, side % 2],
                device_id={axis: place + move},
                device_id_type=MESH,
            )))
        return made

    def publish(index, x, k, value):
        adjoint[k, x] = value
        if index < exchanges:
            product = stiff[x] * value
            weighted[index, k, x + 1] = product
            edge[index, 0, k, pl.ds(x, 1), :] = product[0:1]
            edge[index, 1, k, pl.ds(x, 1), :] = product[size_y - 1 : size_y]

    def first(x, carry):
        for k in range(parts):
            inverse[k, x] = 1.0 / (6.0 * stiff[x] + anchor[k, x] + coupling[4 * k, x])
            publish(0, x, k, load[k, x] * inverse[k, x])
        return carry

    lax.fori_loop(0, size_x, first, 0)
    for index in range(exchanges):
        for present, copy in copies(index):

            @pl.when(present)
            def _():
                copy.start()

        def near(x, carry):
            fields = [adjoint[k, x] for k in range(parts)]
            for k in range(parts):
                product = weighted[index, k, x + 1]
                value = load[k, x]
                for j in range(parts):
                    if j != k:
                        value = value - coupling[3 * j + k, x] * fields[j]
                value = value + jnp.where(z_at == 0, 0.0, pltpu.roll(product, 1, 1))
                value = value + jnp.where(z_at == size_z - 1, 0.0, pltpu.roll(product, size_z - 1, 1))
                value = value + jnp.where(y_at == 0, 0.0, pltpu.roll(product, 1, 0))
                value = value + jnp.where(y_at == size_y - 1, 0.0, pltpu.roll(product, size_y - 1, 0))
                rest[k, x] = value
            return carry

        lax.fori_loop(0, size_x, near, 0)
        for present, copy in arrivals(index):

            @pl.when(present)
            def _():
                copy.wait_recv()

        def far(x, carry):
            for k in range(parts):
                value = rest[k, x] + weighted[index, k, x] + weighted[index, k, x + 2]
                value = value + jnp.where(y_at == 0, halo[index, 0, k, pl.ds(x, 1), :], 0.0)
                value = value + jnp.where(y_at == size_y - 1, halo[index, 1, k, pl.ds(x, 1), :], 0.0)
                publish(index + 1, x, k, value * inverse[k, x])
            return carry

        lax.fori_loop(0, size_x, far, 0)
    for index in range(exchanges):
        for present, copy in copies(index):

            @pl.when(present)
            def _():
                copy.wait_send()


def solve_sweeps(load, stiffness, anchor, coupling):
    parts, size_x, size_y, size_z = load.shape
    exchanges = SWEEPS - 1
    return pl.pallas_call(
        sweep_kernel,
        out_shape=jax.ShapeDtypeStruct(load.shape, F32),
        in_specs=[pl.BlockSpec(memory_space=pltpu.VMEM)] * 4,
        out_specs=pl.BlockSpec(memory_space=pltpu.VMEM),
        scratch_shapes=[
            pltpu.VMEM((exchanges, parts, size_x + 2, size_y, size_z), F32),
            pltpu.VMEM(load.shape, F32),
            pltpu.VMEM(load.shape, F32),
            pltpu.VMEM((exchanges, 2, parts, size_x, size_z), F32),
            pltpu.VMEM((exchanges, 2, parts, size_x, size_z), F32),
        ]
        + [pltpu.SemaphoreType.DMA((exchanges, 2))] * 4,
        compiler_params=pltpu.CompilerParams(collective_id=0, has_side_effects=True),
        name="sweeps",
    )(load, stiffness, anchor, coupling)


def exchange_kernel(live, send, recv, send_sem, recv_sem, own_sem):
    count = send.shape[0]
    width = lax.axis_size("gy")
    me = lax.axis_index("gx") * width + lax.axis_index("gy")
    barrier = pltpu.get_barrier_semaphore()

    def device(index):
        return (index // width, index % width)

    def greet(step, carry):
        pl.semaphore_signal(barrier, inc=1, device_id=device((me + step) % count), device_id_type=MESH)
        return carry

    lax.fori_loop(1, count, greet, 0)
    pl.semaphore_wait(barrier, count - 1)

    def copy(step, source, landing):
        peer = (me + step) % count
        return pltpu.make_async_remote_copy(
            src_ref=send.at[source, pl.ds(0, live)],
            dst_ref=recv.at[landing, pl.ds(0, live)],
            send_sem=send_sem.at[step],
            recv_sem=recv_sem.at[step],
            device_id=device(peer),
            device_id_type=MESH,
        )

    def start(step, carry):
        copy(step, (me + step) % count, me).start()
        return carry

    lax.fori_loop(1, count, start, 0)
    own = pltpu.make_async_copy(send.at[me, pl.ds(0, live)], recv.at[me, pl.ds(0, live)], own_sem)
    own.start()

    def finish(step, carry):
        copy(step, (me + step) % count, (me + count - step) % count).wait_recv()
        copy(step, (me + step) % count, me).wait_send()
        return carry

    lax.fori_loop(1, count, finish, 0)
    own.wait()


def exchange(blocks, live, number):
    count = blocks.shape[0]
    return pl.pallas_call(
        functools.partial(exchange_kernel, live),
        out_shape=jax.ShapeDtypeStruct(blocks.shape, F32),
        in_specs=[pl.BlockSpec(memory_space=pltpu.VMEM)],
        out_specs=pl.BlockSpec(memory_space=pltpu.VMEM),
        scratch_shapes=[pltpu.SemaphoreType.DMA((count,))] * 2 + [pltpu.SemaphoreType.DMA],
        compiler_params=pltpu.CompilerParams(collective_id=number, has_side_effects=True),
        name="exchange_" + str(number),
    )(blocks)


def body(
    sensitivity,
    node_weight,
    dest_device,
    dest_cell,
    box_owner,
    box_slot,
    stiffness,
    anchor,
    coupling,
):
    devices = lax.axis_size("gx") * lax.axis_size("gy")
    row_count = sensitivity.shape[1]
    capacity = 2 * row_count // devices
    size_x, size_y, size_z = stiffness.shape
    size_xy = size_x * size_y
    assert size_xy * size_z <= 2**17 and devices * BOX_DEV <= 2**17

    def row(values):
        return values.reshape(1, row_count)

    packed = pack_rows(
        devices,
        capacity,
        sensitivity,
        row(node_weight),
        row(dest_device),
        row(dest_cell),
        row(box_owner),
        row(box_slot),
    )
    arrived = exchange(packed, SENT, 1)
    tiles, ends = sort_rows(arrived, size_x, size_y * size_z)
    load = scatter_rows(tiles, ends, size_x, size_y, size_z)
    load = load.reshape(3, size_x, size_y, size_z)
    adjoint = solve_sweeps(load, stiffness, anchor, coupling)
    partial = gather_rows(tiles, ends, adjoint)
    partial = exchange(partial.reshape(devices, 1, 3 * BOX_DEV), 1, 2)
    box_gradient = jnp.sum(partial, axis=(0, 1)).reshape(3, BOX_DEV)
    return (adjoint, box_gradient)


def solution(mesh):
    placed = (
        P(None, ("gx", "gy")),
        P(("gx", "gy")),
        P(("gx", "gy"), None),
        P(("gx", "gy")),
        P(("gx", "gy"), None),
        P(("gx", "gy")),
        P("gx", "gy", None),
        P(None, "gx", "gy", None),
        P(None, "gx", "gy", None),
    )
    return jax.shard_map(
        body,
        mesh=mesh,
        in_specs=placed,
        out_specs=(P(None, "gx", "gy", None), P(None, ("gx", "gy"))),
        check_vma=False,
    )
```

```python
import functools

import jax
import jax.numpy as jnp
from jax import lax
from jax.experimental import pallas as pl
from jax.experimental.pallas import tpu as pltpu
from jax.sharding import PartitionSpec as P

BOX_DEV = 64
SWEEPS = 4
SENT = 6
NT = (((1,), (1,)), ((), ()))
F32 = jnp.float32
BF16 = jnp.bfloat16
MESH = pl.DeviceIdType.MESH


def two_terms(x):
    hi = x.astype(BF16).astype(F32)
    return hi, x - hi


def matches(count, row):
    return lax.broadcasted_iota(jnp.int32, (count, row.shape[1]), 0) == row


def one_hot(mask):
    return jnp.where(mask, 1.0, 0.0).astype(BF16)


def scaled(mask, row):
    return jnp.where(mask, row, 0.0).astype(BF16)


def dot_nt(a, b):
    return lax.dot_general(a, b, NT, preferred_element_type=F32)


def pack_kernel(step, sens, weight, device, cell, owner, slot, out, tri, seen):
    targets, fields, capacity = out.shape
    rows = sens.shape[1]
    out[...] = jnp.zeros_like(out)
    seen[...] = jnp.zeros_like(seen)
    tri[...] = one_hot(
        lax.broadcasted_iota(jnp.int32, (step, step), 0)
        < lax.broadcasted_iota(jnp.int32, (step, step), 1)
    )

    def block(index, carry):
        span = pl.ds(pl.multiple_of(index * step, step), step)
        target = device[:, span]
        chosen = matches(targets, target)
        before = jnp.dot(one_hot(chosen), tri[...], preferred_element_type=F32) + seen[:, :1]
        rank = jnp.sum(jnp.where(chosen, before, 0.0), axis=0, keepdims=True).astype(jnp.int32)
        seen[...] = seen[...] + jnp.sum(jnp.where(chosen, 1.0, 0.0), axis=1, keepdims=True)
        place = one_hot(matches(capacity, rank))
        payload = jnp.concatenate(
            [
                sens[:, span],
                cell[:, span].astype(F32),
                weight[:, span],
                (owner[:, span] * BOX_DEV + slot[:, span]).astype(F32),
                jnp.zeros((fields - SENT, step), F32),
            ],
            axis=0,
        )
        wide = (targets, fields, step)
        to = lax.broadcasted_iota(jnp.int32, wide, 0) == target[None]
        terms = [
            jnp.where(to, term[None], 0.0).reshape(targets * fields, step).astype(BF16)
            for term in two_terms(payload)
        ]
        product = dot_nt(jnp.concatenate(terms, axis=0), place)
        product = product[: targets * fields] + product[targets * fields :]
        out[...] = out[...] + product.reshape(targets, fields, capacity)
        return carry

    lax.fori_loop(0, rows // step, block, 0)


def pack_rows(devices, capacity, sens, weight, device, cell, owner, slot):
    step = min(2048, sens.shape[1])
    return pl.pallas_call(
        functools.partial(pack_kernel, step),
        out_shape=jax.ShapeDtypeStruct((devices, 8, capacity), F32),
        in_specs=[pl.BlockSpec(memory_space=pltpu.VMEM)] * 6,
        out_specs=pl.BlockSpec(memory_space=pltpu.VMEM),
        scratch_shapes=[pltpu.VMEM((step, step), BF16), pltpu.VMEM((devices, 128), F32)],
        name="pack_rows",
    )(sens, weight, device, cell, owner, slot)


def split(value, size):
    if size & (size - 1) == 0:
        return value >> (size.bit_length() - 1), value & (size - 1)
    return value // size, value % size


def wide_matches(count, row):
    return lax.broadcasted_iota(jnp.int16, (count, row.shape[1]), 0) == row.astype(jnp.int16)


def wide_one_hot(count, row):
    return jnp.where(wide_matches(count, row), jnp.array(1, BF16), jnp.array(0, BF16))


def kept(mask, values):
    return jnp.where(mask, values, jnp.array(0, BF16))


def sort_kernel(cut, slabs, arrived, tiles, ends):
    senders, fields, capacity = arrived.shape
    per_group, _, width = tiles.shape
    join = max(1, min(senders, 512 // capacity))
    count, length = senders // join, join * capacity
    blocks = [
        jnp.concatenate([arrived[q * join + i] for i in range(join)], axis=1)
        for q in range(count)
    ]
    chosen = [matches(slabs, split(block[3:4].astype(jnp.int32), cut)[0]) for block in blocks]
    stacked = one_hot(jnp.concatenate(chosen, axis=0))
    total = count * slabs
    earlier = one_hot(
        lax.broadcasted_iota(jnp.int32, (length, length), 0)
        < lax.broadcasted_iota(jnp.int32, (length, length), 1)
    )
    before = jnp.dot(stacked, earlier, preferred_element_type=F32)
    number = jnp.dot(stacked, jnp.ones((length, 128), BF16), preferred_element_type=F32)
    this = lax.broadcasted_iota(jnp.int32, (total, total), 0)
    other = lax.broadcasted_iota(jnp.int32, (total, total), 1)
    ahead = one_hot((other % slabs < this % slabs) | ((other % slabs == this % slabs) & (other < this)))
    tens = jnp.floor(number * 0.0625)
    first = 16.0 * jnp.dot(ahead, tens.astype(BF16), preferred_element_type=F32)
    first = first + jnp.dot(ahead, (number - 16.0 * tens).astype(BF16), preferred_element_type=F32)

    steps = per_group + slabs - 1
    start = first[:slabs]
    row = lax.broadcasted_iota(jnp.int32, start.shape, 0).astype(F32)
    step = lax.broadcasted_iota(jnp.int32, start.shape, 1).astype(F32)
    entry = row + jnp.minimum(jnp.floor(start * (1.0 / width)), per_group - 1.0)
    slab = jnp.sum(jnp.where((row > 0) & (entry <= step), 1.0, 0.0), axis=0, keepdims=True)
    slab = jnp.where(step[:1] < steps, slab, slabs)
    ends[0] = jnp.broadcast_to(slab, (8, 128)).astype(jnp.int32)

    sums = jnp.zeros((per_group * 2 * fields, width), F32)
    for q in range(count):
        rows = slice(q * slabs, (q + 1) * slabs)
        where = before[rows] + first[rows, :1]
        place = jnp.sum(jnp.where(chosen[q], where, 0.0), axis=0, keepdims=True).astype(jnp.int32)
        tile, lane = split(place, width)
        terms = jnp.concatenate(two_terms(blocks[q]), axis=0).astype(BF16)
        tile = jnp.broadcast_to(tile, terms.shape).astype(jnp.int16)
        spread = jnp.concatenate([kept(tile == t, terms) for t in range(per_group)], axis=0)
        sums = sums + dot_nt(spread, wide_one_hot(width, lane))
    for t in range(per_group):
        at = t * 2 * fields
        tiles[t] = sums[at : at + fields] + sums[at + fields : at + 2 * fields]


def sort_rows(arrived, slabs, cut):
    devices, fields, capacity = arrived.shape
    rows = devices * capacity
    size = min(4096, rows)
    width = min(256, size)
    groups = rows // size
    return pl.pallas_call(
        functools.partial(sort_kernel, cut, slabs),
        grid=(groups,),
        out_shape=[
            jax.ShapeDtypeStruct((rows // width, fields, width), F32),
            jax.ShapeDtypeStruct((groups, 8, 128), jnp.int32),
        ],
        in_specs=[pl.BlockSpec((size // capacity, fields, capacity), lambda i: (i, 0, 0))],
        out_specs=[
            pl.BlockSpec((size // width, fields, width), lambda i: (i, 0, 0)),
            pl.BlockSpec((1, 8, 128), lambda i: (i, 0, 0)),
        ],
        name="sort_rows",
    )(arrived)


def located(tile, size_z):
    return split(tile[3:4].astype(jnp.int32), size_z)


def scatter_kernel(size_y, slabs_of, tiles, load):
    parts, size_xy, size_z = load.shape
    groups = slabs_of.shape[0]
    per_group = tiles.shape[0] // groups
    slabs = size_xy // size_y
    half = parts * size_y
    load[...] = jnp.zeros_like(load)

    def body(step, carry):
        made = []
        for group in range(groups):
            slab = slabs_of[group, 0, step]
            tile = tiles[group * per_group + jnp.minimum(step - slab, per_group - 1)]
            xy, z = located(tile, size_z)
            at_z = wide_one_hot(size_z, z)
            pairs = [two_terms(tile[k : k + 1]) for k in range(parts)]
            values = [hi for hi, lo in pairs] + [lo for hi, lo in pairs]
            at_y = matches(size_y, xy - slab * size_y)
            terms = jnp.concatenate([scaled(at_y, value) for value in values], axis=0)
            product = dot_nt(terms, at_z)
            made.append((slab, product[:half] + product[half:]))
        for slab, product in made:
            span = pl.ds(pl.multiple_of(jnp.minimum(slab, slabs - 1) * size_y, size_y), size_y)
            for k in range(parts):
                load[k, span] = load[k, span] + product[k * size_y : (k + 1) * size_y]
        return carry

    lax.fori_loop(0, per_group + slabs, body, 0, unroll=4)


def scatter_rows(tiles, ends, size_x, size_y, size_z):
    return pl.pallas_call(
        functools.partial(scatter_kernel, size_y),
        out_shape=jax.ShapeDtypeStruct((3, size_x * size_y, size_z), F32),
        in_specs=[pl.BlockSpec(memory_space=pltpu.SMEM), pl.BlockSpec(memory_space=pltpu.VMEM)],
        out_specs=pl.BlockSpec(memory_space=pltpu.VMEM),
        name="scatter_rows",
    )(ends, tiles)


def gather_kernel(slabs_of, tiles, field, boxes, terms, found):
    parts, size_x, size_y, size_z = field.shape
    groups = slabs_of.shape[0]
    count, _, width = tiles.shape
    per_group = count // groups
    devices = boxes.shape[0]
    half = parts * size_y

    def cut(x, carry):
        for k in range(parts):
            hi, lo = two_terms(field[k, x])
            terms[x, k * size_y : (k + 1) * size_y] = hi.astype(BF16)
            terms[x, half + k * size_y : half + (k + 1) * size_y] = lo.astype(BF16)
        return carry

    lax.fori_loop(0, size_x, cut, 0)
    found[...] = jnp.zeros_like(found)

    def body(step, carry):
        made = []
        for group in range(groups):
            slab = slabs_of[group, 0, step]
            number = group * per_group + jnp.minimum(step - slab, per_group - 1)
            tile = tiles[number]
            xy, z = located(tile, size_z)
            at_z = wide_one_hot(size_z, z)
            at_y = matches(size_y, xy - slab * size_y)
            columns = jnp.dot(terms[jnp.minimum(slab, size_x - 1)], at_z, preferred_element_type=F32)
            columns = columns[:half] + columns[half:]
            sums = [
                jnp.sum(jnp.where(at_y, columns[k * size_y : (k + 1) * size_y], 0.0), axis=0, keepdims=True)
                for k in range(parts)
            ]
            made.append((number, sums))
        for number, sums in made:
            for k in range(parts):
                found[k, pl.ds(number, 1)] = found[k, pl.ds(number, 1)] + sums[k]
        return carry

    lax.fori_loop(0, per_group + size_x, body, 0, unroll=4)
    total = jnp.zeros((2 * parts * devices, BOX_DEV), F32)
    join = 8
    for first in range(0, count, join):
        def line(field):
            return jnp.concatenate([tiles[t, field : field + 1] for t in range(first, first + join)], axis=1)
        owner, slot = split(line(5).astype(jnp.int32), BOX_DEV)
        weight = line(4)
        at_owner = matches(devices, owner)
        pairs = [two_terms(jnp.concatenate([found[k, t : t + 1] for t in range(first, first + join)], axis=1) * weight) for k in range(parts)]
        values = [hi for hi, lo in pairs] + [lo for hi, lo in pairs]
        spread = jnp.concatenate([scaled(at_owner, value) for value in values], axis=0)
        total = total + dot_nt(spread, one_hot(matches(BOX_DEV, slot)))
    for k in range(parts):
        part = total[k * devices : (k + 1) * devices] + total[(parts + k) * devices : (parts + k + 1) * devices]
        boxes[:, k * BOX_DEV : (k + 1) * BOX_DEV] = part


def gather_rows(tiles, ends, field, devices):
    groups = ends.shape[0]
    parts, size_x, size_y, size_z = field.shape
    return pl.pallas_call(
        gather_kernel,
        out_shape=jax.ShapeDtypeStruct((devices, 3 * BOX_DEV), F32),
        in_specs=[pl.BlockSpec(memory_space=pltpu.SMEM)] + [pl.BlockSpec(memory_space=pltpu.VMEM)] * 2,
        out_specs=pl.BlockSpec(memory_space=pltpu.VMEM),
        scratch_shapes=[
            pltpu.VMEM((size_x, 2 * parts * size_y, size_z), BF16),
            pltpu.VMEM((3, tiles.shape[0], tiles.shape[2]), F32),
        ],
        name="gather_rows",
    )(ends, tiles, field)


def sweep_kernel(load, stiff, anchor, coupling, adjoint, weighted, rest, inverse, edge, halo, x_send, x_recv, y_send, y_recv):
    parts, size_x, size_y, size_z = load.shape
    exchanges = weighted.shape[0]
    gx, gy = lax.axis_index("gx"), lax.axis_index("gy")
    last_x, last_y = lax.axis_size("gx") - 1, lax.axis_size("gy") - 1
    sides = (("gx", gx, -1, gx > 0), ("gx", gx, 1, gx < last_x), ("gy", gy, -1, gy > 0), ("gy", gy, 1, gy < last_y))
    y_at = lax.broadcasted_iota(jnp.int32, (size_y, size_z), 0)
    z_at = lax.broadcasted_iota(jnp.int32, (size_y, size_z), 1)

    for index in range(exchanges):
        for k in range(parts):
            weighted[index, k, 0] = jnp.zeros((size_y, size_z), F32)
            weighted[index, k, size_x + 1] = jnp.zeros((size_y, size_z), F32)
    halo[...] = jnp.zeros_like(halo)

    barrier = pltpu.get_barrier_semaphore()
    known = 0
    for axis, place, move, present in sides:
        known = known + present.astype(jnp.int32)

        @pl.when(present)
        def _():
            pl.semaphore_signal(barrier, inc=1, device_id={axis: place + move}, device_id_type=MESH)

    pl.semaphore_wait(barrier, known)

    def copies(index):
        made = []
        for side, (axis, place, move, present) in enumerate(sides):
            there = 1 - side % 2
            if axis == "gx":
                pair = (weighted.at[index, :, 1 if move < 0 else size_x], weighted.at[index, :, size_x + 1 if move < 0 else 0])
                sems = (x_send, x_recv)
            else:
                pair = (edge.at[index, side % 2], halo.at[index, there])
                sems = (y_send, y_recv)
            made.append((present, pltpu.make_async_remote_copy(
                src_ref=pair[0],
                dst_ref=pair[1],
                send_sem=sems[0].at[index, side % 2],
                recv_sem=sems[1].at[index, there],
                device_id={axis: place + move},
                device_id_type=MESH,
            )))
        return made

    def arrivals(index):
        made = []
        for side, (axis, place, move, present) in enumerate(sides):
            if axis == "gx":
                pair = (weighted.at[index, :, 1 if move < 0 else size_x], weighted.at[index, :, 0 if move < 0 else size_x + 1])
                sems = (x_send, x_recv)
            else:
                pair = (edge.at[index, side % 2], halo.at[index, side % 2])
                sems = (y_send, y_recv)
            made.append((present, pltpu.make_async_remote_copy(
                src_ref=pair[0],
                dst_ref=pair[1],
                send_sem=sems[0].at[index, side % 2],
                recv_sem=sems[1].at[index, side % 2],
                device_id={axis: place + move},
                device_id_type=MESH,
            )))
        return made

    def publish(index, x, k, value):
        adjoint[k, x] = value
        if index < exchanges:
            product = stiff[x] * value
            weighted[index, k, x + 1] = product
            edge[index, 0, k, pl.ds(x, 1), :] = product[0:1]
            edge[index, 1, k, pl.ds(x, 1), :] = product[size_y - 1 : size_y]

    def first(x, carry):
        for k in range(parts):
            inverse[k, x] = 1.0 / (6.0 * stiff[x] + anchor[k, x] + coupling[4 * k, x])
            publish(0, x, k, load[k, x] * inverse[k, x])
        return carry

    lax.fori_loop(0, size_x, first, 0)
    for index in range(exchanges):
        for present, copy in copies(index):

            @pl.when(present)
            def _():
                copy.start()

        def near(x, carry):
            fields = [adjoint[k, x] for k in range(parts)]
            for k in range(parts):
                product = weighted[index, k, x + 1]
                value = load[k, x]
                for j in range(parts):
                    if j != k:
                        value = value - coupling[3 * j + k, x] * fields[j]
                value = value + jnp.where(z_at == 0, 0.0, pltpu.roll(product, 1, 1))
                value = value + jnp.where(z_at == size_z - 1, 0.0, pltpu.roll(product, size_z - 1, 1))
                value = value + jnp.where(y_at == 0, 0.0, pltpu.roll(product, 1, 0))
                value = value + jnp.where(y_at == size_y - 1, 0.0, pltpu.roll(product, size_y - 1, 0))
                rest[k, x] = value
            return carry

        lax.fori_loop(0, size_x, near, 0)
        for present, copy in arrivals(index):

            @pl.when(present)
            def _():
                copy.wait_recv()

        def far(x, carry):
            for k in range(parts):
                value = rest[k, x] + weighted[index, k, x] + weighted[index, k, x + 2]
                value = value + jnp.where(y_at == 0, halo[index, 0, k, pl.ds(x, 1), :], 0.0)
                value = value + jnp.where(y_at == size_y - 1, halo[index, 1, k, pl.ds(x, 1), :], 0.0)
                publish(index + 1, x, k, value * inverse[k, x])
            return carry

        lax.fori_loop(0, size_x, far, 0)
    for index in range(exchanges):
        for present, copy in copies(index):

            @pl.when(present)
            def _():
                copy.wait_send()


def solve_sweeps(load, stiffness, anchor, coupling):
    parts, size_x, size_y, size_z = load.shape
    exchanges = SWEEPS - 1
    return pl.pallas_call(
        sweep_kernel,
        out_shape=jax.ShapeDtypeStruct(load.shape, F32),
        in_specs=[pl.BlockSpec(memory_space=pltpu.VMEM)] * 4,
        out_specs=pl.BlockSpec(memory_space=pltpu.VMEM),
        scratch_shapes=[
            pltpu.VMEM((exchanges, parts, size_x + 2, size_y, size_z), F32),
            pltpu.VMEM(load.shape, F32),
            pltpu.VMEM(load.shape, F32),
            pltpu.VMEM((exchanges, 2, parts, size_x, size_z), F32),
            pltpu.VMEM((exchanges, 2, parts, size_x, size_z), F32),
        ]
        + [pltpu.SemaphoreType.DMA((exchanges, 2))] * 4,
        compiler_params=pltpu.CompilerParams(collective_id=0, has_side_effects=True),
        name="sweeps",
    )(load, stiffness, anchor, coupling)


def exchange_kernel(live, send, recv, send_sem, recv_sem, own_sem):
    count = send.shape[0]
    width = lax.axis_size("gy")
    me = lax.axis_index("gx") * width + lax.axis_index("gy")
    barrier = pltpu.get_barrier_semaphore()

    def device(index):
        return (index // width, index % width)

    def greet(step, carry):
        pl.semaphore_signal(barrier, inc=1, device_id=device((me + step) % count), device_id_type=MESH)
        return carry

    lax.fori_loop(1, count, greet, 0)
    pl.semaphore_wait(barrier, count - 1)

    def copy(step, source, landing):
        peer = (me + step) % count
        return pltpu.make_async_remote_copy(
            src_ref=send.at[source, pl.ds(0, live)],
            dst_ref=recv.at[landing, pl.ds(0, live)],
            send_sem=send_sem.at[step],
            recv_sem=recv_sem.at[step],
            device_id=device(peer),
            device_id_type=MESH,
        )

    def start(step, carry):
        copy(step, (me + step) % count, me).start()
        return carry

    lax.fori_loop(1, count, start, 0)
    own = pltpu.make_async_copy(send.at[me, pl.ds(0, live)], recv.at[me, pl.ds(0, live)], own_sem)
    own.start()

    def finish(step, carry):
        copy(step, (me + step) % count, (me + count - step) % count).wait_recv()
        copy(step, (me + step) % count, me).wait_send()
        return carry

    lax.fori_loop(1, count, finish, 0)
    own.wait()


def exchange(blocks, live, number):
    count = blocks.shape[0]
    return pl.pallas_call(
        functools.partial(exchange_kernel, live),
        out_shape=jax.ShapeDtypeStruct(blocks.shape, F32),
        in_specs=[pl.BlockSpec(memory_space=pltpu.VMEM)],
        out_specs=pl.BlockSpec(memory_space=pltpu.VMEM),
        scratch_shapes=[pltpu.SemaphoreType.DMA((count,))] * 2 + [pltpu.SemaphoreType.DMA],
        compiler_params=pltpu.CompilerParams(collective_id=number, has_side_effects=True),
        name="exchange_" + str(number),
    )(blocks)


def body(
    sensitivity,
    node_weight,
    dest_device,
    dest_cell,
    box_owner,
    box_slot,
    stiffness,
    anchor,
    coupling,
):
    devices = lax.axis_size("gx") * lax.axis_size("gy")
    row_count = sensitivity.shape[1]
    capacity = 2 * row_count // devices
    size_x, size_y, size_z = stiffness.shape
    size_xy = size_x * size_y
    assert size_xy * size_z <= 2**17 and devices * BOX_DEV <= 2**17

    def row(values):
        return values.reshape(1, row_count)

    packed = pack_rows(
        devices,
        capacity,
        sensitivity,
        row(node_weight),
        row(dest_device),
        row(dest_cell),
        row(box_owner),
        row(box_slot),
    )
    arrived = exchange(packed, SENT, 1)
    tiles, ends = sort_rows(arrived, size_x, size_y * size_z)
    load = scatter_rows(tiles, ends, size_x, size_y, size_z)
    load = load.reshape(3, size_x, size_y, size_z)
    adjoint = solve_sweeps(load, stiffness, anchor, coupling)
    partial = gather_rows(tiles, ends, adjoint, devices)
    partial = exchange(partial.reshape(devices, 1, 3 * BOX_DEV), 1, 2)
    box_gradient = jnp.sum(partial, axis=(0, 1)).reshape(3, BOX_DEV)
    return (adjoint, box_gradient)


def solution(mesh):
    placed = (
        P(None, ("gx", "gy")),
        P(("gx", "gy")),
        P(("gx", "gy"), None),
        P(("gx", "gy")),
        P(("gx", "gy"), None),
        P(("gx", "gy")),
        P("gx", "gy", None),
        P(None, "gx", "gy", None),
        P(None, "gx", "gy", None),
    )
    return jax.shard_map(
        body,
        mesh=mesh,
        in_specs=placed,
        out_specs=(P(None, "gx", "gy", None), P(None, ("gx", "gy"))),
        check_vma=False,
    )
```

```python
import functools

import jax
import jax.numpy as jnp
from jax import lax
from jax.experimental import pallas as pl
from jax.experimental.pallas import tpu as pltpu
from jax.sharding import PartitionSpec as P

BOX_DEV = 64
SWEEPS = 4
SENT = 6
NT = (((1,), (1,)), ((), ()))
F32 = jnp.float32
BF16 = jnp.bfloat16
MESH = pl.DeviceIdType.MESH


def two_terms(x):
    hi = x.astype(BF16).astype(F32)
    return hi, x - hi


def matches(count, row):
    return lax.broadcasted_iota(jnp.int32, (count, row.shape[1]), 0) == row


def one_hot(mask):
    return jnp.where(mask, 1.0, 0.0).astype(BF16)


def scaled(mask, row):
    return jnp.where(mask, row, 0.0).astype(BF16)


def dot_nt(a, b):
    return lax.dot_general(a, b, NT, preferred_element_type=F32)


def split(value, size):
    if size & (size - 1) == 0:
        return value >> (size.bit_length() - 1), value & (size - 1)
    return value // size, value % size


def wide_matches(count, row):
    return lax.broadcasted_iota(jnp.int16, (count, row.shape[1]), 0) == row.astype(jnp.int16)


def wide_one_hot(count, row):
    return jnp.where(wide_matches(count, row), jnp.array(1, BF16), jnp.array(0, BF16))


def kept(mask, values):
    return jnp.where(mask, values, jnp.array(0, BF16))


def running(numbers):
    totals = [jnp.zeros_like(numbers[0])]
    for number in numbers:
        totals.append(totals[-1] + number)
    return totals


def ordinals(chosen):
    length = chosen[0].shape[1]
    stacked = one_hot(jnp.concatenate(chosen, axis=0))
    earlier = one_hot(
        lax.broadcasted_iota(jnp.int32, (length, length), 0)
        < lax.broadcasted_iota(jnp.int32, (length, length), 1)
    )
    before = jnp.dot(stacked, earlier, preferred_element_type=F32)
    number = jnp.dot(stacked, jnp.ones((length, 128), BF16), preferred_element_type=F32)
    size = chosen[0].shape[0]

    def cut(values):
        return [values[q * size : (q + 1) * size] for q in range(len(chosen))]

    return cut(before), cut(number)


def picked(mask, value):
    return jnp.sum(jnp.where(mask, value, 0.0), axis=0, keepdims=True)


def relay_kernel(cut, slabs, parts, sens, weight, device, cell, owner, slot, tiles, slab_of, send, recv, place, spread, send_sem, recv_sem):
    count, fields, capacity = send.shape
    rows = sens.shape[1]
    _, _, width = tiles.shape
    groups = slab_of.shape[0]
    per_group = tiles.shape[0] // groups
    gx, gy = lax.axis_index("gx"), lax.axis_index("gy")
    size_x, size_y = lax.axis_size("gx"), lax.axis_size("gy")
    me = gx * size_y + gy
    barrier = pltpu.get_barrier_semaphore()

    def peer(step):
        there = (me + step) % count
        return (there // size_y, there % size_y)

    def greet(step, carry):
        pl.semaphore_signal(barrier, inc=1, device_id=peer(step), device_id_type=MESH)
        return carry

    lax.fori_loop(1, count, greet, 0)

    length = min(512, rows)
    chunks = rows // length
    spans = [slice(q * length, (q + 1) * length) for q in range(chunks)]
    target = device[...] - me
    target = jnp.where(target < 0, target + count, target)
    chosen = [matches(count, target[:, span]) for span in spans]
    before, number = ordinals(chosen)
    total = running(number)
    for q, span in enumerate(spans):
        rank = picked(chosen[q], before[q] + total[q][:, :1]).astype(jnp.int32)
        place[:, span] = wide_one_hot(capacity, rank)

    def copy(step):
        return pltpu.make_async_remote_copy(
            src_ref=send.at[step, pl.ds(0, SENT)],
            dst_ref=recv.at[step, pl.ds(0, SENT)],
            send_sem=send_sem.at[step],
            recv_sem=recv_sem.at[step],
            device_id=peer(step),
            device_id_type=MESH,
        )

    def start(step, carry):
        copy(step).start()
        return carry

    share = count // parts
    for part in reversed(range(parts)):
        for q, span in enumerate(spans):
            payload = jnp.concatenate(
                [
                    sens[:, span],
                    cell[:, span].astype(F32),
                    weight[:, span],
                    (owner[:, span] * BOX_DEV + slot[:, span]).astype(F32),
                    jnp.zeros((fields - SENT, length), F32),
                ],
                axis=0,
            )
            terms = jnp.concatenate(two_terms(payload), axis=0).astype(BF16)
            to = jnp.broadcast_to(target[:, span] - part * share, terms.shape).astype(jnp.int16)
            for t in range(share):
                spread[t * 2 * fields : (t + 1) * 2 * fields, span] = kept(to == t, terms)
        product = dot_nt(spread[...], place[...])
        for t in range(share):
            at = t * 2 * fields
            send[part * share + t] = product[at : at + fields] + product[at + fields : at + 2 * fields]
        if part == parts - 1:
            pl.semaphore_wait(barrier, count - 1)
        lax.fori_loop(max(1, part * share), (part + 1) * share, start, 0)

    recv[0] = send[0]

    def arrive(step, carry):
        copy(step).wait_recv()
        return carry

    senders = count // groups
    for group in reversed(range(groups)):
        lax.fori_loop(max(1, group * senders), (group + 1) * senders, arrive, 0)
        sort_group(cut, slabs, [recv.at[group * senders + i] for i in range(senders)], tiles, group * per_group, per_group, slab_of, group)

    def sent(step, carry):
        copy(step).wait_send()
        return carry

    lax.fori_loop(1, count, sent, 0)


def sort_group(cut, slabs, arrived, tiles, first, per_group, slab_of, group):
    senders = len(arrived)
    fields, capacity = arrived[0].shape
    width = tiles.shape[2]
    join = max(1, min(senders, 512 // capacity))
    count = senders // join
    real = lax.broadcasted_iota(jnp.int32, (fields, join * capacity), 0) < SENT
    blocks = [
        jnp.where(real, jnp.concatenate([arrived[q * join + i][...] for i in range(join)], axis=1), 0.0)
        for q in range(count)
    ]
    chosen = [matches(slabs, split(block[3:4].astype(jnp.int32), cut)[0]) for block in blocks]
    before, number = ordinals(chosen)
    total = running(number)
    lower = one_hot(
        lax.broadcasted_iota(jnp.int32, (slabs, slabs), 1)
        < lax.broadcasted_iota(jnp.int32, (slabs, slabs), 0)
    )
    tens = jnp.floor(total[-1] * 0.0625)
    start = 16.0 * jnp.dot(lower, tens.astype(BF16), preferred_element_type=F32)
    start = start + jnp.dot(lower, (total[-1] - 16.0 * tens).astype(BF16), preferred_element_type=F32)

    steps = per_group + slabs - 1
    row = lax.broadcasted_iota(jnp.int32, start.shape, 0).astype(F32)
    step = lax.broadcasted_iota(jnp.int32, start.shape, 1).astype(F32)
    entry = row + jnp.minimum(jnp.floor(start * (1.0 / width)), per_group - 1.0)
    slab = jnp.sum(jnp.where((row > 0) & (entry <= step), 1.0, 0.0), axis=0, keepdims=True)
    slab = jnp.where(step[:1] < steps, slab, slabs)
    slab_of[group] = jnp.broadcast_to(slab, (8, 128)).astype(jnp.int32)

    sums = jnp.zeros((per_group * 2 * fields, width), F32)
    for q in range(count):
        where = picked(chosen[q], before[q] + (total[q] + start)[:, :1]).astype(jnp.int32)
        tile, lane = split(where, width)
        terms = jnp.concatenate(two_terms(blocks[q]), axis=0).astype(BF16)
        tile = jnp.broadcast_to(tile, terms.shape).astype(jnp.int16)
        spread = jnp.concatenate([kept(tile == t, terms) for t in range(per_group)], axis=0)
        sums = sums + dot_nt(spread, wide_one_hot(width, lane))
    for t in range(per_group):
        at = t * 2 * fields
        tiles[first + t] = sums[at : at + fields] + sums[at + fields : at + 2 * fields]


def relay_rows(devices, capacity, slabs, cut, sens, weight, device, cell, owner, slot):
    rows = devices * capacity
    size = min(4096, rows)
    width = min(256, size)
    groups = rows // size
    parts = 2
    return pl.pallas_call(
        functools.partial(relay_kernel, cut, slabs, parts),
        out_shape=[
            jax.ShapeDtypeStruct((rows // width, 8, width), F32),
            jax.ShapeDtypeStruct((groups, 8, 128), jnp.int32),
        ],
        in_specs=[pl.BlockSpec(memory_space=pltpu.VMEM)] * 6,
        out_specs=[pl.BlockSpec(memory_space=pltpu.VMEM)] * 2,
        scratch_shapes=[
            pltpu.VMEM((devices, 8, capacity), F32),
            pltpu.VMEM((devices, 8, capacity), F32),
            pltpu.VMEM((capacity, sens.shape[1]), BF16),
            pltpu.VMEM((devices // parts * 16, sens.shape[1]), BF16),
        ]
        + [pltpu.SemaphoreType.DMA((devices,))] * 2,
        compiler_params=pltpu.CompilerParams(collective_id=1, has_side_effects=True),
        name="relay_rows",
    )(sens, weight, device, cell, owner, slot)


def located(tile, size_z):
    return split(tile[3:4].astype(jnp.int32), size_z)


def scatter_kernel(size_y, slabs_of, tiles, load):
    parts, size_xy, size_z = load.shape
    groups = slabs_of.shape[0]
    per_group = tiles.shape[0] // groups
    slabs = size_xy // size_y
    half = parts * size_y
    load[...] = jnp.zeros_like(load)

    def body(step, carry):
        made = []
        for group in range(groups):
            slab = slabs_of[group, 0, step]
            tile = tiles[group * per_group + jnp.minimum(step - slab, per_group - 1)]
            xy, z = located(tile, size_z)
            at_z = wide_one_hot(size_z, z)
            pairs = [two_terms(tile[k : k + 1]) for k in range(parts)]
            values = [hi for hi, lo in pairs] + [lo for hi, lo in pairs]
            at_y = matches(size_y, xy - slab * size_y)
            terms = jnp.concatenate([scaled(at_y, value) for value in values], axis=0)
            product = dot_nt(terms, at_z)
            made.append((slab, product[:half] + product[half:]))
        for slab, product in made:
            span = pl.ds(pl.multiple_of(jnp.minimum(slab, slabs - 1) * size_y, size_y), size_y)
            for k in range(parts):
                load[k, span] = load[k, span] + product[k * size_y : (k + 1) * size_y]
        return carry

    lax.fori_loop(0, per_group + slabs, body, 0, unroll=4)


def scatter_rows(tiles, ends, size_x, size_y, size_z):
    return pl.pallas_call(
        functools.partial(scatter_kernel, size_y),
        out_shape=jax.ShapeDtypeStruct((3, size_x * size_y, size_z), F32),
        in_specs=[pl.BlockSpec(memory_space=pltpu.SMEM), pl.BlockSpec(memory_space=pltpu.VMEM)],
        out_specs=pl.BlockSpec(memory_space=pltpu.VMEM),
        name="scatter_rows",
    )(ends, tiles)


def gather_kernel(slabs_of, tiles, field, boxes, terms, found):
    parts, size_x, size_y, size_z = field.shape
    groups = slabs_of.shape[0]
    count, _, width = tiles.shape
    per_group = count // groups
    devices = boxes.shape[0]
    half = parts * size_y

    def cut(x, carry):
        for k in range(parts):
            hi, lo = two_terms(field[k, x])
            terms[x, k * size_y : (k + 1) * size_y] = hi.astype(BF16)
            terms[x, half + k * size_y : half + (k + 1) * size_y] = lo.astype(BF16)
        return carry

    lax.fori_loop(0, size_x, cut, 0)
    found[...] = jnp.zeros_like(found)

    def body(step, carry):
        made = []
        for group in range(groups):
            slab = slabs_of[group, 0, step]
            number = group * per_group + jnp.minimum(step - slab, per_group - 1)
            tile = tiles[number]
            xy, z = located(tile, size_z)
            at_z = wide_one_hot(size_z, z)
            at_y = matches(size_y, xy - slab * size_y)
            columns = jnp.dot(terms[jnp.minimum(slab, size_x - 1)], at_z, preferred_element_type=F32)
            columns = columns[:half] + columns[half:]
            sums = [
                jnp.sum(jnp.where(at_y, columns[k * size_y : (k + 1) * size_y], 0.0), axis=0, keepdims=True)
                for k in range(parts)
            ]
            made.append((number, sums))
        for number, sums in made:
            for k in range(parts):
                found[k, pl.ds(number, 1)] = found[k, pl.ds(number, 1)] + sums[k]
        return carry

    lax.fori_loop(0, per_group + size_x, body, 0, unroll=4)
    total = jnp.zeros((2 * parts * devices, BOX_DEV), F32)
    join = 8
    for first in range(0, count, join):
        def line(field):
            return jnp.concatenate([tiles[t, field : field + 1] for t in range(first, first + join)], axis=1)
        owner, slot = split(line(5).astype(jnp.int32), BOX_DEV)
        weight = line(4)
        at_owner = matches(devices, owner)
        pairs = [two_terms(jnp.concatenate([found[k, t : t + 1] for t in range(first, first + join)], axis=1) * weight) for k in range(parts)]
        values = [hi for hi, lo in pairs] + [lo for hi, lo in pairs]
        spread = jnp.concatenate([scaled(at_owner, value) for value in values], axis=0)
        total = total + dot_nt(spread, one_hot(matches(BOX_DEV, slot)))
    for k in range(parts):
        part = total[k * devices : (k + 1) * devices] + total[(parts + k) * devices : (parts + k + 1) * devices]
        boxes[:, k * BOX_DEV : (k + 1) * BOX_DEV] = part


def gather_rows(tiles, ends, field, devices):
    groups = ends.shape[0]
    parts, size_x, size_y, size_z = field.shape
    return pl.pallas_call(
        gather_kernel,
        out_shape=jax.ShapeDtypeStruct((devices, 3 * BOX_DEV), F32),
        in_specs=[pl.BlockSpec(memory_space=pltpu.SMEM)] + [pl.BlockSpec(memory_space=pltpu.VMEM)] * 2,
        out_specs=pl.BlockSpec(memory_space=pltpu.VMEM),
        scratch_shapes=[
            pltpu.VMEM((size_x, 2 * parts * size_y, size_z), BF16),
            pltpu.VMEM((3, tiles.shape[0], tiles.shape[2]), F32),
        ],
        name="gather_rows",
    )(ends, tiles, field)


def sweep_kernel(load, stiff, anchor, coupling, adjoint, weighted, rest, inverse, edge, halo, x_send, x_recv, y_send, y_recv):
    parts, size_x, size_y, size_z = load.shape
    exchanges = weighted.shape[0]
    gx, gy = lax.axis_index("gx"), lax.axis_index("gy")
    last_x, last_y = lax.axis_size("gx") - 1, lax.axis_size("gy") - 1
    sides = (("gx", gx, -1, gx > 0), ("gx", gx, 1, gx < last_x), ("gy", gy, -1, gy > 0), ("gy", gy, 1, gy < last_y))
    y_at = lax.broadcasted_iota(jnp.int32, (size_y, size_z), 0)
    z_at = lax.broadcasted_iota(jnp.int32, (size_y, size_z), 1)

    for index in range(exchanges):
        for k in range(parts):
            weighted[index, k, 0] = jnp.zeros((size_y, size_z), F32)
            weighted[index, k, size_x + 1] = jnp.zeros((size_y, size_z), F32)
    halo[...] = jnp.zeros_like(halo)

    barrier = pltpu.get_barrier_semaphore()
    known = 0
    for axis, place, move, present in sides:
        known = known + present.astype(jnp.int32)

        @pl.when(present)
        def _():
            pl.semaphore_signal(barrier, inc=1, device_id={axis: place + move}, device_id_type=MESH)

    pl.semaphore_wait(barrier, known)

    def copies(index):
        made = []
        for side, (axis, place, move, present) in enumerate(sides):
            there = 1 - side % 2
            if axis == "gx":
                pair = (weighted.at[index, :, 1 if move < 0 else size_x], weighted.at[index, :, size_x + 1 if move < 0 else 0])
                sems = (x_send, x_recv)
            else:
                pair = (edge.at[index, side % 2], halo.at[index, there])
                sems = (y_send, y_recv)
            made.append((present, pltpu.make_async_remote_copy(
                src_ref=pair[0],
                dst_ref=pair[1],
                send_sem=sems[0].at[index, side % 2],
                recv_sem=sems[1].at[index, there],
                device_id={axis: place + move},
                device_id_type=MESH,
            )))
        return made

    def arrivals(index):
        made = []
        for side, (axis, place, move, present) in enumerate(sides):
            if axis == "gx":
                pair = (weighted.at[index, :, 1 if move < 0 else size_x], weighted.at[index, :, 0 if move < 0 else size_x + 1])
                sems = (x_send, x_recv)
            else:
                pair = (edge.at[index, side % 2], halo.at[index, side % 2])
                sems = (y_send, y_recv)
            made.append((present, pltpu.make_async_remote_copy(
                src_ref=pair[0],
                dst_ref=pair[1],
                send_sem=sems[0].at[index, side % 2],
                recv_sem=sems[1].at[index, side % 2],
                device_id={axis: place + move},
                device_id_type=MESH,
            )))
        return made

    def publish(index, x, k, value):
        adjoint[k, x] = value
        if index < exchanges:
            product = stiff[x] * value
            weighted[index, k, x + 1] = product
            edge[index, 0, k, pl.ds(x, 1), :] = product[0:1]
            edge[index, 1, k, pl.ds(x, 1), :] = product[size_y - 1 : size_y]

    def first(x, carry):
        for k in range(parts):
            inverse[k, x] = 1.0 / (6.0 * stiff[x] + anchor[k, x] + coupling[4 * k, x])
            publish(0, x, k, load[k, x] * inverse[k, x])
        return carry

    lax.fori_loop(0, size_x, first, 0)
    for index in range(exchanges):
        for present, copy in copies(index):

            @pl.when(present)
            def _():
                copy.start()

        def near(x, carry):
            fields = [adjoint[k, x] for k in range(parts)]
            for k in range(parts):
                product = weighted[index, k, x + 1]
                value = load[k, x]
                for j in range(parts):
                    if j != k:
                        value = value - coupling[3 * j + k, x] * fields[j]
                value = value + jnp.where(z_at == 0, 0.0, pltpu.roll(product, 1, 1))
                value = value + jnp.where(z_at == size_z - 1, 0.0, pltpu.roll(product, size_z - 1, 1))
                value = value + jnp.where(y_at == 0, 0.0, pltpu.roll(product, 1, 0))
                value = value + jnp.where(y_at == size_y - 1, 0.0, pltpu.roll(product, size_y - 1, 0))
                rest[k, x] = value
            return carry

        lax.fori_loop(0, size_x, near, 0)
        for present, copy in arrivals(index):

            @pl.when(present)
            def _():
                copy.wait_recv()

        def far(x, carry):
            for k in range(parts):
                value = rest[k, x] + weighted[index, k, x] + weighted[index, k, x + 2]
                value = value + jnp.where(y_at == 0, halo[index, 0, k, pl.ds(x, 1), :], 0.0)
                value = value + jnp.where(y_at == size_y - 1, halo[index, 1, k, pl.ds(x, 1), :], 0.0)
                publish(index + 1, x, k, value * inverse[k, x])
            return carry

        lax.fori_loop(0, size_x, far, 0)
    for index in range(exchanges):
        for present, copy in copies(index):

            @pl.when(present)
            def _():
                copy.wait_send()


def solve_sweeps(load, stiffness, anchor, coupling):
    parts, size_x, size_y, size_z = load.shape
    exchanges = SWEEPS - 1
    return pl.pallas_call(
        sweep_kernel,
        out_shape=jax.ShapeDtypeStruct(load.shape, F32),
        in_specs=[pl.BlockSpec(memory_space=pltpu.VMEM)] * 4,
        out_specs=pl.BlockSpec(memory_space=pltpu.VMEM),
        scratch_shapes=[
            pltpu.VMEM((exchanges, parts, size_x + 2, size_y, size_z), F32),
            pltpu.VMEM(load.shape, F32),
            pltpu.VMEM(load.shape, F32),
            pltpu.VMEM((exchanges, 2, parts, size_x, size_z), F32),
            pltpu.VMEM((exchanges, 2, parts, size_x, size_z), F32),
        ]
        + [pltpu.SemaphoreType.DMA((exchanges, 2))] * 4,
        compiler_params=pltpu.CompilerParams(collective_id=0, has_side_effects=True),
        name="sweeps",
    )(load, stiffness, anchor, coupling)


def exchange_kernel(live, send, recv, send_sem, recv_sem, own_sem):
    count = send.shape[0]
    width = lax.axis_size("gy")
    me = lax.axis_index("gx") * width + lax.axis_index("gy")
    barrier = pltpu.get_barrier_semaphore()

    def device(index):
        return (index // width, index % width)

    def greet(step, carry):
        pl.semaphore_signal(barrier, inc=1, device_id=device((me + step) % count), device_id_type=MESH)
        return carry

    lax.fori_loop(1, count, greet, 0)
    pl.semaphore_wait(barrier, count - 1)

    def copy(step, source, landing):
        peer = (me + step) % count
        return pltpu.make_async_remote_copy(
            src_ref=send.at[source, pl.ds(0, live)],
            dst_ref=recv.at[landing, pl.ds(0, live)],
            send_sem=send_sem.at[step],
            recv_sem=recv_sem.at[step],
            device_id=device(peer),
            device_id_type=MESH,
        )

    def start(step, carry):
        copy(step, (me + step) % count, me).start()
        return carry

    lax.fori_loop(1, count, start, 0)
    own = pltpu.make_async_copy(send.at[me, pl.ds(0, live)], recv.at[me, pl.ds(0, live)], own_sem)
    own.start()

    def finish(step, carry):
        copy(step, (me + step) % count, (me + count - step) % count).wait_recv()
        copy(step, (me + step) % count, me).wait_send()
        return carry

    lax.fori_loop(1, count, finish, 0)
    own.wait()


def exchange(blocks, live, number):
    count = blocks.shape[0]
    return pl.pallas_call(
        functools.partial(exchange_kernel, live),
        out_shape=jax.ShapeDtypeStruct(blocks.shape, F32),
        in_specs=[pl.BlockSpec(memory_space=pltpu.VMEM)],
        out_specs=pl.BlockSpec(memory_space=pltpu.VMEM),
        scratch_shapes=[pltpu.SemaphoreType.DMA((count,))] * 2 + [pltpu.SemaphoreType.DMA],
        compiler_params=pltpu.CompilerParams(collective_id=number, has_side_effects=True),
        name="exchange_" + str(number),
    )(blocks)


def body(
    sensitivity,
    node_weight,
    dest_device,
    dest_cell,
    box_owner,
    box_slot,
    stiffness,
    anchor,
    coupling,
):
    devices = lax.axis_size("gx") * lax.axis_size("gy")
    row_count = sensitivity.shape[1]
    capacity = 2 * row_count // devices
    size_x, size_y, size_z = stiffness.shape
    size_xy = size_x * size_y
    assert size_xy * size_z <= 2**17 and devices * BOX_DEV <= 2**17

    def row(values):
        return values.reshape(1, row_count)

    tiles, ends = relay_rows(
        devices,
        capacity,
        size_x,
        size_y * size_z,
        sensitivity,
        row(node_weight),
        row(dest_device),
        row(dest_cell),
        row(box_owner),
        row(box_slot),
    )
    load = scatter_rows(tiles, ends, size_x, size_y, size_z)
    load = load.reshape(3, size_x, size_y, size_z)
    adjoint = solve_sweeps(load, stiffness, anchor, coupling)
    partial = gather_rows(tiles, ends, adjoint, devices)
    partial = exchange(partial.reshape(devices, 1, 3 * BOX_DEV), 1, 2)
    box_gradient = jnp.sum(partial, axis=(0, 1)).reshape(3, BOX_DEV)
    return (adjoint, box_gradient)


def solution(mesh):
    placed = (
        P(None, ("gx", "gy")),
        P(("gx", "gy")),
        P(("gx", "gy"), None),
        P(("gx", "gy")),
        P(("gx", "gy"), None),
        P(("gx", "gy")),
        P("gx", "gy", None),
        P(None, "gx", "gy", None),
        P(None, "gx", "gy", None),
    )
    return jax.shard_map(
        body,
        mesh=mesh,
        in_specs=placed,
        out_specs=(P(None, "gx", "gy", None), P(None, ("gx", "gy"))),
        check_vma=False,
    )
```

```python
import functools

import jax
import jax.numpy as jnp
from jax import lax
from jax.experimental import pallas as pl
from jax.experimental.pallas import tpu as pltpu
from jax.sharding import PartitionSpec as P

BOX_DEV = 64
SWEEPS = 4
SENT = 6
NT = (((1,), (1,)), ((), ()))
F32 = jnp.float32
BF16 = jnp.bfloat16
MESH = pl.DeviceIdType.MESH


def two_terms(x):
    hi = x.astype(BF16).astype(F32)
    return hi, x - hi


def matches(count, row):
    return lax.broadcasted_iota(jnp.int32, (count, row.shape[1]), 0) == row


def one_hot(mask):
    return jnp.where(mask, 1.0, 0.0).astype(BF16)


def scaled(mask, row):
    return jnp.where(mask, row, 0.0).astype(BF16)


def dot_nt(a, b):
    return lax.dot_general(a, b, NT, preferred_element_type=F32)


def split(value, size):
    if size & (size - 1) == 0:
        return value >> (size.bit_length() - 1), value & (size - 1)
    return value // size, value % size


def wide_matches(count, row):
    return lax.broadcasted_iota(jnp.int16, (count, row.shape[1]), 0) == row.astype(jnp.int16)


def wide_one_hot(count, row):
    return jnp.where(wide_matches(count, row), jnp.array(1, BF16), jnp.array(0, BF16))


def kept(mask, values):
    return jnp.where(mask, values, jnp.array(0, BF16))


def running(numbers):
    totals = [jnp.zeros_like(numbers[0])]
    for number in numbers:
        totals.append(totals[-1] + number)
    return totals


def ordinals(chosen):
    length = chosen[0].shape[1]
    stacked = one_hot(jnp.concatenate(chosen, axis=0))
    earlier = one_hot(
        lax.broadcasted_iota(jnp.int32, (length, length), 0)
        < lax.broadcasted_iota(jnp.int32, (length, length), 1)
    )
    before = jnp.dot(stacked, earlier, preferred_element_type=F32)
    number = jnp.dot(stacked, jnp.ones((length, 128), BF16), preferred_element_type=F32)
    size = chosen[0].shape[0]

    def cut(values):
        return [values[q * size : (q + 1) * size] for q in range(len(chosen))]

    return cut(before), cut(number)


def picked(mask, value):
    return jnp.sum(jnp.where(mask, value, 0.0), axis=0, keepdims=True)


def relay_kernel(cut, slabs, parts, sens, weight, device, cell, owner, slot, tiles, slab_of, send, recv, place, spread, send_sem, recv_sem):
    count, fields, capacity = send.shape
    rows = sens.shape[1]
    _, _, width = tiles.shape
    groups = slab_of.shape[0]
    per_group = tiles.shape[0] // groups
    gx, gy = lax.axis_index("gx"), lax.axis_index("gy")
    size_x, size_y = lax.axis_size("gx"), lax.axis_size("gy")
    me = gx * size_y + gy
    barrier = pltpu.get_barrier_semaphore()

    def peer(step):
        there = (me + step) % count
        return (there // size_y, there % size_y)

    def greet(step, carry):
        pl.semaphore_signal(barrier, inc=1, device_id=peer(step), device_id_type=MESH)
        return carry

    lax.fori_loop(1, count, greet, 0)

    length = min(512, rows)
    chunks = rows // length
    spans = [slice(q * length, (q + 1) * length) for q in range(chunks)]
    target = device[...] - me
    target = jnp.where(target < 0, target + count, target)
    chosen = [matches(count, target[:, span]) for span in spans]
    before, number = ordinals(chosen)
    total = running(number)
    for q, span in enumerate(spans):
        rank = picked(chosen[q], before[q] + total[q][:, :1]).astype(jnp.int32)
        place[:, span] = wide_one_hot(capacity, rank)

    def copy(step):
        return pltpu.make_async_remote_copy(
            src_ref=send.at[step, pl.ds(0, SENT)],
            dst_ref=recv.at[step, pl.ds(0, SENT)],
            send_sem=send_sem.at[step],
            recv_sem=recv_sem.at[step],
            device_id=peer(step),
            device_id_type=MESH,
        )

    def start(step, carry):
        copy(step).start()
        return carry

    share = count // parts
    for part in reversed(range(parts)):
        for q, span in enumerate(spans):
            payload = jnp.concatenate(
                [
                    sens[:, span],
                    cell[:, span].astype(F32),
                    weight[:, span],
                    (owner[:, span] * BOX_DEV + slot[:, span]).astype(F32),
                    jnp.zeros((fields - SENT, length), F32),
                ],
                axis=0,
            )
            terms = jnp.concatenate(two_terms(payload), axis=0).astype(BF16)
            to = jnp.broadcast_to(target[:, span] - part * share, terms.shape).astype(jnp.int16)
            for t in range(share):
                spread[t * 2 * fields : (t + 1) * 2 * fields, span] = kept(to == t, terms)
        product = dot_nt(spread[...], place[...])
        for t in range(share):
            at = t * 2 * fields
            send[part * share + t] = product[at : at + fields] + product[at + fields : at + 2 * fields]
        if part == parts - 1:
            pl.semaphore_wait(barrier, count - 1)
        lax.fori_loop(max(1, part * share), (part + 1) * share, start, 0)

    recv[0] = send[0]

    def arrive(step, carry):
        copy(step).wait_recv()
        return carry

    senders = count // groups
    for group in reversed(range(groups)):
        lax.fori_loop(max(1, group * senders), (group + 1) * senders, arrive, 0)
        sort_group(cut, slabs, [recv.at[group * senders + i] for i in range(senders)], tiles, group * per_group, per_group, slab_of, group)

    def sent(step, carry):
        copy(step).wait_send()
        return carry

    lax.fori_loop(1, count, sent, 0)


def sort_group(cut, slabs, arrived, tiles, first, per_group, slab_of, group):
    senders = len(arrived)
    fields, capacity = arrived[0].shape
    width = tiles.shape[2]
    join = max(1, min(senders, 512 // capacity))
    count = senders // join
    real = lax.broadcasted_iota(jnp.int32, (fields, join * capacity), 0) < SENT
    blocks = [
        jnp.where(real, jnp.concatenate([arrived[q * join + i][...] for i in range(join)], axis=1), 0.0)
        for q in range(count)
    ]
    chosen = [matches(slabs, split(block[3:4].astype(jnp.int32), cut)[0]) for block in blocks]
    before, number = ordinals(chosen)
    total = running(number)
    lower = one_hot(
        lax.broadcasted_iota(jnp.int32, (slabs, slabs), 1)
        < lax.broadcasted_iota(jnp.int32, (slabs, slabs), 0)
    )
    tens = jnp.floor(total[-1] * 0.0625)
    start = 16.0 * jnp.dot(lower, tens.astype(BF16), preferred_element_type=F32)
    start = start + jnp.dot(lower, (total[-1] - 16.0 * tens).astype(BF16), preferred_element_type=F32)

    steps = per_group + slabs - 1
    row = lax.broadcasted_iota(jnp.int32, start.shape, 0).astype(F32)
    step = lax.broadcasted_iota(jnp.int32, start.shape, 1).astype(F32)
    entry = row + jnp.minimum(jnp.floor(start * (1.0 / width)), per_group - 1.0)
    slab = jnp.sum(jnp.where((row > 0) & (entry <= step), 1.0, 0.0), axis=0, keepdims=True)
    slab = jnp.where(step[:1] < steps, slab, slabs)
    inside = (row > 0) & (start < (step + 1.0) * width)
    final = step[:1] + jnp.sum(jnp.where(inside, 1.0, 0.0), axis=0, keepdims=True)
    table = jnp.concatenate([slab, final, jnp.zeros((6, 128), F32)], axis=0)
    slab_of[group] = table.astype(jnp.int32)

    sums = jnp.zeros((per_group * 2 * fields, width), F32)
    for q in range(count):
        where = picked(chosen[q], before[q] + (total[q] + start)[:, :1]).astype(jnp.int32)
        tile, lane = split(where, width)
        terms = jnp.concatenate(two_terms(blocks[q]), axis=0).astype(BF16)
        tile = jnp.broadcast_to(tile, terms.shape).astype(jnp.int16)
        spread = jnp.concatenate([kept(tile == t, terms) for t in range(per_group)], axis=0)
        sums = sums + dot_nt(spread, wide_one_hot(width, lane))
    for t in range(per_group):
        at = t * 2 * fields
        tiles[first + t] = sums[at : at + fields] + sums[at + fields : at + 2 * fields]


def relay_rows(devices, capacity, slabs, cut, sens, weight, device, cell, owner, slot):
    rows = devices * capacity
    size = min(4096, rows)
    width = min(256, size)
    groups = rows // size
    parts = 2
    return pl.pallas_call(
        functools.partial(relay_kernel, cut, slabs, parts),
        out_shape=[
            jax.ShapeDtypeStruct((rows // width, 8, width), F32),
            jax.ShapeDtypeStruct((groups, 8, 128), jnp.int32),
        ],
        in_specs=[pl.BlockSpec(memory_space=pltpu.VMEM)] * 6,
        out_specs=[pl.BlockSpec(memory_space=pltpu.VMEM)] * 2,
        scratch_shapes=[
            pltpu.VMEM((devices, 8, capacity), F32),
            pltpu.VMEM((devices, 8, capacity), F32),
            pltpu.VMEM((capacity, sens.shape[1]), BF16),
            pltpu.VMEM((devices // parts * 16, sens.shape[1]), BF16),
        ]
        + [pltpu.SemaphoreType.DMA((devices,))] * 2,
        compiler_params=pltpu.CompilerParams(collective_id=1, has_side_effects=True, vmem_limit_bytes=48 << 20),
        name="relay_rows",
    )(sens, weight, device, cell, owner, slot)


def located(tile, size_z):
    return split(tile[3:4].astype(jnp.int32), size_z)


def scatter_kernel(size_y, slabs_of, tiles, load):
    parts, size_xy, size_z = load.shape
    groups = slabs_of.shape[0]
    per_group = tiles.shape[0] // groups
    slabs = size_xy // size_y
    half = parts * size_y
    load[...] = jnp.zeros_like(load)

    def body(step, carry):
        made = []
        for group in range(groups):
            slab = slabs_of[group, 0, step]
            tile = tiles[group * per_group + jnp.minimum(step - slab, per_group - 1)]
            xy, z = located(tile, size_z)
            at_z = wide_one_hot(size_z, z)
            pairs = [two_terms(tile[k : k + 1]) for k in range(parts)]
            values = [hi for hi, lo in pairs] + [lo for hi, lo in pairs]
            at_y = matches(size_y, xy - slab * size_y)
            terms = jnp.concatenate([scaled(at_y, value) for value in values], axis=0)
            product = dot_nt(terms, at_z)
            made.append((slab, product[:half] + product[half:]))
        for slab, product in made:
            span = pl.ds(pl.multiple_of(jnp.minimum(slab, slabs - 1) * size_y, size_y), size_y)
            for k in range(parts):
                load[k, span] = load[k, span] + product[k * size_y : (k + 1) * size_y]
        return carry

    lax.fori_loop(0, per_group + slabs, body, 0, unroll=4)


def scatter_rows(tiles, ends, size_x, size_y, size_z):
    return pl.pallas_call(
        functools.partial(scatter_kernel, size_y),
        out_shape=jax.ShapeDtypeStruct((3, size_x * size_y, size_z), F32),
        in_specs=[pl.BlockSpec(memory_space=pltpu.SMEM), pl.BlockSpec(memory_space=pltpu.VMEM)],
        out_specs=pl.BlockSpec(memory_space=pltpu.VMEM),
        compiler_params=pltpu.CompilerParams(vmem_limit_bytes=32 << 20),
        name="scatter_rows",
    )(ends, tiles)


def solve_kernel(slab_of, tiles, load, stiff, anchor, coupling, adjoint, box, weighted, inverse, near, edge, halo, terms, found, flat, landed, x_send, x_recv, y_send, y_recv, box_send, box_recv):
    parts, size_x, size_y, size_z = load.shape
    exchanges = weighted.shape[0]
    gx, gy = lax.axis_index("gx"), lax.axis_index("gy")
    count_x, count_y = lax.axis_size("gx"), lax.axis_size("gy")
    devices = count_x * count_y
    me = gx * count_y + gy
    sides = (("gx", gx, -1, gx > 0), ("gx", gx, 1, gx < count_x - 1), ("gy", gy, -1, gy > 0), ("gy", gy, 1, gy < count_y - 1))
    y_at = lax.broadcasted_iota(jnp.int32, (size_y, size_z), 0)
    z_at = lax.broadcasted_iota(jnp.int32, (size_y, size_z), 1)
    barrier = pltpu.get_barrier_semaphore()

    def peer(step):
        there = (me + step) % devices
        return (there // count_y, there % count_y)

    def greet(step, carry):
        pl.semaphore_signal(barrier, inc=1, device_id=peer(step), device_id_type=MESH)
        return carry

    lax.fori_loop(1, devices, greet, 0)

    for side, (axis, place, move, present) in enumerate(sides):

        @pl.when(jnp.logical_not(present))
        def _():
            for index in range(exchanges):
                if axis == "gx":
                    for k in range(parts):
                        weighted[index, k, 0 if move < 0 else size_x + 1] = jnp.zeros((size_y, size_z), F32)
                else:
                    halo[index, side % 2] = jnp.zeros(halo.shape[2:], F32)

    def transfers(index, sending, which=range(4)):
        made = []
        for side in which:
            axis, place, move, present = sides[side]
            there = 1 - side % 2
            landing = there if sending else side % 2
            if axis == "gx":
                into = size_x + 1 if (move < 0) == sending else 0
                pair = (weighted.at[index, :, 1 if move < 0 else size_x], weighted.at[index, :, into])
                sems = (x_send, x_recv)
            else:
                pair = (edge.at[index, side % 2], halo.at[index, landing])
                sems = (y_send, y_recv)
            made.append((present, pltpu.make_async_remote_copy(
                src_ref=pair[0],
                dst_ref=pair[1],
                send_sem=sems[0].at[index, side % 2],
                recv_sem=sems[1].at[index, landing],
                device_id={axis: place + move},
                device_id_type=MESH,
            )))
        return made

    def begin(index):
        for present, copy in transfers(index, True):

            @pl.when(present)
            def _():
                copy.start()

    def arrive(index, which):
        for present, copy in transfers(index, False, which):

            @pl.when(present)
            def _():
                copy.wait_recv()

    rims = (0, size_y - 1)

    def first(x, carry):
        stiffness = stiff[x]
        for side, rim in enumerate(rims):
            near[2, side, 0, pl.ds(x, 1), :] = stiffness[rim : rim + 1]
        for k in range(parts):
            inverted = 1.0 / (6.0 * stiffness + anchor[k, x] + coupling[4 * k, x])
            inverse[k, x] = inverted
            value = load[k, x] * inverted
            adjoint[k, x] = value
            product = stiffness * value
            weighted[0, k, x + 1] = product
            for side, rim in enumerate(rims):
                near[1, side, k, pl.ds(x, 1), :] = inverted[rim : rim + 1]
                edge[0, side, k, pl.ds(x, 1), :] = product[rim : rim + 1]
        return carry

    lax.fori_loop(0, size_x, first, 0)
    pl.semaphore_wait(barrier, devices - 1)
    begin(0)

    for index in range(exchanges):
        last = index + 1 == exchanges

        def update(x, carry):
            fields = [adjoint[k, x] for k in range(parts)]
            for k in range(parts):
                product = weighted[index, k, x + 1]
                value = load[k, x] + weighted[index, k, x] + weighted[index, k, x + 2]
                for j in range(parts):
                    if j != k:
                        value = value - coupling[3 * j + k, x] * fields[j]
                value = value + jnp.where(z_at == 0, 0.0, pltpu.roll(product, 1, 1))
                value = value + jnp.where(z_at == size_z - 1, 0.0, pltpu.roll(product, size_z - 1, 1))
                value = value + jnp.where(y_at == 0, 0.0, pltpu.roll(product, 1, 0))
                value = value + jnp.where(y_at == size_y - 1, 0.0, pltpu.roll(product, size_y - 1, 0))
                value = value * inverse[k, x]
                adjoint[k, x] = value
                for side, rim in enumerate(rims):
                    near[0, side, k, pl.ds(x, 1), :] = value[rim : rim + 1]
                if not last:
                    weighted[index + 1, k, x + 1] = stiff[x] * value
            return carry

        lax.fori_loop(1, size_x - 1, update, 0)
        arrive(index, (0, 1))
        update(0, 0)
        update(size_x - 1, 0)
        arrive(index, (2, 3))
        for side, rim in enumerate(rims):
            for k in range(parts):
                value = near[0, side, k] + halo[index, side, k] * near[1, side, k]
                for x in range(size_x):
                    adjoint[k, x, rim : rim + 1, :] = value[x : x + 1]
                if not last:
                    product = near[2, side, 0] * value
                    edge[index + 1, side, k] = product
                    for x in range(size_x):
                        weighted[index + 1, k, x + 1, rim : rim + 1, :] = product[x : x + 1]
        if not last:
            begin(index + 1)

    count, _, width = tiles.shape
    groups = slab_of.shape[0]
    per_group = count // groups
    steps = per_group + size_x
    half = parts * size_y

    def cut(x, carry):
        for k in range(parts):
            hi, lo = two_terms(adjoint[k, x])
            terms[x, k * size_y : (k + 1) * size_y] = hi.astype(BF16)
            terms[x, half + k * size_y : half + (k + 1) * size_y] = lo.astype(BF16)
        return carry

    lax.fori_loop(0, size_x, cut, 0)

    def look(step, carry):
        made = []
        for group in range(groups):
            held, before = carry[group]
            slab = slab_of[group, 0, step]
            tile = tiles[group * per_group + jnp.minimum(step - slab, per_group - 1)]
            xy, z = located(tile, size_z)
            at_y = matches(size_y, xy - slab * size_y)
            columns = jnp.dot(terms[jnp.minimum(slab, size_x - 1)], wide_one_hot(size_z, z), preferred_element_type=F32)
            columns = columns[:half] + columns[half:]
            value = jnp.concatenate(
                [picked(at_y, columns[k * size_y : (k + 1) * size_y]) for k in range(parts)], axis=0
            )
            held = value + jnp.where(slab == before, 0.0, held)
            found[group * steps + step, :parts] = held
            made.append((held, slab))
        return tuple(made)

    lax.fori_loop(
        0, steps, look, tuple((jnp.zeros((parts, width), F32), jnp.int32(0)) for _ in range(groups)), unroll=4
    )
    total = jnp.zeros((2 * parts * devices, BOX_DEV), F32)
    join = min(8, count)
    for begin_at in range(0, count, join):
        numbers = range(begin_at, begin_at + join)

        def line(field):
            return jnp.concatenate([tiles[t, field : field + 1] for t in numbers], axis=1)

        owner, slot = split(line(5).astype(jnp.int32), BOX_DEV)
        rows = jnp.concatenate(
            [found[t // per_group * steps + slab_of[t // per_group, 1, t % per_group]][:parts] for t in numbers], axis=1
        ) * line(4)
        at_owner = matches(devices, owner)
        pairs = [two_terms(rows[k : k + 1]) for k in range(parts)]
        values = [hi for hi, lo in pairs] + [lo for hi, lo in pairs]
        spread = jnp.concatenate([scaled(at_owner, value) for value in values], axis=0)
        total = total + dot_nt(spread, wide_one_hot(BOX_DEV, slot))
    for k in range(parts):
        part = total[k * devices : (k + 1) * devices] + total[(parts + k) * devices : (parts + k + 1) * devices]
        flat[k] = jnp.concatenate([part, jnp.zeros_like(part)], axis=1)

    def parcel(step):
        return pltpu.make_async_remote_copy(
            src_ref=flat.at[:, pl.ds((me + step) % devices, 1)],
            dst_ref=landed.at[:, pl.ds(step, 1)],
            send_sem=box_send.at[step],
            recv_sem=box_recv.at[step],
            device_id=peer(step),
            device_id_type=MESH,
        )

    def post(step, carry):
        parcel(step).start()
        return carry

    lax.fori_loop(1, devices, post, 0)
    landed[:, 0:1] = flat[:, pl.ds(me, 1)]

    def collect(step, carry):
        parcel(step).wait_recv()
        return carry

    lax.fori_loop(1, devices, collect, 0)
    for k in range(parts):
        box[k : k + 1] = jnp.sum(landed[k], axis=0, keepdims=True)[:, :BOX_DEV]

    def sent(step, carry):
        parcel(step).wait_send()
        return carry

    lax.fori_loop(1, devices, sent, 0)
    for index in range(exchanges):
        for present, copy in transfers(index, True):

            @pl.when(present)
            def _():
                copy.wait_send()


def solve_rows(devices, tiles, slab_of, load, stiffness, anchor, coupling):
    parts, size_x, size_y, size_z = load.shape
    exchanges = SWEEPS - 1
    count, fields, width = tiles.shape
    groups = slab_of.shape[0]
    steps = count // groups + size_x
    return pl.pallas_call(
        solve_kernel,
        out_shape=[jax.ShapeDtypeStruct(load.shape, F32), jax.ShapeDtypeStruct((parts, BOX_DEV), F32)],
        in_specs=[pl.BlockSpec(memory_space=pltpu.SMEM)] + [pl.BlockSpec(memory_space=pltpu.VMEM)] * 5,
        out_specs=[pl.BlockSpec(memory_space=pltpu.VMEM)] * 2,
        scratch_shapes=[
            pltpu.VMEM((exchanges, parts, size_x + 2, size_y, size_z), F32),
            pltpu.VMEM(load.shape, F32),
            pltpu.VMEM((3, 2, parts, size_x, size_z), F32),
            pltpu.VMEM((exchanges, 2, parts, size_x, size_z), F32),
            pltpu.VMEM((exchanges, 2, parts, size_x, size_z), F32),
            pltpu.VMEM((size_x, 2 * parts * size_y, size_z), BF16),
            pltpu.VMEM((groups * steps, fields, width), F32),
            pltpu.VMEM((parts, devices, 2 * BOX_DEV), F32),
            pltpu.VMEM((parts, devices, 2 * BOX_DEV), F32),
        ]
        + [pltpu.SemaphoreType.DMA((exchanges, 2))] * 4
        + [pltpu.SemaphoreType.DMA((devices,))] * 2,
        compiler_params=pltpu.CompilerParams(collective_id=0, has_side_effects=True, vmem_limit_bytes=48 << 20),
        name="solve_rows",
    )(slab_of, tiles, load, stiffness, anchor, coupling)


def body(
    sensitivity,
    node_weight,
    dest_device,
    dest_cell,
    box_owner,
    box_slot,
    stiffness,
    anchor,
    coupling,
):
    devices = lax.axis_size("gx") * lax.axis_size("gy")
    row_count = sensitivity.shape[1]
    capacity = 2 * row_count // devices
    size_x, size_y, size_z = stiffness.shape
    size_xy = size_x * size_y
    assert size_xy * size_z <= 2**17 and devices * BOX_DEV <= 2**17

    def row(values):
        return values.reshape(1, row_count)

    tiles, ends = relay_rows(
        devices,
        capacity,
        size_x,
        size_y * size_z,
        sensitivity,
        row(node_weight),
        row(dest_device),
        row(dest_cell),
        row(box_owner),
        row(box_slot),
    )
    load = scatter_rows(tiles, ends, size_x, size_y, size_z)
    load = load.reshape(3, size_x, size_y, size_z)
    adjoint, box_gradient = solve_rows(devices, tiles, ends, load, stiffness, anchor, coupling)
    return (adjoint, box_gradient)


def solution(mesh):
    placed = (
        P(None, ("gx", "gy")),
        P(("gx", "gy")),
        P(("gx", "gy"), None),
        P(("gx", "gy")),
        P(("gx", "gy"), None),
        P(("gx", "gy")),
        P("gx", "gy", None),
        P(None, "gx", "gy", None),
        P(None, "gx", "gy", None),
    )
    return jax.shard_map(
        body,
        mesh=mesh,
        in_specs=placed,
        out_specs=(P(None, "gx", "gy", None), P(None, ("gx", "gy"))),
        check_vma=False,
    )
```

```python
import functools

import jax
import jax.numpy as jnp
from jax import lax
from jax.experimental import pallas as pl
from jax.experimental.pallas import tpu as pltpu
from jax.sharding import PartitionSpec as P

BOX_DEV = 64
SWEEPS = 4
SENT = 4
FIELDS = 6
NT = (((1,), (1,)), ((), ()))
F32 = jnp.float32
BF16 = jnp.bfloat16
MESH = pl.DeviceIdType.MESH


def two_terms(x):
    hi = x.astype(BF16).astype(F32)
    return hi, x - hi


def matches(count, row):
    return lax.broadcasted_iota(jnp.int32, (count, row.shape[1]), 0) == row


def one_hot(mask):
    return jnp.where(mask, 1.0, 0.0).astype(BF16)


def scaled(mask, row):
    return jnp.where(mask, row, 0.0).astype(BF16)


def dot_nt(a, b):
    return lax.dot_general(a, b, NT, preferred_element_type=F32)


def split(value, size):
    if size & (size - 1) == 0:
        return value >> (size.bit_length() - 1), value & (size - 1)
    return value // size, value % size


def wide_matches(count, row):
    return lax.broadcasted_iota(jnp.int16, (count, row.shape[1]), 0) == row.astype(jnp.int16)


def wide_one_hot(count, row):
    return jnp.where(wide_matches(count, row), jnp.array(1, BF16), jnp.array(0, BF16))


def kept(mask, values):
    return jnp.where(mask, values, jnp.array(0, BF16))


def running(numbers):
    totals = [jnp.zeros_like(numbers[0])]
    for number in numbers:
        totals.append(totals[-1] + number)
    return totals


def ordinals(chosen):
    length = chosen[0].shape[1]
    stacked = one_hot(jnp.concatenate(chosen, axis=0))
    earlier = one_hot(
        lax.broadcasted_iota(jnp.int32, (length, length), 0)
        < lax.broadcasted_iota(jnp.int32, (length, length), 1)
    )
    before = jnp.dot(stacked, earlier, preferred_element_type=F32)
    number = jnp.dot(stacked, jnp.ones((length, 128), BF16), preferred_element_type=F32)
    size = chosen[0].shape[0]

    def cut(values):
        return [values[q * size : (q + 1) * size] for q in range(len(chosen))]

    return cut(before), cut(number)


def picked(mask, value):
    return jnp.sum(jnp.where(mask, value, 0.0), axis=0, keepdims=True)


def relay_kernel(cut, slabs, parts, sens, weight, device, cell, owner, slot, tiles, slab_of, spots, send, recv, place, spread, send_sem, recv_sem):
    count, fields, capacity = send.shape
    rows = sens.shape[1]
    _, _, width = tiles.shape
    groups = slab_of.shape[0]
    per_group = tiles.shape[0] // groups
    gx, gy = lax.axis_index("gx"), lax.axis_index("gy")
    size_x, size_y = lax.axis_size("gx"), lax.axis_size("gy")
    me = gx * size_y + gy
    barrier = pltpu.get_barrier_semaphore()

    def peer(step):
        there = (me + step) % count
        return (there // size_y, there % size_y)

    def greet(step, carry):
        pl.semaphore_signal(barrier, inc=1, device_id=peer(step), device_id_type=MESH)
        return carry

    lax.fori_loop(1, count, greet, 0)

    length = min(512, rows)
    chunks = rows // length
    spans = [slice(q * length, (q + 1) * length) for q in range(chunks)]
    target = device[...] - me
    target = jnp.where(target < 0, target + count, target)
    chosen = [matches(count, target[:, span]) for span in spans]
    before, number = ordinals(chosen)
    total = running(number)
    for q, span in enumerate(spans):
        rank = picked(chosen[q], before[q] + total[q][:, :1]).astype(jnp.int32)
        place[:, span] = wide_one_hot(capacity, rank)

    def copy(step):
        return pltpu.make_async_remote_copy(
            src_ref=send.at[step, pl.ds(0, SENT)],
            dst_ref=recv.at[step, pl.ds(0, SENT)],
            send_sem=send_sem.at[step],
            recv_sem=recv_sem.at[step],
            device_id=peer(step),
            device_id_type=MESH,
        )

    def start(step, carry):
        copy(step).start()
        return carry

    share = count // parts
    for part in reversed(range(parts)):
        for q, span in enumerate(spans):
            payload = jnp.concatenate(
                [
                    sens[:, span],
                    cell[:, span].astype(F32),
                    weight[:, span],
                    (owner[:, span] * BOX_DEV + slot[:, span]).astype(F32),
                    jnp.zeros((fields - FIELDS, length), F32),
                ],
                axis=0,
            )
            terms = jnp.concatenate(two_terms(payload), axis=0).astype(BF16)
            to = jnp.broadcast_to(target[:, span] - part * share, terms.shape).astype(jnp.int16)
            for t in range(share):
                spread[t * 2 * fields : (t + 1) * 2 * fields, span] = kept(to == t, terms)
        product = dot_nt(spread[...], place[...])
        for t in range(share):
            at = t * 2 * fields
            send[part * share + t] = product[at : at + fields] + product[at + fields : at + 2 * fields]
        if part == parts - 1:
            pl.semaphore_wait(barrier, count - 1)
        lax.fori_loop(max(1, part * share), (part + 1) * share, start, 0)

    recv[0] = send[0]

    def arrive(step, carry):
        copy(step).wait_recv()
        return carry

    senders = count // groups
    for group in reversed(range(groups)):
        lax.fori_loop(max(1, group * senders), (group + 1) * senders, arrive, 0)
        sort_group(cut, slabs, [recv.at[group * senders + i] for i in range(senders)], tiles, group * per_group, per_group, slab_of, spots, group)

    def sent(step, carry):
        copy(step).wait_send()
        return carry

    lax.fori_loop(1, count, sent, 0)


def joined(arrived, low, high):
    fields, capacity = arrived[0].shape
    join = max(1, min(len(arrived), 512 // capacity))
    row = lax.broadcasted_iota(jnp.int32, (fields, join * capacity), 0)
    return [
        jnp.where(
            (row >= low) & (row < high),
            jnp.concatenate([arrived[q + i][...] for i in range(join)], axis=1),
            0.0,
        )
        for q in range(0, len(arrived), join)
    ]


def ordered(blocks, spots, per_group, width):
    fields = blocks[0].shape[0]
    sums = jnp.zeros((per_group * 2 * fields, width), F32)
    for block, spot in zip(blocks, spots):
        tile, lane = split(spot, width)
        terms = jnp.concatenate(two_terms(block), axis=0).astype(BF16)
        tile = jnp.broadcast_to(tile, terms.shape).astype(jnp.int16)
        spread = jnp.concatenate([kept(tile == t, terms) for t in range(per_group)], axis=0)
        sums = sums + dot_nt(spread, wide_one_hot(width, lane))
    made = []
    for t in range(per_group):
        at = t * 2 * fields
        made.append(sums[at : at + fields] + sums[at + fields : at + 2 * fields])
    return made


def sort_group(cut, slabs, arrived, tiles, first, per_group, slab_of, spots, group):
    width = tiles.shape[2]
    blocks = joined(arrived, 0, SENT)
    count = len(blocks)
    chosen = [matches(slabs, split(block[3:4].astype(jnp.int32), cut)[0]) for block in blocks]
    before, number = ordinals(chosen)
    total = running(number)
    lower = one_hot(
        lax.broadcasted_iota(jnp.int32, (slabs, slabs), 1)
        < lax.broadcasted_iota(jnp.int32, (slabs, slabs), 0)
    )
    tens = jnp.floor(total[-1] * 0.0625)
    start = 16.0 * jnp.dot(lower, tens.astype(BF16), preferred_element_type=F32)
    start = start + jnp.dot(lower, (total[-1] - 16.0 * tens).astype(BF16), preferred_element_type=F32)

    steps = per_group + slabs - 1
    row = lax.broadcasted_iota(jnp.int32, start.shape, 0).astype(F32)
    step = lax.broadcasted_iota(jnp.int32, start.shape, 1).astype(F32)
    entry = row + jnp.minimum(jnp.floor(start * (1.0 / width)), per_group - 1.0)
    slab = jnp.sum(jnp.where((row > 0) & (entry <= step), 1.0, 0.0), axis=0, keepdims=True)
    slab = jnp.where(step[:1] < steps, slab, slabs)
    inside = (row > 0) & (start < (step + 1.0) * width)
    final = step[:1] + jnp.sum(jnp.where(inside, 1.0, 0.0), axis=0, keepdims=True)
    leave = jnp.sum(jnp.where(row == step + 1.0, entry, 0.0), axis=0, keepdims=True)
    leave = jnp.where(step[:1] == slabs - 1, steps, leave) - 1.0
    table = jnp.concatenate([slab, final, leave, jnp.zeros((5, 128), F32)], axis=0)
    slab_of[group] = table.astype(jnp.int32)

    found = [
        picked(chosen[q], before[q] + (total[q] + start)[:, :1]).astype(jnp.int32) for q in range(count)
    ]
    for q in range(count):
        spots[group * count + q : group * count + q + 1] = found[q]
    for t, tile in enumerate(ordered(blocks, found, per_group, width)):
        tiles[first + t] = tile


def relay_rows(devices, capacity, slabs, cut, sens, weight, device, cell, owner, slot):
    rows = devices * capacity
    size = min(4096, rows)
    width = min(256, size)
    groups = rows // size
    parts = 2
    length = max(1, min(size // capacity, 512 // capacity)) * capacity
    return pl.pallas_call(
        functools.partial(relay_kernel, cut, slabs, parts),
        out_shape=[
            jax.ShapeDtypeStruct((rows // width, 8, width), F32),
            jax.ShapeDtypeStruct((groups, 8, 128), jnp.int32),
            jax.ShapeDtypeStruct((rows // length, length), jnp.int32),
            jax.ShapeDtypeStruct((devices, 8, capacity), F32),
        ],
        in_specs=[pl.BlockSpec(memory_space=pltpu.VMEM)] * 6,
        out_specs=[pl.BlockSpec(memory_space=pltpu.VMEM)] * 4,
        scratch_shapes=[
            pltpu.VMEM((devices, 8, capacity), F32),
            pltpu.VMEM((capacity, sens.shape[1]), BF16),
            pltpu.VMEM((devices // parts * 16, sens.shape[1]), BF16),
        ]
        + [pltpu.SemaphoreType.DMA((devices,))] * 2,
        compiler_params=pltpu.CompilerParams(collective_id=1, has_side_effects=True, vmem_limit_bytes=60 << 20),
        name="relay_rows",
    )(sens, weight, device, cell, owner, slot)


def located(tile, size_z):
    return split(tile[3:4].astype(jnp.int32), size_z)


def solve_kernel(slab_of, tiles, spots, parcels, stiff_in, anchor_in, coupling_in, adjoint, box, stiff, anchor, coupling, load, stage, late, marks, weighted, inverse, near, edge, halo, terms, found, flat, landed, fetch, late_send, late_recv, x_send, x_recv, y_send, y_recv, box_send, box_recv):
    parts, size_x, size_y, size_z = load.shape
    count, _, width = tiles.shape
    groups = slab_of.shape[0]
    per_group = count // groups
    steps = per_group + size_x
    half = parts * size_y
    exchanges = weighted.shape[0]
    gx, gy = lax.axis_index("gx"), lax.axis_index("gy")
    count_x, count_y = lax.axis_size("gx"), lax.axis_size("gy")
    devices = count_x * count_y
    me = gx * count_y + gy
    sides = (("gx", gx, -1, gx > 0), ("gx", gx, 1, gx < count_x - 1), ("gy", gy, -1, gy > 0), ("gy", gy, 1, gy < count_y - 1))
    y_at = lax.broadcasted_iota(jnp.int32, (size_y, size_z), 0)
    z_at = lax.broadcasted_iota(jnp.int32, (size_y, size_z), 1)
    barrier = pltpu.get_barrier_semaphore()

    def peer(step):
        there = (me + step) % devices
        return (there // count_y, there % count_y)

    def greet(step, carry):
        pl.semaphore_signal(barrier, inc=1, device_id=peer(step), device_id_type=MESH)
        return carry

    lax.fori_loop(1, devices, greet, 0)
    fetches = [
        pltpu.make_async_copy(source, target, fetch.at[i])
        for i, (source, target) in enumerate(((stiff_in, stiff), (anchor_in, anchor), (coupling_in, coupling)))
    ]
    for copy in fetches:
        copy.start()

    for side, (axis, place, move, present) in enumerate(sides):

        @pl.when(jnp.logical_not(present))
        def _():
            for index in range(exchanges):
                if axis == "gx":
                    for k in range(parts):
                        weighted[index, k, 0 if move < 0 else size_x + 1] = jnp.zeros((size_y, size_z), F32)
                else:
                    halo[index, side % 2] = jnp.zeros(halo.shape[2:], F32)

    def transfers(index, sending, which=range(4)):
        made = []
        for side in which:
            axis, place, move, present = sides[side]
            there = 1 - side % 2
            landing = there if sending else side % 2
            if axis == "gx":
                into = size_x + 1 if (move < 0) == sending else 0
                pair = (weighted.at[index, :, 1 if move < 0 else size_x], weighted.at[index, :, into])
                sems = (x_send, x_recv)
            else:
                pair = (edge.at[index, side % 2], halo.at[index, landing])
                sems = (y_send, y_recv)
            made.append((present, pltpu.make_async_remote_copy(
                src_ref=pair[0],
                dst_ref=pair[1],
                send_sem=sems[0].at[index, side % 2],
                recv_sem=sems[1].at[index, landing],
                device_id={axis: place + move},
                device_id_type=MESH,
            )))
        return made

    def begin(index):
        for present, copy in transfers(index, True):

            @pl.when(present)
            def _():
                copy.start()

    def arrive(index, which):
        for present, copy in transfers(index, False, which):

            @pl.when(present)
            def _():
                copy.wait_recv()

    rims = (0, size_y - 1)

    def deposit(step, carry):
        made = []
        for group in range(groups):
            slab = slab_of[group, 0, step]
            tile = tiles[group * per_group + jnp.minimum(step - slab, per_group - 1)]
            xy, z = located(tile, size_z)
            pairs = [two_terms(tile[k : k + 1]) for k in range(parts)]
            values = [hi for hi, lo in pairs] + [lo for hi, lo in pairs]
            at_y = matches(size_y, xy - slab * size_y)
            spread = jnp.concatenate([scaled(at_y, value) for value in values], axis=0)
            product = dot_nt(spread, wide_one_hot(size_z, z))
            at = group * steps + step
            earlier = stage[jnp.maximum(at - 1, 0)]
            stage[at] = product[:half] + product[half:] + jnp.where(slab == carry[group], earlier, 0.0)
            made.append(slab)
        return tuple(made)

    late_rows = pl.ds(SENT, FIELDS - SENT)

    def follow(step):
        return pltpu.make_async_remote_copy(
            src_ref=parcels.at[step, late_rows],
            dst_ref=late.at[step, late_rows],
            send_sem=late_send.at[step],
            recv_sem=late_recv.at[step],
            device_id=peer(step),
            device_id_type=MESH,
        )

    def send_late(step, carry):
        follow(step).start()
        return carry

    def take_late(step, carry):
        follow(step).wait_recv()
        return carry

    def sort_late(group):
        senders = devices // groups
        blocks = joined([late.at[group * senders + i] for i in range(senders)], SENT, FIELDS)
        lines = [spots[q : q + 1] for q in range(group * len(blocks), (group + 1) * len(blocks))]
        for t, tile in enumerate(ordered(blocks, lines, per_group, width)):
            marks[group * per_group + t] = tile

    stage[0] = jnp.zeros(stage.shape[1:], F32)
    slabs = lax.fori_loop(0, steps // 2, deposit, tuple(jnp.int32(-1) for _ in range(groups)), unroll=4)
    pl.semaphore_wait(barrier, devices - 1)
    lax.fori_loop(1, devices, send_late, 0)
    late[0] = parcels[0]
    lax.fori_loop(steps // 2, steps, deposit, slabs, unroll=4)
    for copy in fetches:
        copy.wait()

    def first(x, carry):
        stiffness = stiff[x]
        sums = stage[slab_of[0, 2, x]]
        for group in range(1, groups):
            sums = sums + stage[group * steps + slab_of[group, 2, x]]
        for side, rim in enumerate(rims):
            near[2, side, 0, pl.ds(x, 1), :] = stiffness[rim : rim + 1]
        for k in range(parts):
            inverted = 1.0 / (6.0 * stiffness + anchor[k, x] + coupling[4 * k, x])
            inverse[k, x] = inverted
            there = sums[k * size_y : (k + 1) * size_y]
            load[k, x] = there
            value = there * inverted
            adjoint[k, x] = value
            product = stiffness * value
            weighted[0, k, x + 1] = product
            for side, rim in enumerate(rims):
                near[1, side, k, pl.ds(x, 1), :] = inverted[rim : rim + 1]
                edge[0, side, k, pl.ds(x, 1), :] = product[rim : rim + 1]
        return carry

    lax.fori_loop(0, size_x, first, 0)
    begin(0)
    lax.fori_loop(1, devices, take_late, 0)

    for index in range(exchanges):
        last = index + 1 == exchanges
        for group in range(groups * index // exchanges, groups * (index + 1) // exchanges):
            sort_late(group)

        def update(x, carry):
            fields = [adjoint[k, x] for k in range(parts)]
            for k in range(parts):
                product = weighted[index, k, x + 1]
                value = load[k, x] + weighted[index, k, x] + weighted[index, k, x + 2]
                for j in range(parts):
                    if j != k:
                        value = value - coupling[3 * j + k, x] * fields[j]
                value = value + jnp.where(z_at == 0, 0.0, pltpu.roll(product, 1, 1))
                value = value + jnp.where(z_at == size_z - 1, 0.0, pltpu.roll(product, size_z - 1, 1))
                value = value + jnp.where(y_at == 0, 0.0, pltpu.roll(product, 1, 0))
                value = value + jnp.where(y_at == size_y - 1, 0.0, pltpu.roll(product, size_y - 1, 0))
                value = value * inverse[k, x]
                adjoint[k, x] = value
                for side, rim in enumerate(rims):
                    near[0, side, k, pl.ds(x, 1), :] = value[rim : rim + 1]
                if not last:
                    weighted[index + 1, k, x + 1] = stiff[x] * value
            return carry

        lax.fori_loop(1, size_x - 1, update, 0)
        arrive(index, (0, 1))
        update(0, 0)
        update(size_x - 1, 0)
        arrive(index, (2, 3))
        for side, rim in enumerate(rims):
            for k in range(parts):
                value = near[0, side, k] + halo[index, side, k] * near[1, side, k]
                for x in range(size_x):
                    adjoint[k, x, rim : rim + 1, :] = value[x : x + 1]
                if not last:
                    product = near[2, side, 0] * value
                    edge[index + 1, side, k] = product
                    for x in range(size_x):
                        weighted[index + 1, k, x + 1, rim : rim + 1, :] = product[x : x + 1]
        if not last:
            begin(index + 1)

    def cut(x, carry):
        for k in range(parts):
            hi, lo = two_terms(adjoint[k, x])
            terms[x, k * size_y : (k + 1) * size_y] = hi.astype(BF16)
            terms[x, half + k * size_y : half + (k + 1) * size_y] = lo.astype(BF16)
        return carry

    lax.fori_loop(0, size_x, cut, 0)

    def look(step, carry):
        made = []
        for group in range(groups):
            held, before = carry[group]
            slab = slab_of[group, 0, step]
            tile = tiles[group * per_group + jnp.minimum(step - slab, per_group - 1)]
            xy, z = located(tile, size_z)
            at_y = matches(size_y, xy - slab * size_y)
            columns = jnp.dot(terms[jnp.minimum(slab, size_x - 1)], wide_one_hot(size_z, z), preferred_element_type=F32)
            columns = columns[:half] + columns[half:]
            value = jnp.concatenate(
                [picked(at_y, columns[k * size_y : (k + 1) * size_y]) for k in range(parts)], axis=0
            )
            held = value + jnp.where(slab == before, 0.0, held)
            found[group * steps + step, :parts] = held
            made.append((held, slab))
        return tuple(made)

    lax.fori_loop(
        0, steps, look, tuple((jnp.zeros((parts, width), F32), jnp.int32(0)) for _ in range(groups)), unroll=4
    )
    total = jnp.zeros((2 * parts * devices, BOX_DEV), F32)
    join = min(8, count)
    for begin_at in range(0, count, join):
        numbers = range(begin_at, begin_at + join)

        def line(field):
            return jnp.concatenate([marks[t, field : field + 1] for t in numbers], axis=1)

        owner, slot = split(line(5).astype(jnp.int32), BOX_DEV)
        rows = jnp.concatenate(
            [found[t // per_group * steps + slab_of[t // per_group, 1, t % per_group]][:parts] for t in numbers], axis=1
        ) * line(4)
        at_owner = matches(devices, owner)
        pairs = [two_terms(rows[k : k + 1]) for k in range(parts)]
        values = [hi for hi, lo in pairs] + [lo for hi, lo in pairs]
        spread = jnp.concatenate([scaled(at_owner, value) for value in values], axis=0)
        total = total + dot_nt(spread, wide_one_hot(BOX_DEV, slot))
    for k in range(parts):
        part = total[k * devices : (k + 1) * devices] + total[(parts + k) * devices : (parts + k + 1) * devices]
        flat[k] = jnp.concatenate([part, jnp.zeros_like(part)], axis=1)

    def parcel(step):
        return pltpu.make_async_remote_copy(
            src_ref=flat.at[:, pl.ds((me + step) % devices, 1)],
            dst_ref=landed.at[:, pl.ds(step, 1)],
            send_sem=box_send.at[step],
            recv_sem=box_recv.at[step],
            device_id=peer(step),
            device_id_type=MESH,
        )

    def post(step, carry):
        parcel(step).start()
        return carry

    lax.fori_loop(1, devices, post, 0)
    landed[:, 0:1] = flat[:, pl.ds(me, 1)]

    def collect(step, carry):
        parcel(step).wait_recv()
        return carry

    lax.fori_loop(1, devices, collect, 0)
    for k in range(parts):
        box[k : k + 1] = jnp.sum(landed[k], axis=0, keepdims=True)[:, :BOX_DEV]

    def sent(step, carry):
        parcel(step).wait_send()
        return carry

    lax.fori_loop(1, devices, sent, 0)

    def left(step, carry):
        follow(step).wait_send()
        return carry

    lax.fori_loop(1, devices, left, 0)
    for index in range(exchanges):
        for present, copy in transfers(index, True):

            @pl.when(present)
            def _():
                copy.wait_send()


def solve_rows(devices, tiles, slab_of, spots, parcels, stiffness, anchor, coupling):
    size_x, size_y, size_z = stiffness.shape
    parts = anchor.shape[0]
    exchanges = SWEEPS - 1
    count, fields, width = tiles.shape
    groups = slab_of.shape[0]
    steps = count // groups + size_x
    return pl.pallas_call(
        solve_kernel,
        out_shape=[jax.ShapeDtypeStruct(anchor.shape, F32), jax.ShapeDtypeStruct((parts, BOX_DEV), F32)],
        in_specs=[pl.BlockSpec(memory_space=pltpu.SMEM)]
        + [pl.BlockSpec(memory_space=pltpu.VMEM)] * 3
        + [pl.BlockSpec(memory_space=pl.ANY)] * 3,
        out_specs=[pl.BlockSpec(memory_space=pltpu.VMEM)] * 2,
        scratch_shapes=[
            pltpu.VMEM(stiffness.shape, F32),
            pltpu.VMEM(anchor.shape, F32),
            pltpu.VMEM(coupling.shape, F32),
            pltpu.VMEM(anchor.shape, F32),
            pltpu.VMEM((groups * steps, parts * size_y, size_z), F32),
            pltpu.VMEM(parcels.shape, F32),
            pltpu.VMEM(tiles.shape, F32),
            pltpu.VMEM((exchanges, parts, size_x + 2, size_y, size_z), F32),
            pltpu.VMEM(anchor.shape, F32),
            pltpu.VMEM((3, 2, parts, size_x, size_z), F32),
            pltpu.VMEM((exchanges, 2, parts, size_x, size_z), F32),
            pltpu.VMEM((exchanges, 2, parts, size_x, size_z), F32),
            pltpu.VMEM((size_x, 2 * parts * size_y, size_z), BF16),
            pltpu.VMEM((groups * steps, fields, width), F32),
            pltpu.VMEM((parts, devices, 2 * BOX_DEV), F32),
            pltpu.VMEM((parts, devices, 2 * BOX_DEV), F32),
            pltpu.SemaphoreType.DMA((3,)),
        ]
        + [pltpu.SemaphoreType.DMA((devices,))] * 2
        + [pltpu.SemaphoreType.DMA((exchanges, 2))] * 4
        + [pltpu.SemaphoreType.DMA((devices,))] * 2,
        compiler_params=pltpu.CompilerParams(collective_id=0, has_side_effects=True, vmem_limit_bytes=60 << 20),
        name="solve_rows",
    )(slab_of, tiles, spots, parcels, stiffness, anchor, coupling)


def body(
    sensitivity,
    node_weight,
    dest_device,
    dest_cell,
    box_owner,
    box_slot,
    stiffness,
    anchor,
    coupling,
):
    devices = lax.axis_size("gx") * lax.axis_size("gy")
    row_count = sensitivity.shape[1]
    capacity = 2 * row_count // devices
    size_x, size_y, size_z = stiffness.shape
    size_xy = size_x * size_y
    assert size_xy * size_z <= 2**17 and devices * BOX_DEV <= 2**17

    def row(values):
        return values.reshape(1, row_count)

    tiles, slab_of, spots, parcels = relay_rows(
        devices,
        capacity,
        size_x,
        size_y * size_z,
        sensitivity,
        row(node_weight),
        row(dest_device),
        row(dest_cell),
        row(box_owner),
        row(box_slot),
    )
    adjoint, box_gradient = solve_rows(devices, tiles, slab_of, spots, parcels, stiffness, anchor, coupling)
    return (adjoint, box_gradient)


def solution(mesh):
    placed = (
        P(None, ("gx", "gy")),
        P(("gx", "gy")),
        P(("gx", "gy"), None),
        P(("gx", "gy")),
        P(("gx", "gy"), None),
        P(("gx", "gy")),
        P("gx", "gy", None),
        P(None, "gx", "gy", None),
        P(None, "gx", "gy", None),
    )
    return jax.shard_map(
        body,
        mesh=mesh,
        in_specs=placed,
        out_specs=(P(None, "gx", "gy", None), P(None, ("gx", "gy"))),
        check_vma=False,
    )
```

```python
import functools

import jax
import jax.numpy as jnp
from jax import lax
from jax.experimental import pallas as pl
from jax.experimental.pallas import tpu as pltpu
from jax.sharding import PartitionSpec as P

BOX_DEV = 64
SWEEPS = 4
SENT = 4
FIELDS = 6
NT = (((1,), (1,)), ((), ()))
F32 = jnp.float32
BF16 = jnp.bfloat16
MESH = pl.DeviceIdType.MESH


def two_terms(x):
    hi = x.astype(BF16).astype(F32)
    return hi, x - hi


def matches(count, row):
    return lax.broadcasted_iota(jnp.int32, (count, row.shape[1]), 0) == row


def one_hot(mask):
    return jnp.where(mask, 1.0, 0.0).astype(BF16)


def scaled(mask, row):
    return jnp.where(mask, row, 0.0).astype(BF16)


def dot_nt(a, b):
    return lax.dot_general(a, b, NT, preferred_element_type=F32)


def split(value, size):
    if size & (size - 1) == 0:
        return value >> (size.bit_length() - 1), value & (size - 1)
    return value // size, value % size


def wide_matches(count, row):
    return lax.broadcasted_iota(jnp.int16, (count, row.shape[1]), 0) == row.astype(jnp.int16)


def wide_one_hot(count, row):
    return jnp.where(wide_matches(count, row), jnp.array(1, BF16), jnp.array(0, BF16))


def kept(mask, values):
    return jnp.where(mask, values, jnp.array(0, BF16))


def folded(a, b, size):
    if size & (size - 1):
        return (a + b) % size
    total, bit = 0, 1
    while bit < size:
        total = total + bit * ((a // bit + b // bit) % 2)
        bit = 2 * bit
    return total


def peer_of(gx, gy, size_x, size_y):
    return lambda step: (folded(gx, step // size_y, size_x), (gy + step % size_y) % size_y)


def running(numbers):
    totals = [jnp.zeros_like(numbers[0])]
    for number in numbers:
        totals.append(totals[-1] + number)
    return totals


def ordinals(chosen):
    length = chosen[0].shape[1]
    stacked = one_hot(jnp.concatenate(chosen, axis=0))
    earlier = one_hot(
        lax.broadcasted_iota(jnp.int32, (length, length), 0)
        < lax.broadcasted_iota(jnp.int32, (length, length), 1)
    )
    before = jnp.dot(stacked, earlier, preferred_element_type=F32)
    number = jnp.dot(stacked, jnp.ones((length, 128), BF16), preferred_element_type=F32)
    size = chosen[0].shape[0]

    def cut(values):
        return [values[q * size : (q + 1) * size] for q in range(len(chosen))]

    return cut(before), cut(number)


def picked(mask, value):
    return jnp.sum(jnp.where(mask, value, 0.0), axis=0, keepdims=True)


def relay_kernel(cut, slabs, parts, *refs):
    given, refs = refs[:6], refs[6:]
    tiles, slab_of, spots, send, sens, weight, device, cell, owner, slot, recv, place, spread, fetch, send_sem, recv_sem = refs
    count, fields, capacity = send.shape
    rows = sens.shape[1]
    _, _, width = tiles.shape
    groups = slab_of.shape[0]
    per_group = tiles.shape[0] // groups
    gx, gy = lax.axis_index("gx"), lax.axis_index("gy")
    size_x, size_y = lax.axis_size("gx"), lax.axis_size("gy")
    peer = peer_of(gx, gy, size_x, size_y)
    barrier = pltpu.get_barrier_semaphore()
    fetches = [
        pltpu.make_async_copy(source, target, fetch.at[i])
        for i, (source, target) in enumerate(zip(given, (sens, weight, device, cell, owner, slot)))
    ]
    for copy in fetches:
        copy.start()

    def greet(step, carry):
        pl.semaphore_signal(barrier, inc=1, device_id=peer(step), device_id_type=MESH)
        return carry

    lax.fori_loop(1, count, greet, 0)

    length = min(512, rows)
    chunks = rows // length
    spans = [slice(q * length, (q + 1) * length) for q in range(chunks)]
    for copy in fetches:
        copy.wait()
    to_x, to_y = split(device[...], size_y)
    to_y = to_y - gy
    to_y = jnp.where(to_y < 0, to_y + size_y, to_y)
    if size_x & (size_x - 1):
        to_x = to_x - gx
        to_x = jnp.where(to_x < 0, to_x + size_x, to_x)
    else:
        to_x = to_x ^ gx
    target = to_x * size_y + to_y
    chosen = [matches(count, target[:, span]) for span in spans]
    before, number = ordinals(chosen)
    total = running(number)
    for q, span in enumerate(spans):
        rank = picked(chosen[q], before[q] + total[q][:, :1]).astype(jnp.int32)
        place[:, span] = wide_one_hot(capacity, rank)

    def copy(step):
        return pltpu.make_async_remote_copy(
            src_ref=send.at[step, pl.ds(0, SENT)],
            dst_ref=recv.at[step, pl.ds(0, SENT)],
            send_sem=send_sem.at[step],
            recv_sem=recv_sem.at[step],
            device_id=peer(step),
            device_id_type=MESH,
        )

    def start(step, carry):
        copy(step).start()
        return carry

    share = count // parts
    for part in reversed(range(parts)):
        for q, span in enumerate(spans):
            payload = jnp.concatenate(
                [
                    sens[:, span],
                    cell[:, span].astype(F32),
                    weight[:, span],
                    (owner[:, span] * BOX_DEV + slot[:, span]).astype(F32),
                    jnp.zeros((fields - FIELDS, length), F32),
                ],
                axis=0,
            )
            terms = jnp.concatenate(two_terms(payload), axis=0).astype(BF16)
            to = jnp.broadcast_to(target[:, span] - part * share, terms.shape).astype(jnp.int16)
            for t in range(share):
                spread[t * 2 * fields : (t + 1) * 2 * fields, span] = kept(to == t, terms)
        product = dot_nt(spread[...], place[...])
        for t in range(share):
            at = t * 2 * fields
            send[part * share + t] = product[at : at + fields] + product[at + fields : at + 2 * fields]
        if part == parts - 1:
            pl.semaphore_wait(barrier, count - 1)
        lax.fori_loop(max(1, part * share), (part + 1) * share, start, 0)

    recv[0] = send[0]

    def arrive(step, carry):
        copy(step).wait_recv()
        return carry

    senders = count // groups
    for group in range(groups):
        lax.fori_loop(max(1, group * senders), (group + 1) * senders, arrive, 0)
        sort_group(cut, slabs, [recv.at[group * senders + i] for i in range(senders)], tiles, group * per_group, per_group, slab_of, spots, group)

    def sent(step, carry):
        copy(step).wait_send()
        return carry

    lax.fori_loop(1, count, sent, 0)


def joined(arrived, low, high):
    fields, capacity = arrived[0].shape
    join = max(1, min(len(arrived), 512 // capacity))
    row = lax.broadcasted_iota(jnp.int32, (fields, join * capacity), 0)
    return [
        jnp.where(
            (row >= low) & (row < high),
            jnp.concatenate([arrived[q + i][...] for i in range(join)], axis=1),
            0.0,
        )
        for q in range(0, len(arrived), join)
    ]


def ordered(blocks, spots, per_group, width):
    fields = blocks[0].shape[0]
    sums = jnp.zeros((per_group * 2 * fields, width), F32)
    for block, spot in zip(blocks, spots):
        tile, lane = split(spot, width)
        terms = jnp.concatenate(two_terms(block), axis=0).astype(BF16)
        tile = jnp.broadcast_to(tile, terms.shape).astype(jnp.int16)
        spread = jnp.concatenate([kept(tile == t, terms) for t in range(per_group)], axis=0)
        sums = sums + dot_nt(spread, wide_one_hot(width, lane))
    made = []
    for t in range(per_group):
        at = t * 2 * fields
        made.append(sums[at : at + fields] + sums[at + fields : at + 2 * fields])
    return made


def sort_group(cut, slabs, arrived, tiles, first, per_group, slab_of, spots, group):
    width = tiles.shape[2]
    blocks = joined(arrived, 0, SENT)
    count = len(blocks)
    chosen = [matches(slabs, split(block[3:4].astype(jnp.int32), cut)[0]) for block in blocks]
    before, number = ordinals(chosen)
    total = running(number)
    lower = one_hot(
        lax.broadcasted_iota(jnp.int32, (slabs, slabs), 1)
        < lax.broadcasted_iota(jnp.int32, (slabs, slabs), 0)
    )
    tens = jnp.floor(total[-1] * 0.0625)
    start = 16.0 * jnp.dot(lower, tens.astype(BF16), preferred_element_type=F32)
    start = start + jnp.dot(lower, (total[-1] - 16.0 * tens).astype(BF16), preferred_element_type=F32)

    steps = per_group + slabs - 1
    row = lax.broadcasted_iota(jnp.int32, start.shape, 0).astype(F32)
    step = lax.broadcasted_iota(jnp.int32, start.shape, 1).astype(F32)
    entry = row + jnp.minimum(jnp.floor(start * (1.0 / width)), per_group - 1.0)
    slab = jnp.sum(jnp.where((row > 0) & (entry <= step), 1.0, 0.0), axis=0, keepdims=True)
    slab = jnp.where(step[:1] < steps, slab, slabs)
    inside = (row > 0) & (start < (step + 1.0) * width)
    final = step[:1] + jnp.sum(jnp.where(inside, 1.0, 0.0), axis=0, keepdims=True)
    leave = jnp.sum(jnp.where(row == step + 1.0, entry, 0.0), axis=0, keepdims=True)
    leave = jnp.where(step[:1] == slabs - 1, steps, leave) - 1.0
    table = jnp.concatenate([slab, final, leave, jnp.zeros((5, 128), F32)], axis=0)
    slab_of[group] = table.astype(jnp.int32)

    found = [
        picked(chosen[q], before[q] + (total[q] + start)[:, :1]).astype(jnp.int32) for q in range(count)
    ]
    for q in range(count):
        spots[group * count + q : group * count + q + 1] = found[q]
    for t, tile in enumerate(ordered(blocks, found, per_group, width)):
        tiles[first + t] = tile


def relay_rows(devices, capacity, slabs, cut, sens, weight, device, cell, owner, slot):
    rows = devices * capacity
    size = min(4096, rows)
    width = min(256, size)
    groups = rows // size
    parts = 2
    length = max(1, min(size // capacity, 512 // capacity)) * capacity
    return pl.pallas_call(
        functools.partial(relay_kernel, cut, slabs, parts),
        out_shape=[
            pltpu.VMEM((rows // width, 8, width), F32),
            jax.ShapeDtypeStruct((groups, 8, 128), jnp.int32),
            pltpu.VMEM((rows // length, length), jnp.int32),
            pltpu.VMEM((devices, 8, capacity), F32),
        ],
        in_specs=[pl.BlockSpec(memory_space=pltpu.HBM)] * 6,
        out_specs=[pl.BlockSpec(memory_space=pltpu.VMEM)] * 4,
        scratch_shapes=[pltpu.VMEM(given.shape, given.dtype) for given in (sens, weight, device, cell, owner, slot)]
        + [
            pltpu.VMEM((devices, 8, capacity), F32),
            pltpu.VMEM((capacity, sens.shape[1]), BF16),
            pltpu.VMEM((devices // parts * 16, sens.shape[1]), BF16),
            pltpu.SemaphoreType.DMA((6,)),
        ]
        + [pltpu.SemaphoreType.DMA((devices,))] * 2,
        compiler_params=pltpu.CompilerParams(collective_id=1, has_side_effects=True, vmem_limit_bytes=60 << 20),
        name="relay_rows",
    )(sens, weight, device, cell, owner, slot)


def located(tile, size_z):
    return split(tile[3:4].astype(jnp.int32), size_z)


def solve_kernel(slab_of, tiles, spots, parcels, stiff_in, anchor_in, coupling_in, adjoint, box, stiff, anchor, coupling, load, stage, late, marks, weighted, inverse, near, edge, halo, terms, found, flat, landed, fetch, late_send, late_recv, x_send, x_recv, y_send, y_recv, box_send, box_recv):
    parts, size_x, size_y, size_z = load.shape
    count, _, width = tiles.shape
    groups = slab_of.shape[0]
    per_group = count // groups
    steps = per_group + size_x
    half = parts * size_y
    exchanges = weighted.shape[0]
    gx, gy = lax.axis_index("gx"), lax.axis_index("gy")
    count_x, count_y = lax.axis_size("gx"), lax.axis_size("gy")
    devices = count_x * count_y
    peer = peer_of(gx, gy, count_x, count_y)
    sides = (("gx", gx, -1, gx > 0), ("gx", gx, 1, gx < count_x - 1), ("gy", gy, -1, gy > 0), ("gy", gy, 1, gy < count_y - 1))
    y_at = lax.broadcasted_iota(jnp.int32, (size_y, size_z), 0)
    z_at = lax.broadcasted_iota(jnp.int32, (size_y, size_z), 1)
    barrier = pltpu.get_barrier_semaphore()

    def greet(step, carry):
        pl.semaphore_signal(barrier, inc=1, device_id=peer(step), device_id_type=MESH)
        return carry

    lax.fori_loop(1, devices, greet, 0)
    fetches = [
        pltpu.make_async_copy(source, target, fetch.at[i])
        for i, (source, target) in enumerate(((stiff_in, stiff), (anchor_in, anchor), (coupling_in, coupling)))
    ]
    for copy in fetches:
        copy.start()

    for side, (axis, place, move, present) in enumerate(sides):

        @pl.when(jnp.logical_not(present))
        def _():
            for index in range(exchanges):
                if axis == "gx":
                    for k in range(parts):
                        weighted[index, k, 0 if move < 0 else size_x + 1] = jnp.zeros((size_y, size_z), F32)
                else:
                    halo[index, side % 2] = jnp.zeros(halo.shape[2:], F32)

    def transfers(index, sending, which=range(4)):
        made = []
        for side in which:
            axis, place, move, present = sides[side]
            there = 1 - side % 2
            landing = there if sending else side % 2
            if axis == "gx":
                into = size_x + 1 if (move < 0) == sending else 0
                pair = (weighted.at[index, :, 1 if move < 0 else size_x], weighted.at[index, :, into])
                sems = (x_send, x_recv)
            else:
                pair = (edge.at[index, side % 2], halo.at[index, landing])
                sems = (y_send, y_recv)
            made.append((present, pltpu.make_async_remote_copy(
                src_ref=pair[0],
                dst_ref=pair[1],
                send_sem=sems[0].at[index, side % 2],
                recv_sem=sems[1].at[index, landing],
                device_id={axis: place + move},
                device_id_type=MESH,
            )))
        return made

    def begin(index):
        for present, copy in transfers(index, True):

            @pl.when(present)
            def _():
                copy.start()

    def arrive(index, which):
        for present, copy in transfers(index, False, which):

            @pl.when(present)
            def _():
                copy.wait_recv()

    rims = (0, size_y - 1)

    def deposit(step, carry):
        made = []
        for group in range(groups):
            slab = slab_of[group, 0, step]
            tile = tiles[group * per_group + jnp.minimum(step - slab, per_group - 1)]
            xy, z = located(tile, size_z)
            pairs = [two_terms(tile[k : k + 1]) for k in range(parts)]
            values = [hi for hi, lo in pairs] + [lo for hi, lo in pairs]
            at_y = matches(size_y, xy - slab * size_y)
            spread = jnp.concatenate([scaled(at_y, value) for value in values], axis=0)
            product = dot_nt(spread, wide_one_hot(size_z, z))
            at = group * steps + step
            earlier = stage[jnp.maximum(at - 1, 0)]
            stage[at] = product[:half] + product[half:] + jnp.where(slab == carry[group], earlier, 0.0)
            made.append(slab)
        return tuple(made)

    late_rows = pl.ds(SENT, FIELDS - SENT)

    def follow(step):
        return pltpu.make_async_remote_copy(
            src_ref=parcels.at[step, late_rows],
            dst_ref=late.at[step, late_rows],
            send_sem=late_send.at[step],
            recv_sem=late_recv.at[step],
            device_id=peer(step),
            device_id_type=MESH,
        )

    def send_late(step, carry):
        follow(devices - step).start()
        return carry

    def take_late(step, carry):
        follow(step).wait_recv()
        return carry

    def sort_late(group):
        senders = devices // groups
        blocks = joined([late.at[group * senders + i] for i in range(senders)], SENT, FIELDS)
        lines = [spots[q : q + 1] for q in range(group * len(blocks), (group + 1) * len(blocks))]
        for t, tile in enumerate(ordered(blocks, lines, per_group, width)):
            marks[group * per_group + t] = tile

    stage[0] = jnp.zeros(stage.shape[1:], F32)
    slabs = lax.fori_loop(0, steps // 2, deposit, tuple(jnp.int32(-1) for _ in range(groups)), unroll=8)
    pl.semaphore_wait(barrier, devices - 1)
    lax.fori_loop(1, devices, send_late, 0)
    late[0] = parcels[0]
    lax.fori_loop(steps // 2, steps, deposit, slabs, unroll=8)
    for copy in fetches:
        copy.wait()

    def first(x, carry):
        stiffness = stiff[x]
        sums = stage[slab_of[0, 2, x]]
        for group in range(1, groups):
            sums = sums + stage[group * steps + slab_of[group, 2, x]]
        for side, rim in enumerate(rims):
            near[2, side, 0, pl.ds(x, 1), :] = stiffness[rim : rim + 1]
        for k in range(parts):
            inverted = 1.0 / (6.0 * stiffness + anchor[k, x] + coupling[4 * k, x])
            inverse[k, x] = inverted
            there = sums[k * size_y : (k + 1) * size_y]
            load[k, x] = there
            value = there * inverted
            adjoint[k, x] = value
            product = stiffness * value
            weighted[0, k, x + 1] = product
            for side, rim in enumerate(rims):
                near[1, side, k, pl.ds(x, 1), :] = inverted[rim : rim + 1]
                edge[0, side, k, pl.ds(x, 1), :] = product[rim : rim + 1]
        return carry

    lax.fori_loop(0, size_x, first, 0)
    begin(0)
    lax.fori_loop(1, devices, take_late, 0)

    for index in range(exchanges):
        last = index + 1 == exchanges
        for group in range(groups * index // exchanges, groups * (index + 1) // exchanges):
            sort_late(group)

        def update(x, carry):
            fields = [adjoint[k, x] for k in range(parts)]
            for k in range(parts):
                product = weighted[index, k, x + 1]
                value = load[k, x] + weighted[index, k, x] + weighted[index, k, x + 2]
                for j in range(parts):
                    if j != k:
                        value = value - coupling[3 * j + k, x] * fields[j]
                value = value + jnp.where(z_at == 0, 0.0, pltpu.roll(product, 1, 1))
                value = value + jnp.where(z_at == size_z - 1, 0.0, pltpu.roll(product, size_z - 1, 1))
                value = value + jnp.where(y_at == 0, 0.0, pltpu.roll(product, 1, 0))
                value = value + jnp.where(y_at == size_y - 1, 0.0, pltpu.roll(product, size_y - 1, 0))
                value = value * inverse[k, x]
                adjoint[k, x] = value
                for side, rim in enumerate(rims):
                    near[0, side, k, pl.ds(x, 1), :] = value[rim : rim + 1]
                if not last:
                    weighted[index + 1, k, x + 1] = stiff[x] * value
            return carry

        lax.fori_loop(1, size_x - 1, update, 0)
        arrive(index, (0, 1))
        update(0, 0)
        update(size_x - 1, 0)
        arrive(index, (2, 3))
        for side, rim in enumerate(rims):
            for k in range(parts):
                value = near[0, side, k] + halo[index, side, k] * near[1, side, k]
                for x in range(size_x):
                    adjoint[k, x, rim : rim + 1, :] = value[x : x + 1]
                if not last:
                    product = near[2, side, 0] * value
                    edge[index + 1, side, k] = product
                    for x in range(size_x):
                        weighted[index + 1, k, x + 1, rim : rim + 1, :] = product[x : x + 1]
        if not last:
            begin(index + 1)

    def cut(x, carry):
        for k in range(parts):
            hi, lo = two_terms(adjoint[k, x])
            terms[x, k * size_y : (k + 1) * size_y] = hi.astype(BF16)
            terms[x, half + k * size_y : half + (k + 1) * size_y] = lo.astype(BF16)
        return carry

    lax.fori_loop(0, size_x, cut, 0)

    def look(step, carry):
        made = []
        for group in range(groups):
            held, before = carry[group]
            slab = slab_of[group, 0, step]
            tile = tiles[group * per_group + jnp.minimum(step - slab, per_group - 1)]
            xy, z = located(tile, size_z)
            at_y = matches(size_y, xy - slab * size_y)
            columns = jnp.dot(terms[jnp.minimum(slab, size_x - 1)], wide_one_hot(size_z, z), preferred_element_type=F32)
            columns = columns[:half] + columns[half:]
            value = jnp.concatenate(
                [picked(at_y, columns[k * size_y : (k + 1) * size_y]) for k in range(parts)], axis=0
            )
            held = value + jnp.where(slab == before, 0.0, held)
            found[group * steps + step, :parts] = held
            made.append((held, slab))
        return tuple(made)

    lax.fori_loop(
        0, steps, look, tuple((jnp.zeros((parts, width), F32), jnp.int32(0)) for _ in range(groups)), unroll=4
    )
    total = jnp.zeros((2 * parts * devices, BOX_DEV), F32)
    join = min(8, count)
    for begin_at in range(0, count, join):
        numbers = range(begin_at, begin_at + join)

        def line(field):
            return jnp.concatenate([marks[t, field : field + 1] for t in numbers], axis=1)

        owner, slot = split(line(5).astype(jnp.int32), BOX_DEV)
        rows = jnp.concatenate(
            [found[t // per_group * steps + slab_of[t // per_group, 1, t % per_group]][:parts] for t in numbers], axis=1
        ) * line(4)
        at_owner = matches(devices, owner)
        pairs = [two_terms(rows[k : k + 1]) for k in range(parts)]
        values = [hi for hi, lo in pairs] + [lo for hi, lo in pairs]
        spread = jnp.concatenate([scaled(at_owner, value) for value in values], axis=0)
        total = total + dot_nt(spread, wide_one_hot(BOX_DEV, slot))
    for k in range(parts):
        part = total[k * devices : (k + 1) * devices] + total[(parts + k) * devices : (parts + k + 1) * devices]
        flat[k] = jnp.concatenate([part, jnp.zeros_like(part)], axis=1)

    def parcel(step):
        there = peer(step)
        return pltpu.make_async_remote_copy(
            src_ref=flat.at[:, pl.ds(there[0] * count_y + there[1], 1)],
            dst_ref=landed.at[:, pl.ds(step, 1)],
            send_sem=box_send.at[step],
            recv_sem=box_recv.at[step],
            device_id=there,
            device_id_type=MESH,
        )

    def post(step, carry):
        parcel(devices - step).start()
        return carry

    lax.fori_loop(1, devices, post, 0)
    landed[:, 0:1] = flat[:, pl.ds(gx * count_y + gy, 1)]

    def collect(step, carry):
        parcel(step).wait_recv()
        return carry

    lax.fori_loop(1, devices, collect, 0)
    for k in range(parts):
        box[k : k + 1] = jnp.sum(landed[k], axis=0, keepdims=True)[:, :BOX_DEV]

    def sent(step, carry):
        parcel(step).wait_send()
        return carry

    lax.fori_loop(1, devices, sent, 0)

    def left(step, carry):
        follow(step).wait_send()
        return carry

    lax.fori_loop(1, devices, left, 0)
    for index in range(exchanges):
        for present, copy in transfers(index, True):

            @pl.when(present)
            def _():
                copy.wait_send()


def solve_rows(devices, tiles, slab_of, spots, parcels, stiffness, anchor, coupling):
    size_x, size_y, size_z = stiffness.shape
    parts = anchor.shape[0]
    exchanges = SWEEPS - 1
    count, fields, width = tiles.shape
    groups = slab_of.shape[0]
    steps = count // groups + size_x
    kept_near = [pltpu.with_memory_space_constraint(value, pltpu.VMEM) for value in (tiles, spots, parcels)]
    return pl.pallas_call(
        solve_kernel,
        out_shape=[pltpu.VMEM(anchor.shape, F32), pltpu.VMEM((parts, BOX_DEV), F32)],
        in_specs=[pl.BlockSpec(memory_space=pltpu.SMEM)]
        + [pl.BlockSpec(memory_space=pltpu.VMEM)] * 3
        + [pl.BlockSpec(memory_space=pltpu.HBM)] * 3,
        out_specs=[pl.BlockSpec(memory_space=pltpu.VMEM)] * 2,
        scratch_shapes=[
            pltpu.VMEM(stiffness.shape, F32),
            pltpu.VMEM(anchor.shape, F32),
            pltpu.VMEM(coupling.shape, F32),
            pltpu.VMEM(anchor.shape, F32),
            pltpu.VMEM((groups * steps, parts * size_y, size_z), F32),
            pltpu.VMEM(parcels.shape, F32),
            pltpu.VMEM(tiles.shape, F32),
            pltpu.VMEM((exchanges, parts, size_x + 2, size_y, size_z), F32),
            pltpu.VMEM(anchor.shape, F32),
            pltpu.VMEM((3, 2, parts, size_x, size_z), F32),
            pltpu.VMEM((exchanges, 2, parts, size_x, size_z), F32),
            pltpu.VMEM((exchanges, 2, parts, size_x, size_z), F32),
            pltpu.VMEM((size_x, 2 * parts * size_y, size_z), BF16),
            pltpu.VMEM((groups * steps, fields, width), F32),
            pltpu.VMEM((parts, devices, 2 * BOX_DEV), F32),
            pltpu.VMEM((parts, devices, 2 * BOX_DEV), F32),
            pltpu.SemaphoreType.DMA((3,)),
        ]
        + [pltpu.SemaphoreType.DMA((devices,))] * 2
        + [pltpu.SemaphoreType.DMA((exchanges, 2))] * 4
        + [pltpu.SemaphoreType.DMA((devices,))] * 2,
        compiler_params=pltpu.CompilerParams(collective_id=0, has_side_effects=True, vmem_limit_bytes=56 << 20),
        name="solve_rows",
    )(slab_of, *kept_near, stiffness, anchor, coupling)


def body(
    sensitivity,
    node_weight,
    dest_device,
    dest_cell,
    box_owner,
    box_slot,
    stiffness,
    anchor,
    coupling,
):
    devices = lax.axis_size("gx") * lax.axis_size("gy")
    row_count = sensitivity.shape[1]
    capacity = 2 * row_count // devices
    size_x, size_y, size_z = stiffness.shape
    size_xy = size_x * size_y
    assert size_xy * size_z <= 2**17 and devices * BOX_DEV <= 2**17

    def row(values):
        return values.reshape(1, row_count)

    tiles, slab_of, spots, parcels = relay_rows(
        devices,
        capacity,
        size_x,
        size_y * size_z,
        sensitivity,
        row(node_weight),
        row(dest_device),
        row(dest_cell),
        row(box_owner),
        row(box_slot),
    )
    adjoint, box_gradient = solve_rows(devices, tiles, slab_of, spots, parcels, stiffness, anchor, coupling)
    return (adjoint, box_gradient)


def solution(mesh):
    placed = (
        P(None, ("gx", "gy")),
        P(("gx", "gy")),
        P(("gx", "gy"), None),
        P(("gx", "gy")),
        P(("gx", "gy"), None),
        P(("gx", "gy")),
        P("gx", "gy", None),
        P(None, "gx", "gy", None),
        P(None, "gx", "gy", None),
    )
    return jax.shard_map(
        body,
        mesh=mesh,
        in_specs=placed,
        out_specs=(P(None, "gx", "gy", None), P(None, ("gx", "gy"))),
        check_vma=False,
    )
```

```python
import functools

import jax
import jax.numpy as jnp
from jax import lax
from jax.experimental import pallas as pl
from jax.experimental.pallas import tpu as pltpu
from jax.sharding import PartitionSpec as P

BOX_DEV = 64
SWEEPS = 4
SENT = 4
FIELDS = 6
NT = (((1,), (1,)), ((), ()))
F32 = jnp.float32
BF16 = jnp.bfloat16
MESH = pl.DeviceIdType.MESH


def two_terms(x):
    hi = x.astype(BF16).astype(F32)
    return hi, x - hi


def matches(count, row):
    return lax.broadcasted_iota(jnp.int32, (count, row.shape[1]), 0) == row


def one_hot(mask):
    return jnp.where(mask, 1.0, 0.0).astype(BF16)


def scaled(mask, row):
    return jnp.where(mask, row, 0.0).astype(BF16)


def dot_nt(a, b):
    return lax.dot_general(a, b, NT, preferred_element_type=F32)


def split(value, size):
    if size & (size - 1) == 0:
        return value >> (size.bit_length() - 1), value & (size - 1)
    return value // size, value % size


def wide_matches(count, row):
    return lax.broadcasted_iota(jnp.int16, (count, row.shape[1]), 0) == row.astype(jnp.int16)


def wide_one_hot(count, row):
    return jnp.where(wide_matches(count, row), jnp.array(1, BF16), jnp.array(0, BF16))


def kept(mask, values):
    return jnp.where(mask, values, jnp.array(0, BF16))


def fan(values, index, count):
    size, length = values.shape
    many = min(count, max(1, 16 // size))
    terms = jnp.concatenate([values] * many, axis=0).astype(BF16)
    part = lax.broadcasted_iota(jnp.int32, terms.shape, 0) // size
    index = (jnp.broadcast_to(index, terms.shape) - part).astype(jnp.int16)
    return jnp.concatenate([kept(index == t, terms) for t in range(0, count, many)], axis=0)


def two_rows(rows):
    return jnp.concatenate(two_terms(jnp.concatenate(rows, axis=0)), axis=0)


def halves(values):
    size = values.shape[0] // 2
    return values[:size] + values[size:]


def folded(a, b, size):
    if size & (size - 1):
        return (a + b) % size
    total, bit = 0, 1
    while bit < size:
        total = total + bit * ((a // bit + b // bit) % 2)
        bit = 2 * bit
    return total


def peer_of(gx, gy, size_x, size_y):
    return lambda step: (folded(gx, step // size_y, size_x), (gy + step % size_y) % size_y)


def running(numbers):
    totals = [jnp.zeros_like(numbers[0])]
    for number in numbers:
        totals.append(totals[-1] + number)
    return totals


def ordinals(chosen):
    length = chosen[0].shape[1]
    stacked = one_hot(jnp.concatenate(chosen, axis=0))
    earlier = one_hot(
        lax.broadcasted_iota(jnp.int32, (length, length), 0)
        < lax.broadcasted_iota(jnp.int32, (length, length), 1)
    )
    before = jnp.dot(stacked, earlier, preferred_element_type=F32)
    number = jnp.dot(stacked, jnp.ones((length, 128), BF16), preferred_element_type=F32)
    size = chosen[0].shape[0]

    def cut(values):
        return [values[q * size : (q + 1) * size] for q in range(len(chosen))]

    return cut(before), cut(number)


def picked(mask, value):
    return jnp.sum(jnp.where(mask, value, 0.0), axis=0, keepdims=True)


def relay_kernel(cut, slabs, *refs):
    given, refs = refs[:6], refs[6:]
    tiles, slab_of, spots, send, sens, weight, device, cell, owner, slot, recv, place, spread, fetch, send_sem, recv_sem = refs
    count, fields, capacity = send.shape
    rows = sens.shape[1]
    _, _, width = tiles.shape
    groups = slab_of.shape[0]
    per_group = tiles.shape[0] // groups
    gx, gy = lax.axis_index("gx"), lax.axis_index("gy")
    size_x, size_y = lax.axis_size("gx"), lax.axis_size("gy")
    peer = peer_of(gx, gy, size_x, size_y)
    barrier = pltpu.get_barrier_semaphore()
    fetches = [
        pltpu.make_async_copy(source, target, fetch.at[i])
        for i, (source, target) in enumerate(zip(given, (sens, weight, device, cell, owner, slot)))
    ]
    for copy in fetches:
        copy.start()

    def greet(step, carry):
        pl.semaphore_signal(barrier, inc=1, device_id=peer(step), device_id_type=MESH)
        return carry

    lax.fori_loop(1, count, greet, 0)

    length = min(512, rows)
    chunks = rows // length
    spans = [slice(q * length, (q + 1) * length) for q in range(chunks)]
    for copy in fetches:
        copy.wait()
    to_x, to_y = split(device[...], size_y)
    to_y = to_y - gy
    to_y = jnp.where(to_y < 0, to_y + size_y, to_y)
    if size_x & (size_x - 1):
        to_x = to_x - gx
        to_x = jnp.where(to_x < 0, to_x + size_x, to_x)
    else:
        to_x = to_x ^ gx
    target = to_x * size_y + to_y
    chosen = [matches(count, target[:, span]) for span in spans]
    before, number = ordinals(chosen)
    total = running(number)
    for q, span in enumerate(spans):
        rank = picked(chosen[q], before[q] + total[q][:, :1]).astype(jnp.int32)
        place[:, span] = wide_one_hot(capacity, rank)

    def copy(step):
        return pltpu.make_async_remote_copy(
            src_ref=send.at[step, pl.ds(0, SENT)],
            dst_ref=recv.at[step, pl.ds(0, SENT)],
            send_sem=send_sem.at[step],
            recv_sem=recv_sem.at[step],
            device_id=peer(step),
            device_id_type=MESH,
        )

    def start(step, carry):
        copy(step).start()
        return carry

    def packed(rows, low):
        size = 2 * len(rows)
        for span in spans:
            spread[: count * size, span] = fan(two_rows([read(span) for read in rows]), target[:, span], count)
        product = dot_nt(spread[: count * size], place[...])
        for t in range(count):
            send[t, low : low + len(rows)] = halves(product[t * size : (t + 1) * size])

    packed([lambda span, k=k: sens[k : k + 1, span] for k in range(3)] + [lambda span: cell[:, span].astype(F32)], 0)
    pl.semaphore_wait(barrier, count - 1)
    lax.fori_loop(1, count, start, 0)
    packed([lambda span: weight[:, span], lambda span: (owner[:, span] * BOX_DEV + slot[:, span]).astype(F32)], SENT)
    recv[0] = send[0]

    def arrive(step, carry):
        copy(step).wait_recv()
        return carry

    senders = count // groups
    for group in range(groups):
        lax.fori_loop(max(1, group * senders), (group + 1) * senders, arrive, 0)
        sort_group(cut, slabs, [recv.at[group * senders + i] for i in range(senders)], tiles, group * per_group, per_group, slab_of, spots, group)

    def sent(step, carry):
        copy(step).wait_send()
        return carry

    lax.fori_loop(1, count, sent, 0)


def joined(arrived, low, high):
    join = max(1, min(len(arrived), 512 // arrived[0].shape[1]))
    return [
        jnp.concatenate([arrived[q + i][low:high] for i in range(join)], axis=1)
        for q in range(0, len(arrived), join)
    ]


def ordered(blocks, spots, per_group, width):
    size = 2 * blocks[0].shape[0]
    sums = jnp.zeros((per_group * size, width), F32)
    for block, spot in zip(blocks, spots):
        tile, lane = split(spot, width)
        spread = fan(jnp.concatenate(two_terms(block), axis=0), tile, per_group)
        sums = sums + dot_nt(spread, wide_one_hot(width, lane))
    return [halves(sums[t * size : (t + 1) * size]) for t in range(per_group)]


def sort_group(cut, slabs, arrived, tiles, first, per_group, slab_of, spots, group):
    width = tiles.shape[2]
    blocks = joined(arrived, 0, SENT)
    count = len(blocks)
    chosen = [matches(slabs, split(block[3:4].astype(jnp.int32), cut)[0]) for block in blocks]
    before, number = ordinals(chosen)
    total = running(number)
    lower = one_hot(
        lax.broadcasted_iota(jnp.int32, (slabs, slabs), 1)
        < lax.broadcasted_iota(jnp.int32, (slabs, slabs), 0)
    )
    tens = jnp.floor(total[-1] * 0.0625)
    start = 16.0 * jnp.dot(lower, tens.astype(BF16), preferred_element_type=F32)
    start = start + jnp.dot(lower, (total[-1] - 16.0 * tens).astype(BF16), preferred_element_type=F32)

    steps = per_group + slabs - 1
    row = lax.broadcasted_iota(jnp.int32, start.shape, 0).astype(F32)
    step = lax.broadcasted_iota(jnp.int32, start.shape, 1).astype(F32)
    entry = row + jnp.minimum(jnp.floor(start * (1.0 / width)), per_group - 1.0)
    slab = jnp.sum(jnp.where((row > 0) & (entry <= step), 1.0, 0.0), axis=0, keepdims=True)
    slab = jnp.where(step[:1] < steps, slab, slabs)
    inside = (row > 0) & (start < (step + 1.0) * width)
    final = step[:1] + jnp.sum(jnp.where(inside, 1.0, 0.0), axis=0, keepdims=True)
    leave = jnp.sum(jnp.where(row == step + 1.0, entry, 0.0), axis=0, keepdims=True)
    leave = jnp.where(step[:1] == slabs - 1, steps, leave) - 1.0
    table = jnp.concatenate([slab, final, leave, jnp.zeros((5, 128), F32)], axis=0)
    slab_of[group] = table.astype(jnp.int32)

    found = [
        picked(chosen[q], before[q] + (total[q] + start)[:, :1]).astype(jnp.int32) for q in range(count)
    ]
    for q in range(count):
        spots[group * count + q : group * count + q + 1] = found[q]
    for t, tile in enumerate(ordered(blocks, found, per_group, width)):
        tiles[first + t, :SENT] = tile


def relay_rows(devices, capacity, slabs, cut, sens, weight, device, cell, owner, slot):
    rows = devices * capacity
    size = min(4096, rows)
    width = min(256, size)
    groups = rows // size
    length = max(1, min(size // capacity, 512 // capacity)) * capacity
    return pl.pallas_call(
        functools.partial(relay_kernel, cut, slabs),
        out_shape=[
            pltpu.VMEM((rows // width, 8, width), F32),
            jax.ShapeDtypeStruct((groups, 8, 128), jnp.int32),
            pltpu.VMEM((rows // length, length), jnp.int32),
            pltpu.VMEM((devices, 8, capacity), F32),
        ],
        in_specs=[pl.BlockSpec(memory_space=pltpu.HBM)] * 6,
        out_specs=[pl.BlockSpec(memory_space=pltpu.VMEM)] * 4,
        scratch_shapes=[pltpu.VMEM(given.shape, given.dtype) for given in (sens, weight, device, cell, owner, slot)]
        + [
            pltpu.VMEM((devices, 8, capacity), F32),
            pltpu.VMEM((capacity, sens.shape[1]), BF16),
            pltpu.VMEM((devices * 2 * SENT, sens.shape[1]), BF16),
            pltpu.SemaphoreType.DMA((6,)),
        ]
        + [pltpu.SemaphoreType.DMA((devices,))] * 2,
        compiler_params=pltpu.CompilerParams(collective_id=1, has_side_effects=True, vmem_limit_bytes=60 << 20),
        name="relay_rows",
    )(sens, weight, device, cell, owner, slot)


def located(tile, size_z):
    return split(tile[3:4].astype(jnp.int32), size_z)


def solve_kernel(slab_of, tiles, spots, parcels, stiff_in, anchor_in, coupling_in, adjoint, box, stiff, anchor, coupling, load, stage, late, marks, weighted, inverse, near, edge, halo, terms, found, flat, landed, fetch, late_send, late_recv, x_send, x_recv, y_send, y_recv, box_send, box_recv):
    parts, size_x, size_y, size_z = load.shape
    count, _, width = tiles.shape
    groups = slab_of.shape[0]
    per_group = count // groups
    steps = per_group + size_x
    half = parts * size_y
    exchanges = weighted.shape[0]
    gx, gy = lax.axis_index("gx"), lax.axis_index("gy")
    count_x, count_y = lax.axis_size("gx"), lax.axis_size("gy")
    devices = count_x * count_y
    peer = peer_of(gx, gy, count_x, count_y)
    sides = (("gx", gx, -1, gx > 0), ("gx", gx, 1, gx < count_x - 1), ("gy", gy, -1, gy > 0), ("gy", gy, 1, gy < count_y - 1))
    y_at = lax.broadcasted_iota(jnp.int32, (size_y, size_z), 0)
    z_at = lax.broadcasted_iota(jnp.int32, (size_y, size_z), 1)
    barrier = pltpu.get_barrier_semaphore()

    def greet(step, carry):
        pl.semaphore_signal(barrier, inc=1, device_id=peer(step), device_id_type=MESH)
        return carry

    lax.fori_loop(1, devices, greet, 0)
    fetches = [
        pltpu.make_async_copy(source, target, fetch.at[i])
        for i, (source, target) in enumerate(((stiff_in, stiff), (anchor_in, anchor), (coupling_in, coupling)))
    ]
    for copy in fetches:
        copy.start()

    for side, (axis, place, move, present) in enumerate(sides):

        @pl.when(jnp.logical_not(present))
        def _():
            for index in range(exchanges):
                if axis == "gx":
                    for k in range(parts):
                        weighted[index, k, 0 if move < 0 else size_x + 1] = jnp.zeros((size_y, size_z), F32)
                else:
                    halo[index, side % 2] = jnp.zeros(halo.shape[2:], F32)

    def transfers(index, sending, which=range(4)):
        made = []
        for side in which:
            axis, place, move, present = sides[side]
            there = 1 - side % 2
            landing = there if sending else side % 2
            if axis == "gx":
                into = size_x + 1 if (move < 0) == sending else 0
                pair = (weighted.at[index, :, 1 if move < 0 else size_x], weighted.at[index, :, into])
                sems = (x_send, x_recv)
            else:
                pair = (edge.at[index, side % 2], halo.at[index, landing])
                sems = (y_send, y_recv)
            made.append((present, pltpu.make_async_remote_copy(
                src_ref=pair[0],
                dst_ref=pair[1],
                send_sem=sems[0].at[index, side % 2],
                recv_sem=sems[1].at[index, landing],
                device_id={axis: place + move},
                device_id_type=MESH,
            )))
        return made

    def begin(index):
        for present, copy in transfers(index, True):

            @pl.when(present)
            def _():
                copy.start()

    def arrive(index, which):
        for present, copy in transfers(index, False, which):

            @pl.when(present)
            def _():
                copy.wait_recv()

    rims = (0, size_y - 1)

    def deposit(step, carry):
        made = []
        for group in range(groups):
            slab = slab_of[group, 0, step]
            tile = tiles[group * per_group + jnp.minimum(step - slab, per_group - 1)]
            xy, z = located(tile, size_z)
            pairs = [two_terms(tile[k : k + 1]) for k in range(parts)]
            values = [hi for hi, lo in pairs] + [lo for hi, lo in pairs]
            at_y = matches(size_y, xy - slab * size_y)
            spread = jnp.concatenate([scaled(at_y, value) for value in values], axis=0)
            product = dot_nt(spread, wide_one_hot(size_z, z))
            at = group * steps + step
            earlier = stage[jnp.maximum(at - 1, 0)]
            stage[at] = product[:half] + product[half:] + jnp.where(slab == carry[group], earlier, 0.0)
            made.append(slab)
        return tuple(made)

    late_rows = pl.ds(SENT, FIELDS - SENT)

    def follow(step):
        return pltpu.make_async_remote_copy(
            src_ref=parcels.at[step, late_rows],
            dst_ref=late.at[step, late_rows],
            send_sem=late_send.at[step],
            recv_sem=late_recv.at[step],
            device_id=peer(step),
            device_id_type=MESH,
        )

    def send_late(step, carry):
        follow(devices - step).start()
        return carry

    def take_late(step, carry):
        follow(step).wait_recv()
        return carry

    def sort_late(group):
        senders = devices // groups
        blocks = joined([late.at[group * senders + i] for i in range(senders)], SENT, FIELDS)
        lines = [spots[q : q + 1] for q in range(group * len(blocks), (group + 1) * len(blocks))]
        for t, tile in enumerate(ordered(blocks, lines, per_group, width)):
            marks[group * per_group + t, : FIELDS - SENT] = tile

    stage[0] = jnp.zeros(stage.shape[1:], F32)
    slabs = lax.fori_loop(0, steps // 2, deposit, tuple(jnp.int32(-1) for _ in range(groups)), unroll=8)
    pl.semaphore_wait(barrier, devices - 1)
    lax.fori_loop(1, devices, send_late, 0)
    late[0] = parcels[0]
    lax.fori_loop(steps // 2, steps, deposit, slabs, unroll=8)
    for copy in fetches:
        copy.wait()

    def first(x, carry):
        stiffness = stiff[x]
        sums = stage[slab_of[0, 2, x]]
        for group in range(1, groups):
            sums = sums + stage[group * steps + slab_of[group, 2, x]]
        for side, rim in enumerate(rims):
            near[2, side, 0, pl.ds(x, 1), :] = stiffness[rim : rim + 1]
        for k in range(parts):
            inverted = 1.0 / (6.0 * stiffness + anchor[k, x] + coupling[4 * k, x])
            inverse[k, x] = inverted
            there = sums[k * size_y : (k + 1) * size_y]
            load[k, x] = there
            value = there * inverted
            adjoint[k, x] = value
            product = stiffness * value
            weighted[0, k, x + 1] = product
            for side, rim in enumerate(rims):
                near[1, side, k, pl.ds(x, 1), :] = inverted[rim : rim + 1]
                edge[0, side, k, pl.ds(x, 1), :] = product[rim : rim + 1]
        return carry

    lax.fori_loop(0, size_x, first, 0)
    begin(0)
    lax.fori_loop(1, devices, take_late, 0)

    for index in range(exchanges):
        last = index + 1 == exchanges
        for group in range(groups * index // exchanges, groups * (index + 1) // exchanges):
            sort_late(group)

        def update(x, carry):
            fields = [adjoint[k, x] for k in range(parts)]
            for k in range(parts):
                product = weighted[index, k, x + 1]
                value = load[k, x] + weighted[index, k, x] + weighted[index, k, x + 2]
                for j in range(parts):
                    if j != k:
                        value = value - coupling[3 * j + k, x] * fields[j]
                value = value + jnp.where(z_at == 0, 0.0, pltpu.roll(product, 1, 1))
                value = value + jnp.where(z_at == size_z - 1, 0.0, pltpu.roll(product, size_z - 1, 1))
                value = value + jnp.where(y_at == 0, 0.0, pltpu.roll(product, 1, 0))
                value = value + jnp.where(y_at == size_y - 1, 0.0, pltpu.roll(product, size_y - 1, 0))
                value = value * inverse[k, x]
                adjoint[k, x] = value
                for side, rim in enumerate(rims):
                    near[0, side, k, pl.ds(x, 1), :] = value[rim : rim + 1]
                if not last:
                    weighted[index + 1, k, x + 1] = stiff[x] * value
            return carry

        lax.fori_loop(1, size_x - 1, update, 0)
        arrive(index, (0, 1))
        update(0, 0)
        update(size_x - 1, 0)
        arrive(index, (2, 3))
        for side, rim in enumerate(rims):
            for k in range(parts):
                value = near[0, side, k] + halo[index, side, k] * near[1, side, k]
                for x in range(size_x):
                    adjoint[k, x, rim : rim + 1, :] = value[x : x + 1]
                if not last:
                    product = near[2, side, 0] * value
                    edge[index + 1, side, k] = product
                    for x in range(size_x):
                        weighted[index + 1, k, x + 1, rim : rim + 1, :] = product[x : x + 1]
        if not last:
            begin(index + 1)

    def cut(x, carry):
        for k in range(parts):
            hi, lo = two_terms(adjoint[k, x])
            terms[x, k * size_y : (k + 1) * size_y] = hi.astype(BF16)
            terms[x, half + k * size_y : half + (k + 1) * size_y] = lo.astype(BF16)
        return carry

    lax.fori_loop(0, size_x, cut, 0)

    def look(step, carry):
        made = []
        for group in range(groups):
            held, before = carry[group]
            slab = slab_of[group, 0, step]
            tile = tiles[group * per_group + jnp.minimum(step - slab, per_group - 1)]
            xy, z = located(tile, size_z)
            at_y = matches(size_y, xy - slab * size_y)
            columns = jnp.dot(terms[jnp.minimum(slab, size_x - 1)], wide_one_hot(size_z, z), preferred_element_type=F32)
            columns = columns[:half] + columns[half:]
            value = jnp.concatenate(
                [picked(at_y, columns[k * size_y : (k + 1) * size_y]) for k in range(parts)], axis=0
            )
            held = value + jnp.where(slab == before, 0.0, held)
            found[group * steps + step, :parts] = held
            made.append((held, slab))
        return tuple(made)

    lax.fori_loop(
        0, steps, look, tuple((jnp.zeros((parts, width), F32), jnp.int32(0)) for _ in range(groups)), unroll=4
    )
    total = jnp.zeros((2 * parts * devices, BOX_DEV), F32)
    join = min(8, count)
    for begin_at in range(0, count, join):
        numbers = range(begin_at, begin_at + join)

        def line(field):
            return jnp.concatenate([marks[t, field : field + 1] for t in numbers], axis=1)

        owner, slot = split(line(1).astype(jnp.int32), BOX_DEV)
        rows = jnp.concatenate(
            [found[t // per_group * steps + slab_of[t // per_group, 1, t % per_group]][:parts] for t in numbers], axis=1
        ) * line(0)
        at_owner = matches(devices, owner)
        pairs = [two_terms(rows[k : k + 1]) for k in range(parts)]
        values = [hi for hi, lo in pairs] + [lo for hi, lo in pairs]
        spread = jnp.concatenate([scaled(at_owner, value) for value in values], axis=0)
        total = total + dot_nt(spread, wide_one_hot(BOX_DEV, slot))
    for k in range(parts):
        part = total[k * devices : (k + 1) * devices] + total[(parts + k) * devices : (parts + k + 1) * devices]
        flat[k] = jnp.concatenate([part, jnp.zeros_like(part)], axis=1)

    def parcel(step):
        there = peer(step)
        return pltpu.make_async_remote_copy(
            src_ref=flat.at[:, pl.ds(there[0] * count_y + there[1], 1)],
            dst_ref=landed.at[:, pl.ds(step, 1)],
            send_sem=box_send.at[step],
            recv_sem=box_recv.at[step],
            device_id=there,
            device_id_type=MESH,
        )

    def post(step, carry):
        parcel(devices - step).start()
        return carry

    lax.fori_loop(1, devices, post, 0)
    landed[:, 0:1] = flat[:, pl.ds(gx * count_y + gy, 1)]

    def collect(step, carry):
        parcel(step).wait_recv()
        return carry

    lax.fori_loop(1, devices, collect, 0)
    for k in range(parts):
        box[k : k + 1] = jnp.sum(landed[k], axis=0, keepdims=True)[:, :BOX_DEV]

    def sent(step, carry):
        parcel(step).wait_send()
        return carry

    lax.fori_loop(1, devices, sent, 0)

    def left(step, carry):
        follow(step).wait_send()
        return carry

    lax.fori_loop(1, devices, left, 0)
    for index in range(exchanges):
        for present, copy in transfers(index, True):

            @pl.when(present)
            def _():
                copy.wait_send()


def solve_rows(devices, tiles, slab_of, spots, parcels, stiffness, anchor, coupling):
    size_x, size_y, size_z = stiffness.shape
    parts = anchor.shape[0]
    exchanges = SWEEPS - 1
    count, fields, width = tiles.shape
    groups = slab_of.shape[0]
    steps = count // groups + size_x
    kept_near = [pltpu.with_memory_space_constraint(value, pltpu.VMEM) for value in (tiles, spots, parcels)]
    return pl.pallas_call(
        solve_kernel,
        out_shape=[pltpu.VMEM(anchor.shape, F32), pltpu.VMEM((parts, BOX_DEV), F32)],
        in_specs=[pl.BlockSpec(memory_space=pltpu.SMEM)]
        + [pl.BlockSpec(memory_space=pltpu.VMEM)] * 3
        + [pl.BlockSpec(memory_space=pltpu.HBM)] * 3,
        out_specs=[pl.BlockSpec(memory_space=pltpu.VMEM)] * 2,
        scratch_shapes=[
            pltpu.VMEM(stiffness.shape, F32),
            pltpu.VMEM(anchor.shape, F32),
            pltpu.VMEM(coupling.shape, F32),
            pltpu.VMEM(anchor.shape, F32),
            pltpu.VMEM((groups * steps, parts * size_y, size_z), F32),
            pltpu.VMEM(parcels.shape, F32),
            pltpu.VMEM(tiles.shape, F32),
            pltpu.VMEM((exchanges, parts, size_x + 2, size_y, size_z), F32),
            pltpu.VMEM(anchor.shape, F32),
            pltpu.VMEM((3, 2, parts, size_x, size_z), F32),
            pltpu.VMEM((exchanges, 2, parts, size_x, size_z), F32),
            pltpu.VMEM((exchanges, 2, parts, size_x, size_z), F32),
            pltpu.VMEM((size_x, 2 * parts * size_y, size_z), BF16),
            pltpu.VMEM((groups * steps, fields, width), F32),
            pltpu.VMEM((parts, devices, 2 * BOX_DEV), F32),
            pltpu.VMEM((parts, devices, 2 * BOX_DEV), F32),
            pltpu.SemaphoreType.DMA((3,)),
        ]
        + [pltpu.SemaphoreType.DMA((devices,))] * 2
        + [pltpu.SemaphoreType.DMA((exchanges, 2))] * 4
        + [pltpu.SemaphoreType.DMA((devices,))] * 2,
        compiler_params=pltpu.CompilerParams(collective_id=0, has_side_effects=True, vmem_limit_bytes=56 << 20),
        name="solve_rows",
    )(slab_of, *kept_near, stiffness, anchor, coupling)


def body(
    sensitivity,
    node_weight,
    dest_device,
    dest_cell,
    box_owner,
    box_slot,
    stiffness,
    anchor,
    coupling,
):
    devices = lax.axis_size("gx") * lax.axis_size("gy")
    row_count = sensitivity.shape[1]
    capacity = 2 * row_count // devices
    size_x, size_y, size_z = stiffness.shape
    size_xy = size_x * size_y
    assert size_xy * size_z <= 2**17 and devices * BOX_DEV <= 2**17

    def row(values):
        return values.reshape(1, row_count)

    tiles, slab_of, spots, parcels = relay_rows(
        devices,
        capacity,
        size_x,
        size_y * size_z,
        sensitivity,
        row(node_weight),
        row(dest_device),
        row(dest_cell),
        row(box_owner),
        row(box_slot),
    )
    adjoint, box_gradient = solve_rows(devices, tiles, slab_of, spots, parcels, stiffness, anchor, coupling)
    return (adjoint, box_gradient)


def solution(mesh):
    placed = (
        P(None, ("gx", "gy")),
        P(("gx", "gy")),
        P(("gx", "gy"), None),
        P(("gx", "gy")),
        P(("gx", "gy"), None),
        P(("gx", "gy")),
        P("gx", "gy", None),
        P(None, "gx", "gy", None),
        P(None, "gx", "gy", None),
    )
    return jax.shard_map(
        body,
        mesh=mesh,
        in_specs=placed,
        out_specs=(P(None, "gx", "gy", None), P(None, ("gx", "gy"))),
        check_vma=False,
    )
```

```python
import functools

import jax
import jax.numpy as jnp
from jax import lax
from jax.experimental import pallas as pl
from jax.experimental.pallas import tpu as pltpu
from jax.sharding import PartitionSpec as P

BOX_DEV = 64
SWEEPS = 4
SENT = 4
FIELDS = 6
NT = (((1,), (1,)), ((), ()))
F32 = jnp.float32
BF16 = jnp.bfloat16
MESH = pl.DeviceIdType.MESH


def two_terms(x):
    hi = x.astype(BF16).astype(F32)
    return hi, x - hi


def matches(count, row):
    return lax.broadcasted_iota(jnp.int32, (count, row.shape[1]), 0) == row


def one_hot(mask):
    return jnp.where(mask, 1.0, 0.0).astype(BF16)


def scaled(mask, row):
    return jnp.where(mask, row, 0.0).astype(BF16)


def dot_nt(a, b):
    return lax.dot_general(a, b, NT, preferred_element_type=F32)


def split(value, size):
    if size & (size - 1) == 0:
        return value >> (size.bit_length() - 1), value & (size - 1)
    return value // size, value % size


def wide_matches(count, row):
    return lax.broadcasted_iota(jnp.int16, (count, row.shape[1]), 0) == row.astype(jnp.int16)


def wide_one_hot(count, row):
    return jnp.where(wide_matches(count, row), jnp.array(1, BF16), jnp.array(0, BF16))


def kept(mask, values):
    return jnp.where(mask, values, jnp.array(0, BF16))


def fan(values, index, count):
    size, length = values.shape
    many = min(count, max(1, 16 // size))
    terms = jnp.concatenate([values] * many, axis=0).astype(BF16)
    part = lax.broadcasted_iota(jnp.int32, terms.shape, 0) // size
    index = (jnp.broadcast_to(index, terms.shape) - part).astype(jnp.int16)
    return jnp.concatenate([kept(index == t, terms) for t in range(0, count, many)], axis=0)


def two_rows(rows):
    return jnp.concatenate(two_terms(jnp.concatenate(rows, axis=0)), axis=0)


def halves(values):
    size = values.shape[0] // 2
    return values[:size] + values[size:]


def folded(a, b, size):
    if size & (size - 1):
        return (a + b) % size
    total, bit = 0, 1
    while bit < size:
        total = total + bit * ((a // bit + b // bit) % 2)
        bit = 2 * bit
    return total


def peer_of(gx, gy, size_x, size_y):
    return lambda step: (folded(gx, step // size_y, size_x), (gy + step % size_y) % size_y)


def running(numbers):
    totals = [jnp.zeros_like(numbers[0])]
    for number in numbers:
        totals.append(totals[-1] + number)
    return totals


def ordinals(chosen):
    length = chosen[0].shape[1]
    stacked = one_hot(jnp.concatenate(chosen, axis=0))
    earlier = one_hot(
        lax.broadcasted_iota(jnp.int32, (length, length), 0)
        < lax.broadcasted_iota(jnp.int32, (length, length), 1)
    )
    before = jnp.dot(stacked, earlier, preferred_element_type=F32)
    number = jnp.dot(stacked, jnp.ones((length, 128), BF16), preferred_element_type=F32)
    size = chosen[0].shape[0]

    def cut(values):
        return [values[q * size : (q + 1) * size] for q in range(len(chosen))]

    return cut(before), cut(number)


def picked(mask, value):
    return jnp.sum(jnp.where(mask, value, 0.0), axis=0, keepdims=True)


def relay_kernel(cut, slabs, *refs):
    given, refs = refs[:6], refs[6:]
    tiles, slab_of, spots, send, sens, weight, device, cell, owner, slot, recv, place, spread, fetch, send_sem, recv_sem = refs
    count, fields, capacity = send.shape
    rows = sens.shape[1]
    _, _, width = tiles.shape
    groups = slab_of.shape[0]
    per_group = tiles.shape[0] // groups
    gx, gy = lax.axis_index("gx"), lax.axis_index("gy")
    size_x, size_y = lax.axis_size("gx"), lax.axis_size("gy")
    peer = peer_of(gx, gy, size_x, size_y)
    barrier = pltpu.get_barrier_semaphore()
    fetches = [
        pltpu.make_async_copy(source, target, fetch.at[i])
        for i, (source, target) in enumerate(zip(given, (sens, weight, device, cell, owner, slot)))
    ]
    for copy in fetches:
        copy.start()

    def greet(step, carry):
        pl.semaphore_signal(barrier, inc=1, device_id=peer(step), device_id_type=MESH)
        return carry

    lax.fori_loop(1, count, greet, 0)

    length = min(512, rows)
    chunks = rows // length
    spans = [slice(q * length, (q + 1) * length) for q in range(chunks)]
    for copy in fetches:
        copy.wait()
    to_x, to_y = split(device[...], size_y)
    to_y = to_y - gy
    to_y = jnp.where(to_y < 0, to_y + size_y, to_y)
    if size_x & (size_x - 1):
        to_x = to_x - gx
        to_x = jnp.where(to_x < 0, to_x + size_x, to_x)
    else:
        to_x = to_x ^ gx
    target = to_x * size_y + to_y
    chosen = [matches(count, target[:, span]) for span in spans]
    before, number = ordinals(chosen)
    total = running(number)
    for q, span in enumerate(spans):
        rank = picked(chosen[q], before[q] + total[q][:, :1]).astype(jnp.int32)
        place[:, span] = wide_one_hot(capacity, rank)

    senders = count // groups

    def copy(step, size):
        return pltpu.make_async_remote_copy(
            src_ref=send.at[pl.ds(step, size), pl.ds(0, SENT)],
            dst_ref=recv.at[pl.ds(step, size), pl.ds(0, SENT)],
            send_sem=send_sem.at[0],
            recv_sem=recv_sem.at[step // senders],
            device_id=peer(step),
            device_id_type=MESH,
        )

    def start(step, carry):
        copy(step, 1).start()
        return carry

    def packed(rows, low):
        size = 2 * len(rows)
        for span in spans:
            spread[: count * size, span] = fan(two_rows([read(span) for read in rows]), target[:, span], count)
        product = dot_nt(spread[: count * size], place[...])
        for t in range(count):
            send[t, low : low + len(rows)] = halves(product[t * size : (t + 1) * size])

    packed([lambda span, k=k: sens[k : k + 1, span] for k in range(3)] + [lambda span: cell[:, span].astype(F32)], 0)
    pl.semaphore_wait(barrier, count - 1)
    lax.fori_loop(1, count, start, 0)
    packed([lambda span: weight[:, span], lambda span: (owner[:, span] * BOX_DEV + slot[:, span]).astype(F32)], SENT)
    recv[0] = send[0]

    for group in range(groups):
        begin = max(1, group * senders)
        copy(begin, (group + 1) * senders - begin).wait_recv()
        sort_group(cut, slabs, [recv.at[group * senders + i] for i in range(senders)], tiles, group * per_group, per_group, slab_of, spots, group)

    copy(1, count - 1).wait_send()


def joined(arrived, low, high):
    join = max(1, min(len(arrived), 512 // arrived[0].shape[1]))
    return [
        jnp.concatenate([arrived[q + i][low:high] for i in range(join)], axis=1)
        for q in range(0, len(arrived), join)
    ]


def ordered(blocks, spots, per_group, width):
    size = 2 * blocks[0].shape[0]
    sums = jnp.zeros((per_group * size, width), F32)
    for block, spot in zip(blocks, spots):
        tile, lane = split(spot, width)
        spread = fan(jnp.concatenate(two_terms(block), axis=0), tile, per_group)
        sums = sums + dot_nt(spread, wide_one_hot(width, lane))
    return [halves(sums[t * size : (t + 1) * size]) for t in range(per_group)]


def sort_group(cut, slabs, arrived, tiles, first, per_group, slab_of, spots, group):
    width = tiles.shape[2]
    blocks = joined(arrived, 0, SENT)
    count = len(blocks)
    chosen = [matches(slabs, split(block[3:4].astype(jnp.int32), cut)[0]) for block in blocks]
    before, number = ordinals(chosen)
    total = running(number)
    lower = one_hot(
        lax.broadcasted_iota(jnp.int32, (slabs, slabs), 1)
        < lax.broadcasted_iota(jnp.int32, (slabs, slabs), 0)
    )
    tens = jnp.floor(total[-1] * 0.0625)
    start = 16.0 * jnp.dot(lower, tens.astype(BF16), preferred_element_type=F32)
    start = start + jnp.dot(lower, (total[-1] - 16.0 * tens).astype(BF16), preferred_element_type=F32)

    steps = per_group + slabs - 1
    row = lax.broadcasted_iota(jnp.int32, start.shape, 0).astype(F32)
    step = lax.broadcasted_iota(jnp.int32, start.shape, 1).astype(F32)
    entry = row + jnp.minimum(jnp.floor(start * (1.0 / width)), per_group - 1.0)
    slab = jnp.sum(jnp.where((row > 0) & (entry <= step), 1.0, 0.0), axis=0, keepdims=True)
    slab = jnp.where(step[:1] < steps, slab, slabs)
    inside = (row > 0) & (start < (step + 1.0) * width)
    final = step[:1] + jnp.sum(jnp.where(inside, 1.0, 0.0), axis=0, keepdims=True)
    leave = jnp.sum(jnp.where(row == step + 1.0, entry, 0.0), axis=0, keepdims=True)
    leave = jnp.where(step[:1] == slabs - 1, steps, leave) - 1.0
    table = jnp.concatenate([slab, final, leave, jnp.zeros((5, 128), F32)], axis=0)
    slab_of[group] = table.astype(jnp.int32)

    found = [
        picked(chosen[q], before[q] + (total[q] + start)[:, :1]).astype(jnp.int32) for q in range(count)
    ]
    for q in range(count):
        spots[group * count + q : group * count + q + 1] = found[q]
    for t, tile in enumerate(ordered(blocks, found, per_group, width)):
        tiles[first + t, :SENT] = tile


def relay_rows(devices, capacity, slabs, cut, sens, weight, device, cell, owner, slot):
    rows = devices * capacity
    size = min(4096, rows)
    width = min(256, size)
    groups = rows // size
    length = max(1, min(size // capacity, 512 // capacity)) * capacity
    return pl.pallas_call(
        functools.partial(relay_kernel, cut, slabs),
        out_shape=[
            pltpu.VMEM((rows // width, 8, width), F32),
            jax.ShapeDtypeStruct((groups, 8, 128), jnp.int32),
            pltpu.VMEM((rows // length, length), jnp.int32),
            pltpu.VMEM((devices, 8, capacity), F32),
        ],
        in_specs=[pl.BlockSpec(memory_space=pltpu.HBM)] * 6,
        out_specs=[pl.BlockSpec(memory_space=pltpu.VMEM)] * 4,
        scratch_shapes=[pltpu.VMEM(given.shape, given.dtype) for given in (sens, weight, device, cell, owner, slot)]
        + [
            pltpu.VMEM((devices, 8, capacity), F32),
            pltpu.VMEM((capacity, sens.shape[1]), BF16),
            pltpu.VMEM((devices * 2 * SENT, sens.shape[1]), BF16),
            pltpu.SemaphoreType.DMA((6,)),
            pltpu.SemaphoreType.DMA((1,)),
            pltpu.SemaphoreType.DMA((groups,)),
        ],
        compiler_params=pltpu.CompilerParams(collective_id=1, has_side_effects=True, vmem_limit_bytes=60 << 20),
        name="relay_rows",
    )(sens, weight, device, cell, owner, slot)


def located(tile, size_z):
    return split(tile[3:4].astype(jnp.int32), size_z)


def solve_kernel(slab_of, tiles, spots, parcels, stiff_in, anchor_in, coupling_in, adjoint, box, stiff, anchor, coupling, load, stage, late, marks, weighted, inverse, near, edge, halo, terms, found, flat, landed, fetch, late_send, late_recv, x_send, x_recv, y_send, y_recv, box_send, box_recv):
    parts, size_x, size_y, size_z = load.shape
    count, _, width = tiles.shape
    groups = slab_of.shape[0]
    per_group = count // groups
    steps = per_group + size_x
    half = parts * size_y
    exchanges = weighted.shape[0]
    gx, gy = lax.axis_index("gx"), lax.axis_index("gy")
    count_x, count_y = lax.axis_size("gx"), lax.axis_size("gy")
    devices = count_x * count_y
    peer = peer_of(gx, gy, count_x, count_y)
    sides = (("gx", gx, -1, gx > 0), ("gx", gx, 1, gx < count_x - 1), ("gy", gy, -1, gy > 0), ("gy", gy, 1, gy < count_y - 1))
    y_at = lax.broadcasted_iota(jnp.int32, (size_y, size_z), 0)
    z_at = lax.broadcasted_iota(jnp.int32, (size_y, size_z), 1)
    barrier = pltpu.get_barrier_semaphore()

    def greet(step, carry):
        pl.semaphore_signal(barrier, inc=1, device_id=peer(step), device_id_type=MESH)
        return carry

    lax.fori_loop(1, devices, greet, 0)
    fetches = [
        pltpu.make_async_copy(source, target, fetch.at[i])
        for i, (source, target) in enumerate(((stiff_in, stiff), (anchor_in, anchor), (coupling_in, coupling)))
    ]
    for copy in fetches:
        copy.start()

    for side, (axis, place, move, present) in enumerate(sides):

        @pl.when(jnp.logical_not(present))
        def _():
            for index in range(exchanges):
                if axis == "gx":
                    for k in range(parts):
                        weighted[index, k, 0 if move < 0 else size_x + 1] = jnp.zeros((size_y, size_z), F32)
                else:
                    halo[index, side % 2] = jnp.zeros(halo.shape[2:], F32)

    def transfers(index, sending, which=range(4)):
        made = []
        for side in which:
            axis, place, move, present = sides[side]
            there = 1 - side % 2
            landing = there if sending else side % 2
            if axis == "gx":
                into = size_x + 1 if (move < 0) == sending else 0
                pair = (weighted.at[index, :, 1 if move < 0 else size_x], weighted.at[index, :, into])
                sems = (x_send, x_recv)
            else:
                pair = (edge.at[index, side % 2], halo.at[index, landing])
                sems = (y_send, y_recv)
            made.append((present, pltpu.make_async_remote_copy(
                src_ref=pair[0],
                dst_ref=pair[1],
                send_sem=sems[0].at[index, side % 2],
                recv_sem=sems[1].at[index, landing],
                device_id={axis: place + move},
                device_id_type=MESH,
            )))
        return made

    def begin(index):
        for present, copy in transfers(index, True):

            @pl.when(present)
            def _():
                copy.start()

    def arrive(index, which):
        for present, copy in transfers(index, False, which):

            @pl.when(present)
            def _():
                copy.wait_recv()

    rims = (0, size_y - 1)

    def deposit(step, carry):
        made = []
        for group in range(groups):
            slab = slab_of[group, 0, step]
            tile = tiles[group * per_group + jnp.minimum(step - slab, per_group - 1)]
            xy, z = located(tile, size_z)
            pairs = [two_terms(tile[k : k + 1]) for k in range(parts)]
            values = [hi for hi, lo in pairs] + [lo for hi, lo in pairs]
            at_y = matches(size_y, xy - slab * size_y)
            spread = jnp.concatenate([scaled(at_y, value) for value in values], axis=0)
            product = dot_nt(spread, wide_one_hot(size_z, z))
            at = group * steps + step
            earlier = stage[jnp.maximum(at - 1, 0)]
            stage[at] = product[:half] + product[half:] + jnp.where(slab == carry[group], earlier, 0.0)
            made.append(slab)
        return tuple(made)

    late_rows = pl.ds(SENT, FIELDS - SENT)

    def follow(step, size):
        return pltpu.make_async_remote_copy(
            src_ref=parcels.at[pl.ds(step, size), late_rows],
            dst_ref=late.at[pl.ds(step, size), late_rows],
            send_sem=late_send.at[0],
            recv_sem=late_recv.at[0],
            device_id=peer(step),
            device_id_type=MESH,
        )

    def send_late(step, carry):
        follow(devices - step, 1).start()
        return carry

    def sort_late(group):
        senders = devices // groups
        blocks = joined([late.at[group * senders + i] for i in range(senders)], SENT, FIELDS)
        lines = [spots[q : q + 1] for q in range(group * len(blocks), (group + 1) * len(blocks))]
        for t, tile in enumerate(ordered(blocks, lines, per_group, width)):
            marks[group * per_group + t, : FIELDS - SENT] = tile

    stage[0] = jnp.zeros(stage.shape[1:], F32)
    slabs = lax.fori_loop(0, steps // 2, deposit, tuple(jnp.int32(-1) for _ in range(groups)), unroll=8)
    pl.semaphore_wait(barrier, devices - 1)
    lax.fori_loop(1, devices, send_late, 0)
    late[0] = parcels[0]
    lax.fori_loop(steps // 2, steps, deposit, slabs, unroll=8)
    for copy in fetches:
        copy.wait()

    def first(x, carry):
        stiffness = stiff[x]
        sums = stage[slab_of[0, 2, x]]
        for group in range(1, groups):
            sums = sums + stage[group * steps + slab_of[group, 2, x]]
        for side, rim in enumerate(rims):
            near[2, side, 0, pl.ds(x, 1), :] = stiffness[rim : rim + 1]
        for k in range(parts):
            inverted = 1.0 / (6.0 * stiffness + anchor[k, x] + coupling[4 * k, x])
            inverse[k, x] = inverted
            there = sums[k * size_y : (k + 1) * size_y]
            load[k, x] = there
            value = there * inverted
            adjoint[k, x] = value
            product = stiffness * value
            weighted[0, k, x + 1] = product
            for side, rim in enumerate(rims):
                near[1, side, k, pl.ds(x, 1), :] = inverted[rim : rim + 1]
                edge[0, side, k, pl.ds(x, 1), :] = product[rim : rim + 1]
        return carry

    lax.fori_loop(0, size_x, first, 0)
    begin(0)
    follow(1, devices - 1).wait_recv()

    for index in range(exchanges):
        last = index + 1 == exchanges
        for group in range(groups * index // exchanges, groups * (index + 1) // exchanges):
            sort_late(group)

        def update(x, carry):
            fields = [adjoint[k, x] for k in range(parts)]
            for k in range(parts):
                product = weighted[index, k, x + 1]
                value = load[k, x] + weighted[index, k, x] + weighted[index, k, x + 2]
                for j in range(parts):
                    if j != k:
                        value = value - coupling[3 * j + k, x] * fields[j]
                value = value + jnp.where(z_at == 0, 0.0, pltpu.roll(product, 1, 1))
                value = value + jnp.where(z_at == size_z - 1, 0.0, pltpu.roll(product, size_z - 1, 1))
                value = value + jnp.where(y_at == 0, 0.0, pltpu.roll(product, 1, 0))
                value = value + jnp.where(y_at == size_y - 1, 0.0, pltpu.roll(product, size_y - 1, 0))
                value = value * inverse[k, x]
                adjoint[k, x] = value
                for side, rim in enumerate(rims):
                    near[0, side, k, pl.ds(x, 1), :] = value[rim : rim + 1]
                if not last:
                    weighted[index + 1, k, x + 1] = stiff[x] * value
            return carry

        lax.fori_loop(1, size_x - 1, update, 0)
        arrive(index, (0, 1))
        update(0, 0)
        update(size_x - 1, 0)
        arrive(index, (2, 3))
        for side, rim in enumerate(rims):
            for k in range(parts):
                value = near[0, side, k] + halo[index, side, k] * near[1, side, k]
                for x in range(size_x):
                    adjoint[k, x, rim : rim + 1, :] = value[x : x + 1]
                if not last:
                    product = near[2, side, 0] * value
                    edge[index + 1, side, k] = product
                    for x in range(size_x):
                        weighted[index + 1, k, x + 1, rim : rim + 1, :] = product[x : x + 1]
        if not last:
            begin(index + 1)

    def cut(x, carry):
        for k in range(parts):
            hi, lo = two_terms(adjoint[k, x])
            terms[x, k * size_y : (k + 1) * size_y] = hi.astype(BF16)
            terms[x, half + k * size_y : half + (k + 1) * size_y] = lo.astype(BF16)
        return carry

    lax.fori_loop(0, size_x, cut, 0)

    def look(step, carry):
        made = []
        for group in range(groups):
            held, before = carry[group]
            slab = slab_of[group, 0, step]
            tile = tiles[group * per_group + jnp.minimum(step - slab, per_group - 1)]
            xy, z = located(tile, size_z)
            at_y = matches(size_y, xy - slab * size_y)
            columns = jnp.dot(terms[jnp.minimum(slab, size_x - 1)], wide_one_hot(size_z, z), preferred_element_type=F32)
            columns = columns[:half] + columns[half:]
            value = jnp.concatenate(
                [picked(at_y, columns[k * size_y : (k + 1) * size_y]) for k in range(parts)], axis=0
            )
            held = value + jnp.where(slab == before, 0.0, held)
            found[group * steps + step, :parts] = held
            made.append((held, slab))
        return tuple(made)

    lax.fori_loop(
        0, steps, look, tuple((jnp.zeros((parts, width), F32), jnp.int32(0)) for _ in range(groups)), unroll=4
    )
    total = jnp.zeros((2 * parts * devices, BOX_DEV), F32)
    join = min(8, count)
    for begin_at in range(0, count, join):
        numbers = range(begin_at, begin_at + join)

        def line(field):
            return jnp.concatenate([marks[t, field : field + 1] for t in numbers], axis=1)

        owner, slot = split(line(1).astype(jnp.int32), BOX_DEV)
        rows = jnp.concatenate(
            [found[t // per_group * steps + slab_of[t // per_group, 1, t % per_group]][:parts] for t in numbers], axis=1
        ) * line(0)
        at_owner = matches(devices, owner)
        pairs = [two_terms(rows[k : k + 1]) for k in range(parts)]
        values = [hi for hi, lo in pairs] + [lo for hi, lo in pairs]
        spread = jnp.concatenate([scaled(at_owner, value) for value in values], axis=0)
        total = total + dot_nt(spread, wide_one_hot(BOX_DEV, slot))
    for k in range(parts):
        part = total[k * devices : (k + 1) * devices] + total[(parts + k) * devices : (parts + k + 1) * devices]
        flat[k] = jnp.concatenate([part, jnp.zeros_like(part)], axis=1)

    def parcel(step, first, size):
        there = peer(step)
        return pltpu.make_async_remote_copy(
            src_ref=flat.at[:, pl.ds(first, size)],
            dst_ref=landed.at[:, pl.ds(step, size)],
            send_sem=box_send.at[0],
            recv_sem=box_recv.at[0],
            device_id=there,
            device_id_type=MESH,
        )

    def post(step, carry):
        there = peer(devices - step)
        parcel(devices - step, there[0] * count_y + there[1], 1).start()
        return carry

    lax.fori_loop(1, devices, post, 0)
    landed[:, 0:1] = flat[:, pl.ds(gx * count_y + gy, 1)]

    parcel(1, 1, devices - 1).wait_recv()
    for k in range(parts):
        box[k : k + 1] = jnp.sum(landed[k], axis=0, keepdims=True)[:, :BOX_DEV]

    parcel(1, 1, devices - 1).wait_send()
    follow(1, devices - 1).wait_send()
    for index in range(exchanges):
        for present, copy in transfers(index, True):

            @pl.when(present)
            def _():
                copy.wait_send()


def solve_rows(devices, tiles, slab_of, spots, parcels, stiffness, anchor, coupling):
    size_x, size_y, size_z = stiffness.shape
    parts = anchor.shape[0]
    exchanges = SWEEPS - 1
    count, fields, width = tiles.shape
    groups = slab_of.shape[0]
    steps = count // groups + size_x
    kept_near = [pltpu.with_memory_space_constraint(value, pltpu.VMEM) for value in (tiles, spots, parcels)]
    return pl.pallas_call(
        solve_kernel,
        out_shape=[pltpu.VMEM(anchor.shape, F32), pltpu.VMEM((parts, BOX_DEV), F32)],
        in_specs=[pl.BlockSpec(memory_space=pltpu.SMEM)]
        + [pl.BlockSpec(memory_space=pltpu.VMEM)] * 3
        + [pl.BlockSpec(memory_space=pltpu.HBM)] * 3,
        out_specs=[pl.BlockSpec(memory_space=pltpu.VMEM)] * 2,
        scratch_shapes=[
            pltpu.VMEM(stiffness.shape, F32),
            pltpu.VMEM(anchor.shape, F32),
            pltpu.VMEM(coupling.shape, F32),
            pltpu.VMEM(anchor.shape, F32),
            pltpu.VMEM((groups * steps, parts * size_y, size_z), F32),
            pltpu.VMEM(parcels.shape, F32),
            pltpu.VMEM(tiles.shape, F32),
            pltpu.VMEM((exchanges, parts, size_x + 2, size_y, size_z), F32),
            pltpu.VMEM(anchor.shape, F32),
            pltpu.VMEM((3, 2, parts, size_x, size_z), F32),
            pltpu.VMEM((exchanges, 2, parts, size_x, size_z), F32),
            pltpu.VMEM((exchanges, 2, parts, size_x, size_z), F32),
            pltpu.VMEM((size_x, 2 * parts * size_y, size_z), BF16),
            pltpu.VMEM((groups * steps, fields, width), F32),
            pltpu.VMEM((parts, devices, 2 * BOX_DEV), F32),
            pltpu.VMEM((parts, devices, 2 * BOX_DEV), F32),
            pltpu.SemaphoreType.DMA((3,)),
        ]
        + [pltpu.SemaphoreType.DMA((1,))] * 2
        + [pltpu.SemaphoreType.DMA((exchanges, 2))] * 4
        + [pltpu.SemaphoreType.DMA((1,))] * 2,
        compiler_params=pltpu.CompilerParams(collective_id=0, has_side_effects=True, vmem_limit_bytes=56 << 20),
        name="solve_rows",
    )(slab_of, *kept_near, stiffness, anchor, coupling)


def hand_kernel(adjoint, box, adjoint_out, box_out, sem):
    copies = [
        pltpu.make_async_copy(adjoint, adjoint_out, sem.at[0]),
        pltpu.make_async_copy(box, box_out, sem.at[1]),
    ]
    for copy in copies:
        copy.start()
    for copy in copies:
        copy.wait()


def hand_over(adjoint, box):
    values = [pltpu.with_memory_space_constraint(value, pltpu.VMEM) for value in (adjoint, box)]
    return pl.pallas_call(
        hand_kernel,
        out_shape=[jax.ShapeDtypeStruct(value.shape, F32) for value in values],
        in_specs=[pl.BlockSpec(memory_space=pltpu.VMEM)] * 2,
        out_specs=[pl.BlockSpec(memory_space=pltpu.HBM)] * 2,
        scratch_shapes=[pltpu.SemaphoreType.DMA((2,))],
        name="hand_over",
    )(*values)


def body(
    sensitivity,
    node_weight,
    dest_device,
    dest_cell,
    box_owner,
    box_slot,
    stiffness,
    anchor,
    coupling,
):
    devices = lax.axis_size("gx") * lax.axis_size("gy")
    row_count = sensitivity.shape[1]
    capacity = 2 * row_count // devices
    size_x, size_y, size_z = stiffness.shape
    size_xy = size_x * size_y
    assert size_xy * size_z <= 2**17 and devices * BOX_DEV <= 2**17

    def row(values):
        return values.reshape(1, row_count)

    tiles, slab_of, spots, parcels = relay_rows(
        devices,
        capacity,
        size_x,
        size_y * size_z,
        sensitivity,
        row(node_weight),
        row(dest_device),
        row(dest_cell),
        row(box_owner),
        row(box_slot),
    )
    adjoint, box_gradient = hand_over(*solve_rows(devices, tiles, slab_of, spots, parcels, stiffness, anchor, coupling))
    return (adjoint, box_gradient)


def solution(mesh):
    placed = (
        P(None, ("gx", "gy")),
        P(("gx", "gy")),
        P(("gx", "gy"), None),
        P(("gx", "gy")),
        P(("gx", "gy"), None),
        P(("gx", "gy")),
        P("gx", "gy", None),
        P(None, "gx", "gy", None),
        P(None, "gx", "gy", None),
    )
    return jax.shard_map(
        body,
        mesh=mesh,
        in_specs=placed,
        out_specs=(P(None, "gx", "gy", None), P(None, ("gx", "gy"))),
        check_vma=False,
    )
```

```python
import functools

import jax
import jax.numpy as jnp
from jax import lax
from jax.experimental import pallas as pl
from jax.experimental.pallas import tpu as pltpu
from jax.sharding import PartitionSpec as P

BOX_DEV = 64
SWEEPS = 4
SENT = 4
FIELDS = 6
NT = (((1,), (1,)), ((), ()))
F32 = jnp.float32
BF16 = jnp.bfloat16
MESH = pl.DeviceIdType.MESH


def two_terms(x):
    hi = x.astype(BF16).astype(F32)
    return hi, x - hi


def matches(count, row):
    return lax.broadcasted_iota(jnp.int32, (count, row.shape[1]), 0) == row


def one_hot(mask):
    return jnp.where(mask, 1.0, 0.0).astype(BF16)


def scaled(mask, row):
    return jnp.where(mask, row, 0.0).astype(BF16)


def dot_nt(a, b):
    return lax.dot_general(a, b, NT, preferred_element_type=F32)


def split(value, size):
    if size & (size - 1) == 0:
        return value >> (size.bit_length() - 1), value & (size - 1)
    return value // size, value % size


def wide_matches(count, row):
    return lax.broadcasted_iota(jnp.int16, (count, row.shape[1]), 0) == row.astype(jnp.int16)


def wide_one_hot(count, row):
    return jnp.where(wide_matches(count, row), jnp.array(1, BF16), jnp.array(0, BF16))


def kept(mask, values):
    return jnp.where(mask, values, jnp.array(0, BF16))


def fan(values, index, count):
    size, length = values.shape
    many = min(count, max(1, 16 // size))
    terms = jnp.concatenate([values] * many, axis=0).astype(BF16)
    part = lax.broadcasted_iota(jnp.int32, terms.shape, 0) // size
    index = (jnp.broadcast_to(index, terms.shape) - part).astype(jnp.int16)
    return jnp.concatenate([kept(index == t, terms) for t in range(0, count, many)], axis=0)


def two_rows(rows):
    return jnp.concatenate(two_terms(jnp.concatenate(rows, axis=0)), axis=0)


def halves(values):
    size = values.shape[0] // 2
    return values[:size] + values[size:]


def folded(a, b, size):
    if size & (size - 1):
        return (a + b) % size
    total, bit = 0, 1
    while bit < size:
        total = total + bit * ((a // bit + b // bit) % 2)
        bit = 2 * bit
    return total


def peers_of(gx, gy, size_x, size_y):
    along = [(gy + step) % size_y for step in range(size_y)]
    return [(across, there) for across in [folded(gx, step, size_x) for step in range(size_x)] for there in along]


def running(numbers):
    totals = [jnp.zeros_like(numbers[0])]
    for number in numbers:
        totals.append(totals[-1] + number)
    return totals


def ordinals(chosen):
    length = chosen[0].shape[1]
    stacked = one_hot(jnp.concatenate(chosen, axis=0))
    earlier = one_hot(
        lax.broadcasted_iota(jnp.int32, (length, length), 0)
        < lax.broadcasted_iota(jnp.int32, (length, length), 1)
    )
    before = jnp.dot(stacked, earlier, preferred_element_type=F32)
    number = jnp.dot(stacked, jnp.ones((length, 128), BF16), preferred_element_type=F32)
    size = chosen[0].shape[0]

    def cut(values):
        return [values[q * size : (q + 1) * size] for q in range(len(chosen))]

    return cut(before), cut(number)


def picked(mask, value):
    return jnp.sum(jnp.where(mask, value, 0.0), axis=0, keepdims=True)


def relay_kernel(cut, slabs, *refs):
    given, refs = refs[:6], refs[6:]
    tiles, slab_of, spots, send, sens, weight, device, cell, owner, slot, recv, place, spread, fetch, send_sem, recv_sem = refs
    count, fields, capacity = send.shape
    rows = sens.shape[1]
    _, _, width = tiles.shape
    groups = slab_of.shape[0]
    per_group = tiles.shape[0] // groups
    gx, gy = lax.axis_index("gx"), lax.axis_index("gy")
    size_x, size_y = lax.axis_size("gx"), lax.axis_size("gy")
    peers = peers_of(gx, gy, size_x, size_y)
    barrier = pltpu.get_barrier_semaphore()
    fetches = [
        pltpu.make_async_copy(source, target, fetch.at[i])
        for i, (source, target) in enumerate(zip(given, (sens, weight, device, cell, owner, slot)))
    ]
    for copy in fetches:
        copy.start()

    for peer in peers[1:]:
        pl.semaphore_signal(barrier, inc=1, device_id=peer, device_id_type=MESH)

    length = min(512, rows)
    chunks = rows // length
    spans = [slice(q * length, (q + 1) * length) for q in range(chunks)]
    for copy in fetches:
        copy.wait()
    to_x, to_y = split(device[...], size_y)
    to_y = to_y - gy
    to_y = jnp.where(to_y < 0, to_y + size_y, to_y)
    if size_x & (size_x - 1):
        to_x = to_x - gx
        to_x = jnp.where(to_x < 0, to_x + size_x, to_x)
    else:
        to_x = to_x ^ gx
    target = to_x * size_y + to_y
    chosen = [matches(count, target[:, span]) for span in spans]
    before, number = ordinals(chosen)
    total = running(number)
    for q, span in enumerate(spans):
        rank = picked(chosen[q], before[q] + total[q][:, :1]).astype(jnp.int32)
        place[:, span] = wide_one_hot(capacity, rank)

    senders = count // groups

    def copy(step, size):
        return pltpu.make_async_remote_copy(
            src_ref=send.at[pl.ds(step, size), pl.ds(0, SENT)],
            dst_ref=recv.at[pl.ds(step, size), pl.ds(0, SENT)],
            send_sem=send_sem.at[0],
            recv_sem=recv_sem.at[step // senders],
            device_id=peers[step],
            device_id_type=MESH,
        )

    def packed(rows, low):
        size = 2 * len(rows)
        for span in spans:
            spread[: count * size, span] = fan(two_rows([read(span) for read in rows]), target[:, span], count)
        product = dot_nt(spread[: count * size], place[...])
        for t in range(count):
            send[t, low : low + len(rows)] = halves(product[t * size : (t + 1) * size])

    packed([lambda span, k=k: sens[k : k + 1, span] for k in range(3)] + [lambda span: cell[:, span].astype(F32)], 0)
    pl.semaphore_wait(barrier, count - 1)
    for step in range(1, count):
        copy(step, 1).start()
    packed([lambda span: weight[:, span], lambda span: (owner[:, span] * BOX_DEV + slot[:, span]).astype(F32)], SENT)
    recv[0] = send[0]

    for group in range(groups):
        begin = max(1, group * senders)
        copy(begin, (group + 1) * senders - begin).wait_recv()
        sort_group(cut, slabs, [recv.at[group * senders + i] for i in range(senders)], tiles, group * per_group, per_group, slab_of, spots, group)

    copy(1, count - 1).wait_send()


def joined(arrived, low, high):
    join = max(1, min(len(arrived), 512 // arrived[0].shape[1]))
    return [
        jnp.concatenate([arrived[q + i][low:high] for i in range(join)], axis=1)
        for q in range(0, len(arrived), join)
    ]


def ordered(blocks, spots, per_group, width):
    size = 2 * blocks[0].shape[0]
    sums = jnp.zeros((per_group * size, width), F32)
    for block, spot in zip(blocks, spots):
        tile, lane = split(spot, width)
        spread = fan(jnp.concatenate(two_terms(block), axis=0), tile, per_group)
        sums = sums + dot_nt(spread, wide_one_hot(width, lane))
    return [halves(sums[t * size : (t + 1) * size]) for t in range(per_group)]


def sort_group(cut, slabs, arrived, tiles, first, per_group, slab_of, spots, group):
    width = tiles.shape[2]
    blocks = joined(arrived, 0, SENT)
    count = len(blocks)
    chosen = [matches(slabs, split(block[3:4].astype(jnp.int32), cut)[0]) for block in blocks]
    before, number = ordinals(chosen)
    total = running(number)
    lower = one_hot(
        lax.broadcasted_iota(jnp.int32, (slabs, slabs), 1)
        < lax.broadcasted_iota(jnp.int32, (slabs, slabs), 0)
    )
    tens = jnp.floor(total[-1] * 0.0625)
    start = 16.0 * jnp.dot(lower, tens.astype(BF16), preferred_element_type=F32)
    start = start + jnp.dot(lower, (total[-1] - 16.0 * tens).astype(BF16), preferred_element_type=F32)

    steps = per_group + slabs - 1
    row = lax.broadcasted_iota(jnp.int32, start.shape, 0).astype(F32)
    step = lax.broadcasted_iota(jnp.int32, start.shape, 1).astype(F32)
    entry = row + jnp.minimum(jnp.floor(start * (1.0 / width)), per_group - 1.0)
    slab = jnp.sum(jnp.where((row > 0) & (entry <= step), 1.0, 0.0), axis=0, keepdims=True)
    slab = jnp.where(step[:1] < steps, slab, slabs)
    inside = (row > 0) & (start < (step + 1.0) * width)
    final = step[:1] + jnp.sum(jnp.where(inside, 1.0, 0.0), axis=0, keepdims=True)
    leave = jnp.sum(jnp.where(row == step + 1.0, entry, 0.0), axis=0, keepdims=True)
    leave = jnp.where(step[:1] == slabs - 1, steps, leave) - 1.0
    table = jnp.concatenate([slab, final, leave, jnp.zeros((5, 128), F32)], axis=0)
    slab_of[group] = table.astype(jnp.int32)

    found = [
        picked(chosen[q], before[q] + (total[q] + start)[:, :1]).astype(jnp.int32) for q in range(count)
    ]
    for q in range(count):
        spots[group * count + q : group * count + q + 1] = found[q]
    for t, tile in enumerate(ordered(blocks, found, per_group, width)):
        tiles[first + t, :SENT] = tile


def relay_rows(devices, capacity, slabs, cut, sens, weight, device, cell, owner, slot):
    rows = devices * capacity
    size = min(4096, rows)
    width = min(256, size)
    groups = rows // size
    length = max(1, min(size // capacity, 512 // capacity)) * capacity
    return pl.pallas_call(
        functools.partial(relay_kernel, cut, slabs),
        out_shape=[
            pltpu.VMEM((rows // width, 8, width), F32),
            jax.ShapeDtypeStruct((groups, 8, 128), jnp.int32),
            pltpu.VMEM((rows // length, length), jnp.int32),
            pltpu.VMEM((devices, 8, capacity), F32),
        ],
        in_specs=[pl.BlockSpec(memory_space=pltpu.HBM)] * 6,
        out_specs=[pl.BlockSpec(memory_space=pltpu.VMEM)] * 4,
        scratch_shapes=[pltpu.VMEM(given.shape, given.dtype) for given in (sens, weight, device, cell, owner, slot)]
        + [
            pltpu.VMEM((devices, 8, capacity), F32),
            pltpu.VMEM((capacity, sens.shape[1]), BF16),
            pltpu.VMEM((devices * 2 * SENT, sens.shape[1]), BF16),
            pltpu.SemaphoreType.DMA((6,)),
            pltpu.SemaphoreType.DMA((1,)),
            pltpu.SemaphoreType.DMA((groups,)),
        ],
        compiler_params=pltpu.CompilerParams(collective_id=1, has_side_effects=True, vmem_limit_bytes=60 << 20),
        name="relay_rows",
    )(sens, weight, device, cell, owner, slot)


def located(tile, size_z):
    return split(tile[3:4].astype(jnp.int32), size_z)


def solve_kernel(slab_of, tiles, spots, parcels, stiff_in, anchor_in, coupling_in, adjoint, box, stiff, anchor, coupling, load, stage, late, marks, weighted, inverse, near, edge, halo, terms, found, flat, landed, fetch, late_send, late_recv, x_send, x_recv, y_send, y_recv, box_send, box_recv):
    parts, size_x, size_y, size_z = load.shape
    count, _, width = tiles.shape
    groups = slab_of.shape[0]
    per_group = count // groups
    steps = per_group + size_x
    half = parts * size_y
    exchanges = weighted.shape[0]
    gx, gy = lax.axis_index("gx"), lax.axis_index("gy")
    count_x, count_y = lax.axis_size("gx"), lax.axis_size("gy")
    devices = count_x * count_y
    peers = peers_of(gx, gy, count_x, count_y)
    sides = (("gx", gx, -1, gx > 0), ("gx", gx, 1, gx < count_x - 1), ("gy", gy, -1, gy > 0), ("gy", gy, 1, gy < count_y - 1))
    y_at = lax.broadcasted_iota(jnp.int32, (size_y, size_z), 0)
    z_at = lax.broadcasted_iota(jnp.int32, (size_y, size_z), 1)
    barrier = pltpu.get_barrier_semaphore()

    for peer in peers[1:]:
        pl.semaphore_signal(barrier, inc=1, device_id=peer, device_id_type=MESH)
    fetches = [
        pltpu.make_async_copy(source, target, fetch.at[i])
        for i, (source, target) in enumerate(((stiff_in, stiff), (anchor_in, anchor), (coupling_in, coupling)))
    ]
    for copy in fetches:
        copy.start()

    for side, (axis, place, move, present) in enumerate(sides):

        @pl.when(jnp.logical_not(present))
        def _():
            for index in range(exchanges):
                if axis == "gx":
                    for k in range(parts):
                        weighted[index, k, 0 if move < 0 else size_x + 1] = jnp.zeros((size_y, size_z), F32)
                else:
                    halo[index, side % 2] = jnp.zeros(halo.shape[2:], F32)

    def transfers(index, sending, which=range(4)):
        made = []
        for side in which:
            axis, place, move, present = sides[side]
            there = 1 - side % 2
            landing = there if sending else side % 2
            if axis == "gx":
                into = size_x + 1 if (move < 0) == sending else 0
                pair = (weighted.at[index, :, 1 if move < 0 else size_x], weighted.at[index, :, into])
                sems = (x_send, x_recv)
            else:
                pair = (edge.at[index, side % 2], halo.at[index, landing])
                sems = (y_send, y_recv)
            made.append((present, pltpu.make_async_remote_copy(
                src_ref=pair[0],
                dst_ref=pair[1],
                send_sem=sems[0].at[index, side % 2],
                recv_sem=sems[1].at[index, landing],
                device_id={axis: place + move},
                device_id_type=MESH,
            )))
        return made

    def begin(index):
        for present, copy in transfers(index, True):

            @pl.when(present)
            def _():
                copy.start()

    def arrive(index, which):
        for present, copy in transfers(index, False, which):

            @pl.when(present)
            def _():
                copy.wait_recv()

    rims = (0, size_y - 1)

    def deposit(step, carry):
        made = []
        for group in range(groups):
            slab = slab_of[group, 0, step]
            tile = tiles[group * per_group + jnp.minimum(step - slab, per_group - 1)]
            xy, z = located(tile, size_z)
            pairs = [two_terms(tile[k : k + 1]) for k in range(parts)]
            values = [hi for hi, lo in pairs] + [lo for hi, lo in pairs]
            at_y = matches(size_y, xy - slab * size_y)
            spread = jnp.concatenate([scaled(at_y, value) for value in values], axis=0)
            product = dot_nt(spread, wide_one_hot(size_z, z))
            at = group * steps + step
            earlier = stage[jnp.maximum(at - 1, 0)]
            stage[at] = product[:half] + product[half:] + jnp.where(slab == carry[group], earlier, 0.0)
            made.append(slab)
        return tuple(made)

    late_rows = pl.ds(SENT, FIELDS - SENT)

    def follow(step, size):
        return pltpu.make_async_remote_copy(
            src_ref=parcels.at[pl.ds(step, size), late_rows],
            dst_ref=late.at[pl.ds(step, size), late_rows],
            send_sem=late_send.at[0],
            recv_sem=late_recv.at[0],
            device_id=peers[step],
            device_id_type=MESH,
        )

    def sort_late(group):
        senders = devices // groups
        blocks = joined([late.at[group * senders + i] for i in range(senders)], SENT, FIELDS)
        lines = [spots[q : q + 1] for q in range(group * len(blocks), (group + 1) * len(blocks))]
        for t, tile in enumerate(ordered(blocks, lines, per_group, width)):
            marks[group * per_group + t, : FIELDS - SENT] = tile

    stage[0] = jnp.zeros(stage.shape[1:], F32)
    slabs = lax.fori_loop(0, steps // 2, deposit, tuple(jnp.int32(-1) for _ in range(groups)), unroll=8)
    pl.semaphore_wait(barrier, devices - 1)
    for step in reversed(range(1, devices)):
        follow(step, 1).start()
    late[0] = parcels[0]
    lax.fori_loop(steps // 2, steps, deposit, slabs, unroll=8)
    for copy in fetches:
        copy.wait()

    def first(x, carry):
        stiffness = stiff[x]
        sums = stage[slab_of[0, 2, x]]
        for group in range(1, groups):
            sums = sums + stage[group * steps + slab_of[group, 2, x]]
        for side, rim in enumerate(rims):
            near[2, side, 0, pl.ds(x, 1), :] = stiffness[rim : rim + 1]
        for k in range(parts):
            inverted = 1.0 / (6.0 * stiffness + anchor[k, x] + coupling[4 * k, x])
            inverse[k, x] = inverted
            there = sums[k * size_y : (k + 1) * size_y]
            load[k, x] = there
            value = there * inverted
            adjoint[k, x] = value
            product = stiffness * value
            weighted[0, k, x + 1] = product
            for side, rim in enumerate(rims):
                near[1, side, k, pl.ds(x, 1), :] = inverted[rim : rim + 1]
                edge[0, side, k, pl.ds(x, 1), :] = product[rim : rim + 1]
        return carry

    lax.fori_loop(0, size_x, first, 0)
    begin(0)
    follow(1, devices - 1).wait_recv()

    for index in range(exchanges):
        last = index + 1 == exchanges
        for group in range(groups * index // exchanges, groups * (index + 1) // exchanges):
            sort_late(group)

        def update(x, carry):
            fields = [adjoint[k, x] for k in range(parts)]
            for k in range(parts):
                product = weighted[index, k, x + 1]
                value = load[k, x] + weighted[index, k, x] + weighted[index, k, x + 2]
                for j in range(parts):
                    if j != k:
                        value = value - coupling[3 * j + k, x] * fields[j]
                value = value + jnp.where(z_at == 0, 0.0, pltpu.roll(product, 1, 1))
                value = value + jnp.where(z_at == size_z - 1, 0.0, pltpu.roll(product, size_z - 1, 1))
                value = value + jnp.where(y_at == 0, 0.0, pltpu.roll(product, 1, 0))
                value = value + jnp.where(y_at == size_y - 1, 0.0, pltpu.roll(product, size_y - 1, 0))
                value = value * inverse[k, x]
                adjoint[k, x] = value
                for side, rim in enumerate(rims):
                    near[0, side, k, pl.ds(x, 1), :] = value[rim : rim + 1]
                if not last:
                    weighted[index + 1, k, x + 1] = stiff[x] * value
            return carry

        lax.fori_loop(1, size_x - 1, update, 0)
        arrive(index, (0, 1))
        update(0, 0)
        update(size_x - 1, 0)
        arrive(index, (2, 3))
        for side, rim in enumerate(rims):
            for k in range(parts):
                value = near[0, side, k] + halo[index, side, k] * near[1, side, k]
                for x in range(size_x):
                    adjoint[k, x, rim : rim + 1, :] = value[x : x + 1]
                if not last:
                    product = near[2, side, 0] * value
                    edge[index + 1, side, k] = product
                    for x in range(size_x):
                        weighted[index + 1, k, x + 1, rim : rim + 1, :] = product[x : x + 1]
        if not last:
            begin(index + 1)

    def cut(x, carry):
        for k in range(parts):
            hi, lo = two_terms(adjoint[k, x])
            terms[x, k * size_y : (k + 1) * size_y] = hi.astype(BF16)
            terms[x, half + k * size_y : half + (k + 1) * size_y] = lo.astype(BF16)
        return carry

    lax.fori_loop(0, size_x, cut, 0)

    def look(step, carry):
        made = []
        for group in range(groups):
            held, before = carry[group]
            slab = slab_of[group, 0, step]
            tile = tiles[group * per_group + jnp.minimum(step - slab, per_group - 1)]
            xy, z = located(tile, size_z)
            at_y = matches(size_y, xy - slab * size_y)
            columns = jnp.dot(terms[jnp.minimum(slab, size_x - 1)], wide_one_hot(size_z, z), preferred_element_type=F32)
            columns = columns[:half] + columns[half:]
            value = jnp.concatenate(
                [picked(at_y, columns[k * size_y : (k + 1) * size_y]) for k in range(parts)], axis=0
            )
            held = value + jnp.where(slab == before, 0.0, held)
            found[group * steps + step, :parts] = held
            made.append((held, slab))
        return tuple(made)

    lax.fori_loop(
        0, steps, look, tuple((jnp.zeros((parts, width), F32), jnp.int32(0)) for _ in range(groups)), unroll=4
    )
    total = jnp.zeros((2 * parts * devices, BOX_DEV), F32)
    join = min(8, count)
    for begin_at in range(0, count, join):
        numbers = range(begin_at, begin_at + join)

        def line(field):
            return jnp.concatenate([marks[t, field : field + 1] for t in numbers], axis=1)

        owner, slot = split(line(1).astype(jnp.int32), BOX_DEV)
        rows = jnp.concatenate(
            [found[t // per_group * steps + slab_of[t // per_group, 1, t % per_group]][:parts] for t in numbers], axis=1
        ) * line(0)
        at_owner = matches(devices, owner)
        pairs = [two_terms(rows[k : k + 1]) for k in range(parts)]
        values = [hi for hi, lo in pairs] + [lo for hi, lo in pairs]
        spread = jnp.concatenate([scaled(at_owner, value) for value in values], axis=0)
        total = total + dot_nt(spread, wide_one_hot(BOX_DEV, slot))
    for k in range(parts):
        part = total[k * devices : (k + 1) * devices] + total[(parts + k) * devices : (parts + k + 1) * devices]
        flat[k] = jnp.concatenate([part, jnp.zeros_like(part)], axis=1)

    def parcel(step, first, size):
        return pltpu.make_async_remote_copy(
            src_ref=flat.at[:, pl.ds(first, size)],
            dst_ref=landed.at[:, pl.ds(step, size)],
            send_sem=box_send.at[0],
            recv_sem=box_recv.at[0],
            device_id=peers[step],
            device_id_type=MESH,
        )

    for step in reversed(range(1, devices)):
        there = peers[step]
        parcel(step, there[0] * count_y + there[1], 1).start()
    landed[:, 0:1] = flat[:, pl.ds(gx * count_y + gy, 1)]

    parcel(1, 1, devices - 1).wait_recv()
    for k in range(parts):
        box[k : k + 1] = jnp.sum(landed[k], axis=0, keepdims=True)[:, :BOX_DEV]

    parcel(1, 1, devices - 1).wait_send()
    follow(1, devices - 1).wait_send()
    for index in range(exchanges):
        for present, copy in transfers(index, True):

            @pl.when(present)
            def _():
                copy.wait_send()


def solve_rows(devices, tiles, slab_of, spots, parcels, stiffness, anchor, coupling):
    size_x, size_y, size_z = stiffness.shape
    parts = anchor.shape[0]
    exchanges = SWEEPS - 1
    count, fields, width = tiles.shape
    groups = slab_of.shape[0]
    steps = count // groups + size_x
    kept_near = [pltpu.with_memory_space_constraint(value, pltpu.VMEM) for value in (tiles, spots, parcels)]
    return pl.pallas_call(
        solve_kernel,
        out_shape=[pltpu.VMEM(anchor.shape, F32), pltpu.VMEM((parts, BOX_DEV), F32)],
        in_specs=[pl.BlockSpec(memory_space=pltpu.SMEM)]
        + [pl.BlockSpec(memory_space=pltpu.VMEM)] * 3
        + [pl.BlockSpec(memory_space=pltpu.HBM)] * 3,
        out_specs=[pl.BlockSpec(memory_space=pltpu.VMEM)] * 2,
        scratch_shapes=[
            pltpu.VMEM(stiffness.shape, F32),
            pltpu.VMEM(anchor.shape, F32),
            pltpu.VMEM(coupling.shape, F32),
            pltpu.VMEM(anchor.shape, F32),
            pltpu.VMEM((groups * steps, parts * size_y, size_z), F32),
            pltpu.VMEM(parcels.shape, F32),
            pltpu.VMEM(tiles.shape, F32),
            pltpu.VMEM((exchanges, parts, size_x + 2, size_y, size_z), F32),
            pltpu.VMEM(anchor.shape, F32),
            pltpu.VMEM((3, 2, parts, size_x, size_z), F32),
            pltpu.VMEM((exchanges, 2, parts, size_x, size_z), F32),
            pltpu.VMEM((exchanges, 2, parts, size_x, size_z), F32),
            pltpu.VMEM((size_x, 2 * parts * size_y, size_z), BF16),
            pltpu.VMEM((groups * steps, fields, width), F32),
            pltpu.VMEM((parts, devices, 2 * BOX_DEV), F32),
            pltpu.VMEM((parts, devices, 2 * BOX_DEV), F32),
            pltpu.SemaphoreType.DMA((3,)),
        ]
        + [pltpu.SemaphoreType.DMA((1,))] * 2
        + [pltpu.SemaphoreType.DMA((exchanges, 2))] * 4
        + [pltpu.SemaphoreType.DMA((1,))] * 2,
        compiler_params=pltpu.CompilerParams(collective_id=0, has_side_effects=True, vmem_limit_bytes=56 << 20),
        name="solve_rows",
    )(slab_of, *kept_near, stiffness, anchor, coupling)


def hand_kernel(adjoint, box, adjoint_out, box_out, sem):
    copies = [
        pltpu.make_async_copy(adjoint, adjoint_out, sem.at[0]),
        pltpu.make_async_copy(box, box_out, sem.at[1]),
    ]
    for copy in copies:
        copy.start()
    for copy in copies:
        copy.wait()


def hand_over(adjoint, box):
    values = [pltpu.with_memory_space_constraint(value, pltpu.VMEM) for value in (adjoint, box)]
    return pl.pallas_call(
        hand_kernel,
        out_shape=[jax.ShapeDtypeStruct(value.shape, F32) for value in values],
        in_specs=[pl.BlockSpec(memory_space=pltpu.VMEM)] * 2,
        out_specs=[pl.BlockSpec(memory_space=pltpu.HBM)] * 2,
        scratch_shapes=[pltpu.SemaphoreType.DMA((2,))],
        name="hand_over",
    )(*values)


def body(
    sensitivity,
    node_weight,
    dest_device,
    dest_cell,
    box_owner,
    box_slot,
    stiffness,
    anchor,
    coupling,
):
    devices = lax.axis_size("gx") * lax.axis_size("gy")
    row_count = sensitivity.shape[1]
    capacity = 2 * row_count // devices
    size_x, size_y, size_z = stiffness.shape
    size_xy = size_x * size_y
    assert size_xy * size_z <= 2**17 and devices * BOX_DEV <= 2**17

    def row(values):
        return values.reshape(1, row_count)

    tiles, slab_of, spots, parcels = relay_rows(
        devices,
        capacity,
        size_x,
        size_y * size_z,
        sensitivity,
        row(node_weight),
        row(dest_device),
        row(dest_cell),
        row(box_owner),
        row(box_slot),
    )
    adjoint, box_gradient = hand_over(*solve_rows(devices, tiles, slab_of, spots, parcels, stiffness, anchor, coupling))
    return (adjoint, box_gradient)


def solution(mesh):
    placed = (
        P(None, ("gx", "gy")),
        P(("gx", "gy")),
        P(("gx", "gy"), None),
        P(("gx", "gy")),
        P(("gx", "gy"), None),
        P(("gx", "gy")),
        P("gx", "gy", None),
        P(None, "gx", "gy", None),
        P(None, "gx", "gy", None),
    )
    return jax.shard_map(
        body,
        mesh=mesh,
        in_specs=placed,
        out_specs=(P(None, "gx", "gy", None), P(None, ("gx", "gy"))),
        check_vma=False,
    )
```

```python
import functools

import jax
import jax.numpy as jnp
from jax import lax
from jax.experimental import pallas as pl
from jax.experimental.pallas import tpu as pltpu
from jax.sharding import PartitionSpec as P

BOX_DEV = 64
SWEEPS = 4
SENT = 4
FIELDS = 6
NT = (((1,), (1,)), ((), ()))
F32 = jnp.float32
BF16 = jnp.bfloat16
MESH = pl.DeviceIdType.MESH


def two_terms(x):
    hi = x.astype(BF16).astype(F32)
    return hi, x - hi


def matches(count, row):
    return lax.broadcasted_iota(jnp.int32, (count, row.shape[1]), 0) == row


def one_hot(mask):
    return jnp.where(mask, 1.0, 0.0).astype(BF16)


def scaled(mask, row):
    return jnp.where(mask, row, 0.0).astype(BF16)


def dot_nt(a, b):
    return lax.dot_general(a, b, NT, preferred_element_type=F32)


def split(value, size):
    if size & (size - 1) == 0:
        return value >> (size.bit_length() - 1), value & (size - 1)
    return value // size, value % size


def wide_matches(count, row):
    return lax.broadcasted_iota(jnp.int16, (count, row.shape[1]), 0) == row.astype(jnp.int16)


def wide_one_hot(count, row):
    return jnp.where(wide_matches(count, row), jnp.array(1, BF16), jnp.array(0, BF16))


def kept(mask, values):
    return jnp.where(mask, values, jnp.array(0, BF16))


def fan(values, index, count):
    size, length = values.shape
    many = min(count, max(1, 16 // size))
    terms = jnp.concatenate([values] * many, axis=0).astype(BF16)
    part = lax.broadcasted_iota(jnp.int32, terms.shape, 0) // size
    index = (jnp.broadcast_to(index, terms.shape) - part).astype(jnp.int16)
    return jnp.concatenate([kept(index == t, terms) for t in range(0, count, many)], axis=0)


def two_rows(rows):
    return jnp.concatenate(two_terms(jnp.concatenate(rows, axis=0)), axis=0)


def halves(values):
    size = values.shape[0] // 2
    return values[:size] + values[size:]


def folded(a, b, size):
    if size & (size - 1):
        return (a + b) % size
    total, bit = 0, 1
    while bit < size:
        total = total + bit * ((a // bit + b // bit) % 2)
        bit = 2 * bit
    return total


def peers_of(gx, gy, size_x, size_y):
    along = [(gy + step) % size_y for step in range(size_y)]
    return [(across, there) for across in [folded(gx, step, size_x) for step in range(size_x)] for there in along]


def running(numbers):
    totals = [jnp.zeros_like(numbers[0])]
    for number in numbers:
        totals.append(totals[-1] + number)
    return totals


def ordinals(chosen):
    length = chosen[0].shape[1]
    stacked = one_hot(jnp.concatenate(chosen, axis=0))
    earlier = one_hot(
        lax.broadcasted_iota(jnp.int32, (length, length), 0)
        < lax.broadcasted_iota(jnp.int32, (length, length), 1)
    )
    before = jnp.dot(stacked, earlier, preferred_element_type=F32)
    number = jnp.dot(stacked, jnp.ones((length, 128), BF16), preferred_element_type=F32)
    size = chosen[0].shape[0]

    def cut(values):
        return [values[q * size : (q + 1) * size] for q in range(len(chosen))]

    return cut(before), cut(number)


def picked(mask, value):
    return jnp.sum(jnp.where(mask, value, 0.0), axis=0, keepdims=True)


def relay_kernel(cut, slabs, *refs):
    given, refs = refs[:6], refs[6:]
    tiles, slab_of, spots, send, sens, weight, device, cell, owner, slot, recv, place, spread, fetch, send_sem, recv_sem = refs
    count, fields, capacity = send.shape
    rows = sens.shape[1]
    _, _, width = tiles.shape
    groups = slab_of.shape[0]
    per_group = tiles.shape[0] // groups
    gx, gy = lax.axis_index("gx"), lax.axis_index("gy")
    size_x, size_y = lax.axis_size("gx"), lax.axis_size("gy")
    peers = peers_of(gx, gy, size_x, size_y)
    barrier = pltpu.get_barrier_semaphore()
    fetches = [
        pltpu.make_async_copy(source, target, fetch.at[i])
        for i, (source, target) in enumerate(zip(given, (sens, weight, device, cell, owner, slot)))
    ]
    for copy in fetches:
        copy.start()

    for peer in peers[1:]:
        pl.semaphore_signal(barrier, inc=1, device_id=peer, device_id_type=MESH)

    length = min(512, rows)
    chunks = rows // length
    spans = [slice(q * length, (q + 1) * length) for q in range(chunks)]
    for copy in fetches:
        copy.wait()
    to_x, to_y = split(device[...], size_y)
    to_y = to_y - gy
    to_y = jnp.where(to_y < 0, to_y + size_y, to_y)
    if size_x & (size_x - 1):
        to_x = to_x - gx
        to_x = jnp.where(to_x < 0, to_x + size_x, to_x)
    else:
        to_x = to_x ^ gx
    target = to_x * size_y + to_y
    chosen = [matches(count, target[:, span]) for span in spans]
    before, number = ordinals(chosen)
    total = running(number)
    for q, span in enumerate(spans):
        rank = picked(chosen[q], before[q] + total[q][:, :1]).astype(jnp.int32)
        place[:, span] = wide_one_hot(capacity, rank)

    senders = count // groups

    def copy(step, size):
        return pltpu.make_async_remote_copy(
            src_ref=send.at[pl.ds(step, size), pl.ds(0, SENT)],
            dst_ref=recv.at[pl.ds(step, size), pl.ds(0, SENT)],
            send_sem=send_sem.at[0],
            recv_sem=recv_sem.at[step // senders],
            device_id=peers[step],
            device_id_type=MESH,
        )

    def packed(rows, low):
        size = 2 * len(rows)
        for span in spans:
            spread[: count * size, span] = fan(two_rows([read(span) for read in rows]), target[:, span], count)
        product = dot_nt(spread[: count * size], place[...])
        for t in range(count):
            send[t, low : low + len(rows)] = halves(product[t * size : (t + 1) * size])

    packed([lambda span, k=k: sens[k : k + 1, span] for k in range(3)] + [lambda span: cell[:, span].astype(F32)], 0)
    pl.semaphore_wait(barrier, count - 1)
    for step in range(1, count):
        copy(step, 1).start()
    packed([lambda span: weight[:, span], lambda span: (owner[:, span] * BOX_DEV + slot[:, span]).astype(F32)], SENT)
    recv[0] = send[0]

    for group in range(groups):
        begin = max(1, group * senders)
        copy(begin, (group + 1) * senders - begin).wait_recv()
        sort_group(cut, slabs, [recv.at[group * senders + i] for i in range(senders)], tiles, group * per_group, per_group, slab_of, spots, group)

    copy(1, count - 1).wait_send()


def joined(arrived, low, high):
    join = max(1, min(len(arrived), 512 // arrived[0].shape[1]))
    return [
        jnp.concatenate([arrived[q + i][low:high] for i in range(join)], axis=1)
        for q in range(0, len(arrived), join)
    ]


def ordered(blocks, spots, per_group, width):
    size = 2 * blocks[0].shape[0]
    sums = jnp.zeros((per_group * size, width), F32)
    for block, spot in zip(blocks, spots):
        tile, lane = split(spot, width)
        spread = fan(jnp.concatenate(two_terms(block), axis=0), tile, per_group)
        sums = sums + dot_nt(spread, wide_one_hot(width, lane))
    return [halves(sums[t * size : (t + 1) * size]) for t in range(per_group)]


def sort_group(cut, slabs, arrived, tiles, first, per_group, slab_of, spots, group):
    width = tiles.shape[2]
    blocks = joined(arrived, 0, SENT)
    count = len(blocks)
    chosen = [matches(slabs, split(block[3:4].astype(jnp.int32), cut)[0]) for block in blocks]
    before, number = ordinals(chosen)
    total = running(number)
    lower = one_hot(
        lax.broadcasted_iota(jnp.int32, (slabs, slabs), 1)
        < lax.broadcasted_iota(jnp.int32, (slabs, slabs), 0)
    )
    tens = jnp.floor(total[-1] * 0.0625)
    start = 16.0 * jnp.dot(lower, tens.astype(BF16), preferred_element_type=F32)
    start = start + jnp.dot(lower, (total[-1] - 16.0 * tens).astype(BF16), preferred_element_type=F32)

    steps = per_group + slabs - 1
    row = lax.broadcasted_iota(jnp.int32, start.shape, 0).astype(F32)
    step = lax.broadcasted_iota(jnp.int32, start.shape, 1).astype(F32)
    entry = row + jnp.minimum(jnp.floor(start * (1.0 / width)), per_group - 1.0)
    slab = jnp.sum(jnp.where((row > 0) & (entry <= step), 1.0, 0.0), axis=0, keepdims=True)
    slab = jnp.where(step[:1] < steps, slab, slabs)
    inside = (row > 0) & (start < (step + 1.0) * width)
    final = step[:1] + jnp.sum(jnp.where(inside, 1.0, 0.0), axis=0, keepdims=True)
    leave = jnp.sum(jnp.where(row == step + 1.0, entry, 0.0), axis=0, keepdims=True)
    leave = jnp.where(step[:1] == slabs - 1, steps, leave) - 1.0
    table = jnp.concatenate([slab, final, leave, jnp.zeros((5, 128), F32)], axis=0)
    slab_of[group] = table.astype(jnp.int32)

    found = [
        picked(chosen[q], before[q] + (total[q] + start)[:, :1]).astype(jnp.int32) for q in range(count)
    ]
    for q in range(count):
        spots[group * count + q : group * count + q + 1] = found[q]
    for t, tile in enumerate(ordered(blocks, found, per_group, width)):
        tiles[first + t, :SENT] = tile


def relay_rows(devices, capacity, slabs, cut, sens, weight, device, cell, owner, slot):
    rows = devices * capacity
    size = min(4096, rows)
    width = min(256, size)
    groups = rows // size
    length = max(1, min(size // capacity, 512 // capacity)) * capacity
    return pl.pallas_call(
        functools.partial(relay_kernel, cut, slabs),
        out_shape=[
            pltpu.VMEM((rows // width, 8, width), F32),
            jax.ShapeDtypeStruct((groups, 8, 128), jnp.int32),
            pltpu.VMEM((rows // length, length), jnp.int32),
            pltpu.VMEM((devices, 8, capacity), F32),
        ],
        in_specs=[pl.BlockSpec(memory_space=pltpu.HBM)] * 6,
        out_specs=[pl.BlockSpec(memory_space=pltpu.VMEM)] * 4,
        scratch_shapes=[pltpu.VMEM(given.shape, given.dtype) for given in (sens, weight, device, cell, owner, slot)]
        + [
            pltpu.VMEM((devices, 8, capacity), F32),
            pltpu.VMEM((capacity, sens.shape[1]), BF16),
            pltpu.VMEM((devices * 2 * SENT, sens.shape[1]), BF16),
            pltpu.SemaphoreType.DMA((6,)),
            pltpu.SemaphoreType.DMA((1,)),
            pltpu.SemaphoreType.DMA((groups,)),
        ],
        compiler_params=pltpu.CompilerParams(collective_id=1, has_side_effects=True, vmem_limit_bytes=60 << 20),
        name="relay_rows",
    )(sens, weight, device, cell, owner, slot)


def located(tile, size_z):
    return split(tile[3:4].astype(jnp.int32), size_z)


def solve_kernel(slab_of, tiles, spots, parcels, stiff_in, anchor_in, coupling_in, adjoint, box, stiff, anchor, coupling, load, stage, late, marks, weighted, inverse, near, edge, halo, terms, found, flat, landed, fetch, late_send, late_recv, x_send, x_recv, y_send, y_recv, box_send, box_recv):
    parts, size_x, size_y, size_z = load.shape
    count, _, width = tiles.shape
    groups = slab_of.shape[0]
    per_group = count // groups
    steps = per_group + size_x
    half = parts * size_y
    exchanges = weighted.shape[0]
    gx, gy = lax.axis_index("gx"), lax.axis_index("gy")
    count_x, count_y = lax.axis_size("gx"), lax.axis_size("gy")
    devices = count_x * count_y
    peers = peers_of(gx, gy, count_x, count_y)
    sides = (("gx", gx, -1, gx > 0), ("gx", gx, 1, gx < count_x - 1), ("gy", gy, -1, gy > 0), ("gy", gy, 1, gy < count_y - 1))
    y_at = lax.broadcasted_iota(jnp.int32, (size_y, size_z), 0)
    z_at = lax.broadcasted_iota(jnp.int32, (size_y, size_z), 1)
    barrier = pltpu.get_barrier_semaphore()

    for peer in peers[1:]:
        pl.semaphore_signal(barrier, inc=1, device_id=peer, device_id_type=MESH)
    fetches = [
        pltpu.make_async_copy(source, target, fetch.at[i])
        for i, (source, target) in enumerate(((stiff_in, stiff), (anchor_in, anchor), (coupling_in, coupling)))
    ]
    for copy in fetches:
        copy.start()

    for side, (axis, place, move, present) in enumerate(sides):

        @pl.when(jnp.logical_not(present))
        def _():
            for index in range(exchanges):
                if axis == "gx":
                    for k in range(parts):
                        weighted[index, k, 0 if move < 0 else size_x + 1] = jnp.zeros((size_y, size_z), F32)
                else:
                    halo[index, side % 2] = jnp.zeros(halo.shape[2:], F32)

    def transfers(index, sending, which=range(4)):
        made = []
        for side in which:
            axis, place, move, present = sides[side]
            there = 1 - side % 2
            landing = there if sending else side % 2
            if axis == "gx":
                into = size_x + 1 if (move < 0) == sending else 0
                pair = (weighted.at[index, :, 1 if move < 0 else size_x], weighted.at[index, :, into])
                sems = (x_send, x_recv)
            else:
                pair = (edge.at[index, side % 2], halo.at[index, landing])
                sems = (y_send, y_recv)
            made.append((present, pltpu.make_async_remote_copy(
                src_ref=pair[0],
                dst_ref=pair[1],
                send_sem=sems[0].at[index, side % 2],
                recv_sem=sems[1].at[index, landing],
                device_id={axis: place + move},
                device_id_type=MESH,
            )))
        return made

    def begin(index):
        for present, copy in transfers(index, True):

            @pl.when(present)
            def _():
                copy.start()

    def arrive(index, which):
        for present, copy in transfers(index, False, which):

            @pl.when(present)
            def _():
                copy.wait_recv()

    rims = (0, size_y - 1)

    def deposit(step, carry):
        made = []
        for group in range(groups):
            slab = slab_of[group, 0, step]
            tile = tiles[group * per_group + jnp.minimum(step - slab, per_group - 1)]
            xy, z = located(tile, size_z)
            pairs = [two_terms(tile[k : k + 1]) for k in range(parts)]
            values = [hi for hi, lo in pairs] + [lo for hi, lo in pairs]
            at_y = matches(size_y, xy - slab * size_y)
            spread = jnp.concatenate([scaled(at_y, value) for value in values], axis=0)
            product = dot_nt(spread, wide_one_hot(size_z, z))
            at = group * steps + step
            earlier = stage[jnp.maximum(at - 1, 0)]
            stage[at] = product[:half] + product[half:] + jnp.where(slab == carry[group], earlier, 0.0)
            made.append(slab)
        return tuple(made)

    late_rows = pl.ds(SENT, FIELDS - SENT)

    def follow(step, size):
        return pltpu.make_async_remote_copy(
            src_ref=parcels.at[pl.ds(step, size), late_rows],
            dst_ref=late.at[pl.ds(step, size), late_rows],
            send_sem=late_send.at[0],
            recv_sem=late_recv.at[0],
            device_id=peers[step],
            device_id_type=MESH,
        )

    def sort_late(group):
        senders = devices // groups
        blocks = joined([late.at[group * senders + i] for i in range(senders)], SENT, FIELDS)
        lines = [spots[q : q + 1] for q in range(group * len(blocks), (group + 1) * len(blocks))]
        for t, tile in enumerate(ordered(blocks, lines, per_group, width)):
            marks[group * per_group + t, : FIELDS - SENT] = tile

    stage[0] = jnp.zeros(stage.shape[1:], F32)
    slabs = lax.fori_loop(0, steps // 2, deposit, tuple(jnp.int32(-1) for _ in range(groups)), unroll=16)
    pl.semaphore_wait(barrier, devices - 1)
    for step in reversed(range(1, devices)):
        follow(step, 1).start()
    late[0] = parcels[0]
    lax.fori_loop(steps // 2, steps, deposit, slabs, unroll=16)
    for copy in fetches:
        copy.wait()

    def first(x, carry):
        stiffness = stiff[x]
        sums = stage[slab_of[0, 2, x]]
        for group in range(1, groups):
            sums = sums + stage[group * steps + slab_of[group, 2, x]]
        for side, rim in enumerate(rims):
            near[2, side, 0, pl.ds(x, 1), :] = stiffness[rim : rim + 1]
        for k in range(parts):
            inverted = 1.0 / (6.0 * stiffness + anchor[k, x] + coupling[4 * k, x])
            inverse[k, x] = inverted
            there = sums[k * size_y : (k + 1) * size_y]
            load[k, x] = there
            value = there * inverted
            adjoint[k, x] = value
            product = stiffness * value
            weighted[0, k, x + 1] = product
            for side, rim in enumerate(rims):
                near[1, side, k, pl.ds(x, 1), :] = inverted[rim : rim + 1]
                edge[0, side, k, pl.ds(x, 1), :] = product[rim : rim + 1]
        return carry

    lax.fori_loop(0, size_x, first, 0)
    begin(0)
    follow(1, devices - 1).wait_recv()

    for index in range(exchanges):
        last = index + 1 == exchanges
        for group in range(groups * index // exchanges, groups * (index + 1) // exchanges):
            sort_late(group)

        def update(x, carry):
            fields = [adjoint[k, x] for k in range(parts)]
            for k in range(parts):
                product = weighted[index, k, x + 1]
                value = load[k, x] + weighted[index, k, x] + weighted[index, k, x + 2]
                for j in range(parts):
                    if j != k:
                        value = value - coupling[3 * j + k, x] * fields[j]
                value = value + jnp.where(z_at == 0, 0.0, pltpu.roll(product, 1, 1))
                value = value + jnp.where(z_at == size_z - 1, 0.0, pltpu.roll(product, size_z - 1, 1))
                value = value + jnp.where(y_at == 0, 0.0, pltpu.roll(product, 1, 0))
                value = value + jnp.where(y_at == size_y - 1, 0.0, pltpu.roll(product, size_y - 1, 0))
                value = value * inverse[k, x]
                adjoint[k, x] = value
                for side, rim in enumerate(rims):
                    near[0, side, k, pl.ds(x, 1), :] = value[rim : rim + 1]
                if not last:
                    weighted[index + 1, k, x + 1] = stiff[x] * value
            return carry

        lax.fori_loop(1, size_x - 1, update, 0)
        arrive(index, (0, 1))
        update(0, 0)
        update(size_x - 1, 0)
        arrive(index, (2, 3))
        for side, rim in enumerate(rims):
            for k in range(parts):
                value = near[0, side, k] + halo[index, side, k] * near[1, side, k]
                for x in range(size_x):
                    adjoint[k, x, rim : rim + 1, :] = value[x : x + 1]
                if not last:
                    product = near[2, side, 0] * value
                    edge[index + 1, side, k] = product
                    for x in range(size_x):
                        weighted[index + 1, k, x + 1, rim : rim + 1, :] = product[x : x + 1]
        if not last:
            begin(index + 1)

    def cut(x, carry):
        for k in range(parts):
            hi, lo = two_terms(adjoint[k, x])
            terms[x, k * size_y : (k + 1) * size_y] = hi.astype(BF16)
            terms[x, half + k * size_y : half + (k + 1) * size_y] = lo.astype(BF16)
        return carry

    lax.fori_loop(0, size_x, cut, 0)

    def look(step, carry):
        made = []
        for group in range(groups):
            held, before = carry[group]
            slab = slab_of[group, 0, step]
            tile = tiles[group * per_group + jnp.minimum(step - slab, per_group - 1)]
            xy, z = located(tile, size_z)
            at_y = matches(size_y, xy - slab * size_y)
            columns = jnp.dot(terms[jnp.minimum(slab, size_x - 1)], wide_one_hot(size_z, z), preferred_element_type=F32)
            columns = columns[:half] + columns[half:]
            value = jnp.concatenate(
                [picked(at_y, columns[k * size_y : (k + 1) * size_y]) for k in range(parts)], axis=0
            )
            held = value + jnp.where(slab == before, 0.0, held)
            found[group * steps + step, :parts] = held
            made.append((held, slab))
        return tuple(made)

    lax.fori_loop(
        0, steps, look, tuple((jnp.zeros((parts, width), F32), jnp.int32(0)) for _ in range(groups)), unroll=4
    )
    total = jnp.zeros((2 * parts * devices, BOX_DEV), F32)
    join = min(8, count)
    for begin_at in range(0, count, join):
        numbers = range(begin_at, begin_at + join)

        def line(field):
            return jnp.concatenate([marks[t, field : field + 1] for t in numbers], axis=1)

        owner, slot = split(line(1).astype(jnp.int32), BOX_DEV)
        rows = jnp.concatenate(
            [found[t // per_group * steps + slab_of[t // per_group, 1, t % per_group]][:parts] for t in numbers], axis=1
        ) * line(0)
        at_owner = matches(devices, owner)
        pairs = [two_terms(rows[k : k + 1]) for k in range(parts)]
        values = [hi for hi, lo in pairs] + [lo for hi, lo in pairs]
        spread = jnp.concatenate([scaled(at_owner, value) for value in values], axis=0)
        total = total + dot_nt(spread, wide_one_hot(BOX_DEV, slot))
    for k in range(parts):
        part = total[k * devices : (k + 1) * devices] + total[(parts + k) * devices : (parts + k + 1) * devices]
        flat[k] = jnp.concatenate([part, jnp.zeros_like(part)], axis=1)

    def parcel(step, first, size):
        return pltpu.make_async_remote_copy(
            src_ref=flat.at[:, pl.ds(first, size)],
            dst_ref=landed.at[:, pl.ds(step, size)],
            send_sem=box_send.at[0],
            recv_sem=box_recv.at[0],
            device_id=peers[step],
            device_id_type=MESH,
        )

    for step in reversed(range(1, devices)):
        there = peers[step]
        parcel(step, there[0] * count_y + there[1], 1).start()
    landed[:, 0:1] = flat[:, pl.ds(gx * count_y + gy, 1)]

    parcel(1, 1, devices - 1).wait_recv()
    for k in range(parts):
        box[k : k + 1] = jnp.sum(landed[k], axis=0, keepdims=True)[:, :BOX_DEV]

    parcel(1, 1, devices - 1).wait_send()
    follow(1, devices - 1).wait_send()
    for index in range(exchanges):
        for present, copy in transfers(index, True):

            @pl.when(present)
            def _():
                copy.wait_send()


def solve_rows(devices, tiles, slab_of, spots, parcels, stiffness, anchor, coupling):
    size_x, size_y, size_z = stiffness.shape
    parts = anchor.shape[0]
    exchanges = SWEEPS - 1
    count, fields, width = tiles.shape
    groups = slab_of.shape[0]
    steps = count // groups + size_x
    kept_near = [pltpu.with_memory_space_constraint(value, pltpu.VMEM) for value in (tiles, spots, parcels)]
    return pl.pallas_call(
        solve_kernel,
        out_shape=[pltpu.VMEM(anchor.shape, F32), pltpu.VMEM((parts, BOX_DEV), F32)],
        in_specs=[pl.BlockSpec(memory_space=pltpu.SMEM)]
        + [pl.BlockSpec(memory_space=pltpu.VMEM)] * 3
        + [pl.BlockSpec(memory_space=pltpu.HBM)] * 3,
        out_specs=[pl.BlockSpec(memory_space=pltpu.VMEM)] * 2,
        scratch_shapes=[
            pltpu.VMEM(stiffness.shape, F32),
            pltpu.VMEM(anchor.shape, F32),
            pltpu.VMEM(coupling.shape, F32),
            pltpu.VMEM(anchor.shape, F32),
            pltpu.VMEM((groups * steps, parts * size_y, size_z), F32),
            pltpu.VMEM(parcels.shape, F32),
            pltpu.VMEM(tiles.shape, F32),
            pltpu.VMEM((exchanges, parts, size_x + 2, size_y, size_z), F32),
            pltpu.VMEM(anchor.shape, F32),
            pltpu.VMEM((3, 2, parts, size_x, size_z), F32),
            pltpu.VMEM((exchanges, 2, parts, size_x, size_z), F32),
            pltpu.VMEM((exchanges, 2, parts, size_x, size_z), F32),
            pltpu.VMEM((size_x, 2 * parts * size_y, size_z), BF16),
            pltpu.VMEM((groups * steps, fields, width), F32),
            pltpu.VMEM((parts, devices, 2 * BOX_DEV), F32),
            pltpu.VMEM((parts, devices, 2 * BOX_DEV), F32),
            pltpu.SemaphoreType.DMA((3,)),
        ]
        + [pltpu.SemaphoreType.DMA((1,))] * 2
        + [pltpu.SemaphoreType.DMA((exchanges, 2))] * 4
        + [pltpu.SemaphoreType.DMA((1,))] * 2,
        compiler_params=pltpu.CompilerParams(collective_id=0, has_side_effects=True, vmem_limit_bytes=56 << 20),
        name="solve_rows",
    )(slab_of, *kept_near, stiffness, anchor, coupling)


def hand_kernel(adjoint, box, adjoint_out, box_out, sem):
    copies = [
        pltpu.make_async_copy(adjoint, adjoint_out, sem.at[0]),
        pltpu.make_async_copy(box, box_out, sem.at[1]),
    ]
    for copy in copies:
        copy.start()
    for copy in copies:
        copy.wait()


def hand_over(adjoint, box):
    values = [pltpu.with_memory_space_constraint(value, pltpu.VMEM) for value in (adjoint, box)]
    return pl.pallas_call(
        hand_kernel,
        out_shape=[jax.ShapeDtypeStruct(value.shape, F32) for value in values],
        in_specs=[pl.BlockSpec(memory_space=pltpu.VMEM)] * 2,
        out_specs=[pl.BlockSpec(memory_space=pltpu.HBM)] * 2,
        scratch_shapes=[pltpu.SemaphoreType.DMA((2,))],
        name="hand_over",
    )(*values)


def body(
    sensitivity,
    node_weight,
    dest_device,
    dest_cell,
    box_owner,
    box_slot,
    stiffness,
    anchor,
    coupling,
):
    devices = lax.axis_size("gx") * lax.axis_size("gy")
    row_count = sensitivity.shape[1]
    capacity = 2 * row_count // devices
    size_x, size_y, size_z = stiffness.shape
    size_xy = size_x * size_y
    assert size_xy * size_z <= 2**17 and devices * BOX_DEV <= 2**17

    def row(values):
        return values.reshape(1, row_count)

    tiles, slab_of, spots, parcels = relay_rows(
        devices,
        capacity,
        size_x,
        size_y * size_z,
        sensitivity,
        row(node_weight),
        row(dest_device),
        row(dest_cell),
        row(box_owner),
        row(box_slot),
    )
    adjoint, box_gradient = hand_over(*solve_rows(devices, tiles, slab_of, spots, parcels, stiffness, anchor, coupling))
    return (adjoint, box_gradient)


def solution(mesh):
    placed = (
        P(None, ("gx", "gy")),
        P(("gx", "gy")),
        P(("gx", "gy"), None),
        P(("gx", "gy")),
        P(("gx", "gy"), None),
        P(("gx", "gy")),
        P("gx", "gy", None),
        P(None, "gx", "gy", None),
        P(None, "gx", "gy", None),
    )
    return jax.shard_map(
        body,
        mesh=mesh,
        in_specs=placed,
        out_specs=(P(None, "gx", "gy", None), P(None, ("gx", "gy"))),
        check_vma=False,
    )
```
